32 devices in a mesh: rep: 2 (over y), dp: 4 (over z), mp: 4 (over x, core).
Axes of the slice: x: 2, y: 2, z: 4, core: 2. Of those that a mesh axis runs over, the one named last changes fastest.
Arguments:
- inputs: float32 [8, 4, 512, 1024], P(('rep', 'mp'), 'dp'), may hold values from -6 to 6
- norm1_gain: float32 [1024], replicated, may hold values from 0.1 to 1.9
- query_key_value_weight: bfloat16 [3, 1024, 1024], P(None, None, 'mp'), may hold values from -0.1875 to 0.1875
- output_weight: bfloat16 [1024, 1024], P('mp'), may hold values from -1.5 to 1.5
- norm2_gain: float32 [1024], replicated, may hold values from 0.1 to 1.9
- expansion_matrix: bfloat16 [1024, 1024], P(None, 'mp'), may hold values from -0.1875 to 0.1875
- contraction_matrix: bfloat16 [1024, 1024], P('mp'), may hold values from -0.1875 to 0.1875
- cotangent: float32 [8, 4, 512, 1024], P(('rep', 'mp'), 'dp'), may hold values from -6 to 6
Outputs:
- output: float32 [8, 4, 512, 1024], P(('rep', 'mp'), 'dp')
- grad_inputs: float32 [8, 4, 512, 1024], P(('rep', 'mp'), 'dp')
- grad_norm1: float32 [1024], replicated
- grad_qkv: float32 [3, 1024, 1024], P(None, None, 'mp')
- grad_out: float32 [1024, 1024], P('mp')
- grad_norm2: float32 [1024], replicated
- grad_up: float32 [1024, 1024], P(None, 'mp')
- grad_down: float32 [1024, 1024], P('mp')
The draws below stay inside these ranges and needn't reach their ends.
All inputs are finite; a program needn't handle non-finite values.
Results may differ from the reference program's by a relative error of at most 0.018.
Values may be sent and summed in bfloat16 or wider, within the bound.
No kernel may reach another device: no remote copies, remote signals or barrier semaphores. Data moves between devices by JAX's collectives and lax.ppermute only.
A program may use at most 128 MiB of HBM per device.

```python
import jax
import jax.numpy as jnp
from jax import lax

D = 1024
HEADS = 8
HEAD_DIM = 128
FF = 1024
LAT = 512
REP_DEV = 4
IMG_DEV = 1
REPEATS = 8
IMAGES = 4


def levels(stream_key, dims, cuts, least, top_value):
    def one(axis_at, shards_of):
        heights = jax.random.uniform(jax.random.fold_in(jax.random.fold_in(stream_key, 6), axis_at), (shards_of,), jnp.float32, least / len(cuts), top_value / len(cuts))
        return jnp.repeat(jnp.exp(heights), dims[axis_at] // shards_of).reshape((-1,) + (1,) * (len(dims) - axis_at - 1))

    level = one(*cuts[0])
    for cut in cuts[1:]:
        level = level * one(*cut)
    return level


def bell_draw(stream_key, shape, scale, reach, pieces=(), held_as=jnp.bfloat16):
    drawn = jax.random.normal(stream_key, shape, jnp.float32) * scale
    if len(pieces) > 0:
        drawn = levels(stream_key, shape, pieces, -0.22, 0.18) * drawn
    return jnp.clip(drawn, min=-reach, max=reach).astype(held_as)


def setup_inputs(seed: int = 0) -> dict:
    keys = jax.random.split(jax.random.key(seed), 9)
    inputs = bell_draw(keys[0], (REPEATS, IMAGES, LAT, D), 1.0, 6.0, ((0, 8), (1, 4)), jnp.float32)
    norm1_gain = jnp.clip(1.0 + 0.18 * jax.random.normal(keys[1], (D,), jnp.float32), 0.1, 1.9)
    query_key_value_weight = bell_draw(keys[2], (3, D, D), D ** -0.5, 0.1875, ((2, 4),))
    output_weight = bell_draw(keys[3], (D, D), (D * 8 // LAT) ** -0.5, 1.5, ((0, 4),))
    norm2_gain = jnp.clip(1.0 + 0.18 * jax.random.normal(keys[4], (D,), jnp.float32), 0.1, 1.9)
    expansion_matrix = bell_draw(keys[5], (D, FF), D ** -0.5, 0.1875, ((1, 4),))
    contraction_matrix = bell_draw(keys[6], (FF, D), FF ** -0.5, 0.1875, ((0, 4),))
    cotangent = bell_draw(keys[7], (REPEATS, IMAGES, LAT, D), 1.0, 6.0, ((0, 8), (1, 4)), jnp.float32)
    return {"inputs": inputs, "norm1_gain": norm1_gain, "query_key_value_weight": query_key_value_weight, "output_weight": output_weight, "norm2_gain": norm2_gain, "expansion_matrix": expansion_matrix, "contraction_matrix": contraction_matrix, "cotangent": cotangent}


@jax.custom_vjp
def low_precision(v):
    return lax.optimization_barrier(v.astype(jnp.bfloat16)).astype(jnp.float32)

@jax.custom_vjp
def coarse_derivative_pass(v):
    return v

def low_keep(v):
    return (low_precision(v), None)

def low_pass(kept, grad):
    return (grad,)

def back_keep(v):
    return (v, None)

def back_low(kept, grad):
    return (low_precision(grad),)
low_precision.defvjp(low_keep, low_pass)
coarse_derivative_pass.defvjp(back_keep, back_low)
norm_eps = 1e-05
exact_arithmetic = lax.Precision.HIGHEST

def layer_norm(values, gain):
    mean = lax.optimization_barrier(jnp.mean(values, axis=-1, keepdims=True))
    centred = values - mean
    spread = lax.optimization_barrier(jnp.mean(centred * centred, axis=-1, keepdims=True))
    return centred * lax.rsqrt(spread + norm_eps) * gain

def block(latents, norm1_gain, query_key_value_weight, output_weight, norm2_gain, expansion_matrix, contraction_matrix):
    seqs = latents.shape[0]
    first_layer = low_precision(layer_norm(latents, norm1_gain))
    query_key_value = coarse_derivative_pass(low_precision(jnp.einsum('gxy,nyh->ngxh', first_layer, query_key_value_weight, precision=exact_arithmetic)))
    query = query_key_value[0].reshape(seqs, LAT, HEADS, HEAD_DIM)
    key_part = query_key_value[1].reshape(seqs, LAT, HEADS, HEAD_DIM)
    value_part = query_key_value[2].reshape(seqs, LAT, HEADS, HEAD_DIM)
    scores = coarse_derivative_pass(jnp.einsum('sqhd,skhd->shqk', query, key_part, precision=exact_arithmetic) * HEAD_DIM ** (-0.5))
    probs = low_precision(jax.nn.softmax(scores, axis=-1))
    mixed_heads = coarse_derivative_pass(low_precision(jnp.einsum('shqk,skhd->sqhd', probs, value_part, precision=exact_arithmetic)))
    mixed_heads = mixed_heads.reshape(seqs, LAT, D)
    attention_block = coarse_derivative_pass(jnp.einsum('qrp,pv->qrv', mixed_heads, output_weight, precision=exact_arithmetic))
    resid = latents + attention_block
    contraction_product = low_precision(layer_norm(resid, norm2_gain))
    expansion_product = coarse_derivative_pass(jnp.einsum('yrp,pb->yrb', contraction_product, expansion_matrix, precision=exact_arithmetic))
    hidden_state = low_precision(jax.nn.gelu(expansion_product))
    feedforward_block = coarse_derivative_pass(jnp.einsum('tcx,xp->tcp', hidden_state, contraction_matrix, precision=exact_arithmetic))
    return resid + feedforward_block

def reference(inputs, norm1_gain, query_key_value_weight, output_weight, norm2_gain, expansion_matrix, contraction_matrix, cotangent):
    per_block = REP_DEV * IMG_DEV
    w_qkv32 = query_key_value_weight.astype(jnp.float32)
    w_out32 = output_weight.astype(jnp.float32)
    w_up32 = expansion_matrix.astype(jnp.float32)
    w_down32 = contraction_matrix.astype(jnp.float32)

    def forward(latents, gain_one, weight_qkv, weight_out, gain_two, weight_up, weight_down):
        blocks = latents.reshape(-1, per_block, LAT, D)

        def run(piece):
            return block(piece, gain_one, weight_qkv, weight_out, gain_two, weight_up, weight_down)
        return lax.map(jax.checkpoint(run), blocks).reshape(latents.shape)
    output, pullback = jax.vjp(forward, inputs, norm1_gain, w_qkv32, w_out32, norm2_gain, w_up32, w_down32)
    grads = pullback(cotangent)
    return (output, grads[0], grads[1], grads[2], grads[3], grads[4], grads[5], grads[6])
```

```python
import functools

import jax
import jax.numpy as jnp
from jax import lax
from jax.experimental import pallas as pl
from jax.experimental.pallas import tpu as pltpu
from jax.sharding import PartitionSpec as P

HEAD_DIM = 128
EPS = 1e-05
LOG2E = 1.4426950408889634
GELU_A = 0.7978845608028654
GELU_B = 0.044715
f32 = jnp.float32
bf16 = jnp.bfloat16

NN = (((1,), (0,)), ((), ()))
NT = (((1,), (1,)), ((), ()))
TN = (((0,), (0,)), ((), ()))


def dot(a, b, dims=NN):
    return lax.dot_general(a, b, dims, preferred_element_type=f32)


def normed(v):
    mean = jnp.mean(v, axis=-1, keepdims=True)
    centred = v - mean
    r = lax.rsqrt(jnp.mean(centred * centred, axis=-1, keepdims=True) + EPS)
    return centred * r, r


def fold(v):
    return jnp.sum(v.reshape(-1, 8, v.shape[-1]), axis=0)


def params(mib=40):
    return pltpu.CompilerParams(vmem_limit_bytes=mib * 2**20)


def cost(flops, nbytes):
    return pl.CostEstimate(flops=int(flops), bytes_accessed=int(nbytes), transcendentals=0)


def whole(n):
    return [pl.BlockSpec(memory_space=pltpu.VMEM)] * n


def sds(shape, dtype):
    return jax.ShapeDtypeStruct(shape, dtype)


def rows_spec(rows, cols):
    return pl.BlockSpec((rows, cols), lambda i: (i, 0))


def fixed_spec(shape):
    return pl.BlockSpec(shape, lambda i: (0,) * len(shape), pipeline_mode=pl.Buffered(1))


def prep_kernel(x_ref, c_ref, g_ref, a_ref, d_ref):
    a_ref[...] = (normed(x_ref[...])[0] * g_ref[...]).astype(bf16)
    d_ref[...] = c_ref[...].astype(bf16)


def prep(x, cot, gain, block=128):
    length, width = x.shape
    spec = rows_spec(block, width)
    return pl.pallas_call(
        prep_kernel,
        grid=(length // block,),
        in_specs=[spec, spec, fixed_spec((1, width))],
        out_specs=[spec, spec],
        out_shape=[sds(x.shape, bf16)] * 2,
        compiler_params=params(16),
        cost_estimate=cost(10 * x.size, 12 * x.size),
        name="prep",
    )(x, cot, gain)


def attend_kernel(a_ref, w_ref, qkv_ref, mixed_ref, lse_ref):
    scale = HEAD_DIM**-0.5 * LOG2E
    for c in range(3):
        qkv_ref[c] = dot(a_ref[...], w_ref[c]).astype(bf16)
    for h in range(w_ref.shape[2] // HEAD_DIM):
        cols = slice(h * HEAD_DIM, (h + 1) * HEAD_DIM)
        q, k, v = (qkv_ref[c, :, cols] for c in range(3))
        scores = dot(k, q, NT)
        top = jnp.max(scores, axis=0, keepdims=True)
        expd = jnp.exp2((scores - top) * scale)
        total = jnp.sum(expd, axis=0, keepdims=True)
        mixed = dot(v, expd.astype(bf16), TN) / total
        mixed_ref[:, cols] = mixed.T.astype(bf16)
        lse_ref[h : h + 1, :] = top * scale + jnp.log2(total)


def attend(a, w):
    length, width = a.shape
    local = w.shape[2]
    heads = local // HEAD_DIM
    return pl.pallas_call(
        attend_kernel,
        in_specs=whole(2),
        out_specs=whole(3),
        out_shape=[sds((3, length, local), bf16), sds((length, local), bf16), sds((heads, length), f32)],
        compiler_params=params(),
        cost_estimate=cost(6 * length * width * local + 4 * heads * length * length * HEAD_DIM * 4, 4e6),
        name="attend",
    )(a, w)


def project_kernel(n, *refs):
    mixed, w = refs[:n], refs[n : 2 * n]
    x_ref, g_ref, resid_ref, a_ref = refs[2 * n :]
    resid = x_ref[...]
    total = dot(mixed[0][...], w[0][...])
    for j in range(1, n):
        total += dot(mixed[j][...], w[j][...])
    resid = x_ref[...] + total
    resid_ref[...] = resid
    a_ref[...] = (normed(resid)[0] * g_ref[...]).astype(bf16)


def project(mixed, w, x, gain, block=128):
    n = len(mixed)
    length, width = x.shape
    local = mixed[0].shape[1]
    spec = rows_spec(block, width)
    return pl.pallas_call(
        functools.partial(project_kernel, n),
        grid=(length // block,),
        in_specs=[rows_spec(block, local)] * n + [fixed_spec((local, width))] * n + [spec, fixed_spec((1, width))],
        out_specs=[spec, spec],
        out_shape=[sds(x.shape, f32), sds(x.shape, bf16)],
        compiler_params=params(),
        cost_estimate=cost(2 * length * width * local * n, 9e6),
        name="project",
    )(*mixed, *w, x, gain)


def mlp_kernel(n, *refs):
    a_ref, d_ref = refs[:2]
    up, down = refs[2 : 2 + n], refs[2 + n : 2 + 2 * n]
    hid_ref, dpre_ref, grad_ref = refs[2 + 2 * n :]
    for j in range(n):
        u = dot(a_ref[...], up[j][...])
        d_hidden = dot(d_ref[...], down[j][...], NT)
        sq = u * u
        t = jnp.tanh(GELU_A * u * (1.0 + GELU_B * sq))
        half = 0.5 * (1.0 + t)
        hidden = (u * half).astype(bf16)
        slope = half + 0.5 * u * (1.0 - t * t) * (GELU_A * (1.0 + 3.0 * GELU_B * sq))
        d_pre = (d_hidden * slope).astype(bf16)
        hid_ref[j] = hidden
        dpre_ref[j] = d_pre
        grad_ref[j, 0] = dot(hidden, d_ref[...], TN).astype(bf16)
        grad_ref[j, 1] = dot(d_pre, a_ref[...], TN).astype(bf16)


def mlp(a, d, up, down):
    n = len(up)
    length, width = a.shape
    local = up[0].shape[1]
    return pl.pallas_call(
        functools.partial(mlp_kernel, n),
        in_specs=whole(2 + 2 * n),
        out_specs=whole(3),
        out_shape=[sds((n, length, local), bf16), sds((n, length, local), bf16), sds((n, 2, local, width), bf16)],
        compiler_params=params(),
        cost_estimate=cost(8 * length * width * local * n, 8e6),
        name="mlp",
    )(a, d, *up, *down)


def norm_back(d_a, v, gain):
    xhat, r = normed(v)
    e = d_a * gain
    back = r * (e - jnp.mean(e, axis=-1, keepdims=True) - xhat * jnp.mean(e * xhat, axis=-1, keepdims=True))
    return back, fold(d_a * xhat)


def mlp_back_kernel(n, *refs):
    d_pre, up = refs[:2], refs[2 : 2 + n]
    resid_ref, c_ref, g_ref, dres_ref, datt_ref, gain_ref = refs[2 + n :]
    total = None
    for j in range(n):
        part = dot(d_pre[j // (n // 2)][j % (n // 2)], up[j][...], NT)
        total = part if total is None else total + part
    back, gain = norm_back(total, resid_ref[...], g_ref[...])
    d_resid = c_ref[...] + back
    dres_ref[...] = d_resid
    datt_ref[...] = d_resid.astype(bf16)

    @pl.when(pl.program_id(0) == 0)
    def _():
        gain_ref[...] = jnp.zeros_like(gain_ref)

    gain_ref[...] += gain


def mlp_back(d_pre, up, resid, cot, gain, block=128):
    n = len(up)
    length, width = resid.shape
    local = up[0].shape[1]
    spec = rows_spec(block, width)
    part = pl.BlockSpec((n // 2, block, local), lambda i: (0, i, 0))
    return pl.pallas_call(
        functools.partial(mlp_back_kernel, n),
        grid=(length // block,),
        in_specs=[part] * 2 + [fixed_spec((width, local))] * n + [spec, spec, fixed_spec((1, width))],
        out_specs=[spec, spec, pl.BlockSpec((8, width), lambda i: (0, 0))],
        out_shape=[sds(resid.shape, f32), sds(resid.shape, bf16), sds((8, width), f32)],
        compiler_params=params(),
        cost_estimate=cost(2 * length * width * local * n, 9e6),
        name="mlp_back",
    )(*d_pre, *up, resid, cot, gain)


def mlp_out_kernel(n, *refs):
    hid, down = refs[:2], refs[2 : 2 + n]
    resid_ref, out_ref = refs[2 + n :]
    total = resid_ref[...]
    for j in range(n):
        total += dot(hid[j // (n // 2)][j % (n // 2)], down[j][...])
    out_ref[...] = total


def mlp_out(hid, down, resid, block=128):
    n = len(down)
    length, width = resid.shape
    local = down[0].shape[0]
    spec = rows_spec(block, width)
    part = pl.BlockSpec((n // 2, block, local), lambda i: (0, i, 0))
    return pl.pallas_call(
        functools.partial(mlp_out_kernel, n),
        grid=(length // block,),
        in_specs=[part] * 2 + [fixed_spec((local, width))] * n + [spec],
        out_specs=spec,
        out_shape=sds(resid.shape, f32),
        compiler_params=params(),
        cost_estimate=cost(2 * length * width * local * n, 7e6),
        name="mlp_out",
    )(*hid, *down, resid)


def grad_out_kernel(n, *refs):
    d_ref, mixed, out_ref = refs[0], refs[1 : 1 + n], refs[1 + n]
    for j in range(n):
        out_ref[j] = dot(mixed[j][...], d_ref[...], TN).astype(bf16)


def grad_out(d, mixed):
    n = len(mixed)
    length, width = d.shape
    local = mixed[0].shape[1]
    return pl.pallas_call(
        functools.partial(grad_out_kernel, n),
        in_specs=whole(1 + n),
        out_specs=pl.BlockSpec(memory_space=pltpu.VMEM),
        out_shape=sds((n, local, width), bf16),
        compiler_params=params(),
        cost_estimate=cost(2 * length * width * local * n, 4e6),
        name="grad_out",
    )(d, *mixed)


def attend_back_kernel(a_ref, d_ref, w_ref, qkv_ref, lse_ref, dqkv_ref, grad_ref):
    scale = HEAD_DIM**-0.5
    d_mixed = dot(d_ref[...], w_ref[...], NT).astype(bf16)
    for h in range(w_ref.shape[0] // HEAD_DIM):
        cols = slice(h * HEAD_DIM, (h + 1) * HEAD_DIM)
        q, k, v = (qkv_ref[c, :, cols] for c in range(3))
        dm = d_mixed[:, cols]
        probs = jnp.exp2(dot(k, q, NT) * (scale * LOG2E) - lse_ref[h : h + 1, :])
        d_probs = dot(v, dm, NT)
        dqkv_ref[2, :, cols] = dot(probs.astype(bf16), dm).astype(bf16)
        delta = jnp.sum(d_probs * probs, axis=0, keepdims=True)
        d_scores = (probs * (d_probs - delta)).astype(bf16)
        dqkv_ref[1, :, cols] = (dot(d_scores, q) * scale).astype(bf16)
        dqkv_ref[0, :, cols] = (dot(k, d_scores, TN) * scale).T.astype(bf16)
    for c in range(3):
        grad_ref[c] = dot(dqkv_ref[c], a_ref[...], TN).astype(bf16)


def attend_back(a, d, w, qkv, lse):
    length, width = a.shape
    local = w.shape[0]
    heads = local // HEAD_DIM
    return pl.pallas_call(
        attend_back_kernel,
        in_specs=whole(5),
        out_specs=whole(2),
        out_shape=[sds((3, length, local), bf16), sds((3, local, width), bf16)],
        compiler_params=params(),
        cost_estimate=cost(8 * length * width * local + 10 * heads * length * length * HEAD_DIM * 4, 7e6),
        name="attend_back",
    )(a, d, w, qkv, lse)


def input_back_kernel(n, *refs):
    d_qkv, w = refs[:n], refs[n : 2 * n]
    x_ref, dres_ref, g_ref, out_ref, gain_ref = refs[2 * n :]
    total = None
    for j in range(n):
        for c in range(3):
            part = dot(d_qkv[j][c], w[j][c], NT)
            total = part if total is None else total + part
    back, gain = norm_back(total, x_ref[...], g_ref[...])
    out_ref[...] = dres_ref[...] + back

    @pl.when(pl.program_id(0) == 0)
    def _():
        gain_ref[...] = jnp.zeros_like(gain_ref)

    gain_ref[...] += gain


def input_back(d_qkv, w, x, d_resid, gain, block=128):
    n = len(w)
    length, width = x.shape
    local = w[0].shape[2]
    spec = rows_spec(block, width)
    part = pl.BlockSpec((3, block, local), lambda i: (0, i, 0))
    return pl.pallas_call(
        functools.partial(input_back_kernel, n),
        grid=(length // block,),
        in_specs=[part] * n + [fixed_spec((3, width, local))] * n + [spec, spec, fixed_spec((1, width))],
        out_specs=[spec, pl.BlockSpec((8, width), lambda i: (0, 0))],
        out_shape=[sds(x.shape, f32), sds((8, width), f32)],
        compiler_params=params(),
        cost_estimate=cost(6 * length * width * local * n, 15e6),
        name="input_back",
    )(*d_qkv, *w, x, d_resid, gain)


def swap(axis, size, bit):
    pairs = [(i, i ^ bit) for i in range(size)]
    return lambda v: lax.ppermute(v, axis, pairs)


def bits_of(size):
    return [1 << b for b in reversed(range(size.bit_length() - 1))]


class Order:
    def __init__(self):
        self.token = None

    def send(self, move, v):
        if self.token is not None:
            v, _ = lax.optimization_barrier((v, self.token))
        self.token = v
        return move(v)


def per_device(
    sizes,
    inputs,
    norm1_gain,
    weight_qkv,
    weight_out,
    norm2_gain,
    weight_up,
    weight_down,
    cotangent,
):
    n_rep, n_dp, n_mp = sizes["rep"], sizes["dp"], sizes["mp"]
    shape = inputs.shape
    x = inputs.reshape(shape[-2:])
    cot = cotangent.reshape(shape[-2:])
    gain1, gain2 = norm1_gain.reshape(1, -1), norm2_gain.reshape(1, -1)
    mp_bits = bits_of(n_mp)
    half = n_mp // 2

    def gather(v):
        got = [v]
        for bit in mp_bits:
            got += [swap("mp", n_mp, bit)(g) for g in got]
        return got

    w_qkv = gather(weight_qkv)
    w_out = gather(weight_out)
    w_up = gather(weight_up)
    w_down = gather(weight_down)

    order = Order()
    dp_at = lax.axis_index("dp")
    rep_at = lax.axis_index("rep")

    def over_dp(v):
        if n_dp == 4:
            s = v + order.send(lambda t: lax.ppermute(t, "dp", [(0, 1), (3, 2)]), v)
            t = s + order.send(lambda t: lax.ppermute(t, "dp", [(1, 2), (2, 1)]), s)
            r = order.send(lambda t: lax.ppermute(t, "dp", [(1, 0), (2, 3)]), t)
            return jnp.where((dp_at == 0) | (dp_at == 3), r, t)
        if n_dp & (n_dp - 1):
            return lax.psum(v, "dp")
        for bit in bits_of(n_dp):
            v = v + order.send(swap("dp", n_dp, bit), v)
        return v

    def over_replicas(keep, got):
        if n_rep != 2:
            return lax.psum(over_dp(keep + got), "rep")
        rows = keep.shape[-2] // 2

        def part(v, at):
            return lax.dynamic_slice_in_dim(v, at * rows, rows, keep.ndim - 2)

        y = swap("rep", 2, 1)
        mine = part(keep, rep_at) + part(got, rep_at)
        mine = mine + order.send(y, part(keep, 1 - rep_at) + part(got, 1 - rep_at))
        mine = over_dp(mine)
        other = order.send(y, mine)
        lo = jnp.where(rep_at == 0, mine, other)
        hi = jnp.where(rep_at == 0, other, mine)
        return jnp.concatenate([lo, hi], axis=keep.ndim - 2)

    def reduce_tail(parts):
        for bit in reversed(mp_bits[:-1]):
            h = len(parts) // 2
            got = [order.send(swap("mp", n_mp, bit), p) for p in parts[h:]]
            if h == 1:
                return over_replicas(parts[0], got[0])
            parts = [p + g for p, g in zip(parts[:h], got)]
        return over_replicas(parts[0], jnp.zeros_like(parts[0]))

    core = swap("mp", n_mp, 1)

    a1, d_mlp = prep(x, cot, gain1)
    qkv, mixed, lse = [None] * n_mp, [None] * n_mp, [None] * n_mp
    for j in [i for i in range(n_mp) if i % half == 0] + [i for i in range(n_mp) if i % half]:
        qkv[j], mixed[j], lse[j] = attend(a1, w_qkv[j])
    resid, a2 = project(mixed, w_out, x, gain2)

    hid_b, dpre_b, grad_b = mlp(a2, d_mlp, w_up[half:], w_down[half:])
    got_b = order.send(core, grad_b)
    hid_a, dpre_a, grad_a = mlp(a2, d_mlp, w_up[:half], w_down[:half])
    sum_ffn = reduce_tail([grad_a[j] + got_b[j] for j in range(half)])
    d_resid, d_attn, part2 = mlp_back([dpre_a, dpre_b], w_up, resid, cot, gain2)

    g_out = grad_out(d_attn, mixed)
    got_out = order.send(core, g_out[half:])
    sum_out = reduce_tail([g_out[j] + got_out[j] for j in range(half)])

    d_qkv, sent = [None] * n_mp, [None] * half
    kept = [None] * half
    for j in reversed(range(half)):
        d_qkv[j + half], g = attend_back(a1, d_attn, w_out[j + half], qkv[j + half], lse[j + half])
        sent[j] = order.send(core, g)
        d_qkv[j], kept[j] = attend_back(a1, d_attn, w_out[j], qkv[j], lse[j])
    sum_qkv = reduce_tail([kept[j] + sent[j] for j in range(half)])
    output = mlp_out([hid_a, hid_b], w_down, resid)
    grad_inputs, part1 = input_back(d_qkv, w_qkv, x, d_resid, gain1)

    gains = jnp.stack([jnp.sum(part1, axis=0), jnp.sum(part2, axis=0)])
    for axis, size in (("mp", n_mp), ("rep", n_rep), ("dp", n_dp)):
        if size & (size - 1):
            gains = lax.psum(gains, axis)
            continue
        for bit in bits_of(size):
            gains = gains + order.send(swap(axis, size, bit), gains)
    return (
        output.reshape(shape),
        grad_inputs.reshape(shape),
        gains[0],
        jnp.swapaxes(sum_qkv, 1, 2).astype(f32),
        sum_out.astype(f32),
        gains[1],
        sum_ffn[1].T.astype(f32),
        sum_ffn[0].astype(f32),
    )


def solution(mesh):
    return jax.shard_map(
        functools.partial(per_device, dict(mesh.shape)),
        mesh=mesh,
        in_specs=(
            P(("rep", "mp"), "dp", None, None),
            P(),
            P(None, None, "mp"),
            P("mp", None),
            P(),
            P(None, "mp"),
            P("mp", None),
            P(("rep", "mp"), "dp", None, None),
        ),
        out_specs=(
            P(("rep", "mp"), "dp", None, None),
            P(("rep", "mp"), "dp", None, None),
            P(),
            P(None, None, "mp"),
            P("mp", None),
            P(),
            P(None, "mp"),
            P("mp", None),
        ),
        check_vma=False,
    )
```

```python
import functools

import jax
import jax.numpy as jnp
from jax import lax
from jax.experimental import pallas as pl
from jax.experimental.pallas import tpu as pltpu
from jax.sharding import PartitionSpec as P

HEAD_DIM = 128
EPS = 1e-05
LOG2E = 1.4426950408889634
GELU_A = 0.7978845608028654
GELU_B = 0.044715
f32 = jnp.float32
bf16 = jnp.bfloat16

NN = (((1,), (0,)), ((), ()))
NT = (((1,), (1,)), ((), ()))
TN = (((0,), (0,)), ((), ()))


def dot(a, b, dims=NN):
    return lax.dot_general(a, b, dims, preferred_element_type=f32)


def normed(v):
    mean = jnp.mean(v, axis=-1, keepdims=True)
    centred = v - mean
    r = lax.rsqrt(jnp.mean(centred * centred, axis=-1, keepdims=True) + EPS)
    return centred * r, r


def fold(v):
    return jnp.sum(v.reshape(-1, 8, v.shape[-1]), axis=0)


def params(mib=20):
    return pltpu.CompilerParams(vmem_limit_bytes=mib * 2**20)


def cost(flops, nbytes):
    return pl.CostEstimate(flops=int(flops), bytes_accessed=int(nbytes), transcendentals=0)


def whole(n):
    return [pl.BlockSpec(memory_space=pltpu.VMEM)] * n


def sds(shape, dtype):
    return jax.ShapeDtypeStruct(shape, dtype)


def rows_spec(rows, cols):
    return pl.BlockSpec((rows, cols), lambda i: (i, 0))


def fixed_spec(shape):
    return pl.BlockSpec(shape, lambda i: (0,) * len(shape), pipeline_mode=pl.Buffered(1))


def prep_kernel(x_ref, c_ref, g_ref, a_ref, d_ref):
    a_ref[...] = (normed(x_ref[...])[0] * g_ref[...]).astype(bf16)
    d_ref[...] = c_ref[...].astype(bf16)


def prep(x, cot, gain, block=128):
    length, width = x.shape
    spec = rows_spec(block, width)
    return pl.pallas_call(
        prep_kernel,
        grid=(length // block,),
        in_specs=[spec, spec, fixed_spec((1, width))],
        out_specs=[spec, spec],
        out_shape=[sds(x.shape, bf16)] * 2,
        compiler_params=params(16),
        cost_estimate=cost(10 * x.size, 12 * x.size),
        name="prep",
    )(x, cot, gain)


def attend_kernel(a_ref, w_ref, qkv_ref, mixed_ref, lse_ref):
    scale = HEAD_DIM**-0.5 * LOG2E
    for c in range(3):
        qkv_ref[c] = dot(a_ref[...], w_ref[c]).astype(bf16)
    for h in range(w_ref.shape[2] // HEAD_DIM):
        cols = slice(h * HEAD_DIM, (h + 1) * HEAD_DIM)
        q, k, v = (qkv_ref[c, :, cols] for c in range(3))
        scores = dot(k, q, NT)
        top = jnp.max(scores, axis=0, keepdims=True)
        expd = jnp.exp2((scores - top) * scale)
        total = jnp.sum(expd, axis=0, keepdims=True)
        mixed = dot(v, expd.astype(bf16), TN) / total
        mixed_ref[:, cols] = mixed.T.astype(bf16)
        lse_ref[h : h + 1, :] = top * scale + jnp.log2(total)


def attend(a, w):
    length, width = a.shape
    local = w.shape[2]
    heads = local // HEAD_DIM
    return pl.pallas_call(
        attend_kernel,
        in_specs=whole(2),
        out_specs=whole(3),
        out_shape=[sds((3, length, local), bf16), sds((length, local), bf16), sds((heads, length), f32)],
        compiler_params=params(),
        cost_estimate=cost(6 * length * width * local + 4 * heads * length * length * HEAD_DIM * 4, 4e6),
        name="attend",
    )(a, w)


def project_kernel(n, *refs):
    mixed, w = refs[:n], refs[n : 2 * n]
    x_ref, g_ref, resid_ref, a_ref = refs[2 * n :]
    resid = x_ref[...]
    total = dot(mixed[0][...], w[0][...])
    for j in range(1, n):
        total += dot(mixed[j][...], w[j][...])
    resid = x_ref[...] + total
    resid_ref[...] = resid
    a_ref[...] = (normed(resid)[0] * g_ref[...]).astype(bf16)


def project(mixed, w, x, gain, block=128):
    n = len(mixed)
    length, width = x.shape
    local = mixed[0].shape[1]
    spec = rows_spec(block, width)
    return pl.pallas_call(
        functools.partial(project_kernel, n),
        grid=(length // block,),
        in_specs=[rows_spec(block, local)] * n + [fixed_spec((local, width))] * n + [spec, fixed_spec((1, width))],
        out_specs=[spec, spec],
        out_shape=[sds(x.shape, f32), sds(x.shape, bf16)],
        compiler_params=params(),
        cost_estimate=cost(2 * length * width * local * n, 9e6),
        name="project",
    )(*mixed, *w, x, gain)


def mlp_kernel(n, *refs):
    a_ref, d_ref = refs[:2]
    up, down = refs[2 : 2 + n], refs[2 + n : 2 + 2 * n]
    outs = refs[2 + 2 * n :]
    hid, dpre, grads = outs[:n], outs[n : 2 * n], outs[2 * n :]
    for j in range(n):
        u = dot(a_ref[...], up[j][...])
        d_hidden = dot(d_ref[...], down[j][...], NT)
        sq = u * u
        t = jnp.tanh(GELU_A * u * (1.0 + GELU_B * sq))
        half = 0.5 * (1.0 + t)
        hidden = (u * half).astype(bf16)
        slope = half + 0.5 * u * (1.0 - t * t) * (GELU_A * (1.0 + 3.0 * GELU_B * sq))
        d_pre = (d_hidden * slope).astype(bf16)
        hid[j][...] = hidden
        dpre[j][...] = d_pre
        grads[j][0] = dot(hidden, d_ref[...], TN).astype(bf16)
        grads[j][1] = dot(d_pre, a_ref[...], TN).astype(bf16)


def mlp(a, d, up, down):
    n = len(up)
    length, width = a.shape
    local = up[0].shape[1]
    act, grad = sds((length, local), bf16), sds((2, local, width), bf16)
    outs = pl.pallas_call(
        functools.partial(mlp_kernel, n),
        in_specs=whole(2 + 2 * n),
        out_specs=whole(3 * n),
        out_shape=[act] * (2 * n) + [grad] * n,
        compiler_params=params(20),
        cost_estimate=cost(8 * length * width * local * n, 8e6),
        name="mlp",
    )(a, d, *up, *down)
    return outs[:n], outs[n : 2 * n], outs[2 * n :]


def norm_back(d_a, v, gain):
    xhat, r = normed(v)
    e = d_a * gain
    back = r * (e - jnp.mean(e, axis=-1, keepdims=True) - xhat * jnp.mean(e * xhat, axis=-1, keepdims=True))
    return back, fold(d_a * xhat)


def mlp_back_kernel(n, *refs):
    d_pre, up = refs[:n], refs[n : 2 * n]
    resid_ref, c_ref, g_ref, dres_ref, datt_ref, gain_ref = refs[2 * n :]
    total = None
    for j in range(n):
        part = dot(d_pre[j][...], up[j][...], NT)
        total = part if total is None else total + part
    back, gain = norm_back(total, resid_ref[...], g_ref[...])
    d_resid = c_ref[...] + back
    dres_ref[...] = d_resid
    datt_ref[...] = d_resid.astype(bf16)

    @pl.when(pl.program_id(0) == 0)
    def _():
        gain_ref[...] = jnp.zeros_like(gain_ref)

    gain_ref[...] += gain


def mlp_back(d_pre, up, resid, cot, gain, block=128):
    n = len(up)
    length, width = resid.shape
    local = up[0].shape[1]
    spec = rows_spec(block, width)
    return pl.pallas_call(
        functools.partial(mlp_back_kernel, n),
        grid=(length // block,),
        in_specs=[rows_spec(block, local)] * n + [fixed_spec((width, local))] * n + [spec, spec, fixed_spec((1, width))],
        out_specs=[spec, spec, pl.BlockSpec((8, width), lambda i: (0, 0))],
        out_shape=[sds(resid.shape, f32), sds(resid.shape, bf16), sds((8, width), f32)],
        compiler_params=params(),
        cost_estimate=cost(2 * length * width * local * n, 9e6),
        name="mlp_back",
    )(*d_pre, *up, resid, cot, gain)


def mlp_out_kernel(n, *refs):
    hid, down = refs[:n], refs[n : 2 * n]
    resid_ref, out_ref = refs[2 * n :]
    total = resid_ref[...]
    for j in range(n):
        total += dot(hid[j][...], down[j][...])
    out_ref[...] = total


def mlp_out(hid, down, resid, block=128):
    n = len(down)
    length, width = resid.shape
    local = down[0].shape[0]
    spec = rows_spec(block, width)
    return pl.pallas_call(
        functools.partial(mlp_out_kernel, n),
        grid=(length // block,),
        in_specs=[rows_spec(block, local)] * n + [fixed_spec((local, width))] * n + [spec],
        out_specs=spec,
        out_shape=sds(resid.shape, f32),
        compiler_params=params(),
        cost_estimate=cost(2 * length * width * local * n, 7e6),
        name="mlp_out",
    )(*hid, *down, resid)


def grad_out_kernel(n, *refs):
    d_ref, mixed, kept_ref, sent_ref = refs[0], refs[1 : 1 + n], refs[1 + n], refs[2 + n]
    for j in range(n):
        into = (kept_ref, sent_ref)[j // (n // 2)]
        into[j % (n // 2)] = dot(mixed[j][...], d_ref[...], TN).astype(bf16)


def grad_out(d, mixed):
    n = len(mixed)
    length, width = d.shape
    local = mixed[0].shape[1]
    return pl.pallas_call(
        functools.partial(grad_out_kernel, n),
        in_specs=whole(1 + n),
        out_specs=whole(2),
        out_shape=[sds((n // 2, local, width), bf16)] * 2,
        compiler_params=params(12),
        cost_estimate=cost(2 * length * width * local * n, 4e6),
        name="grad_out",
    )(d, *mixed)


def attend_back_kernel(added, a_ref, d_ref, w_ref, qkv_ref, lse_ref, *refs):
    scale = HEAD_DIM**-0.5
    got_ref = refs[0] if added else None
    dqkv_ref, grads = refs[added], refs[added + 1 :]
    d_mixed = dot(d_ref[...], w_ref[...], NT).astype(bf16)
    for h in range(w_ref.shape[0] // HEAD_DIM):
        cols = slice(h * HEAD_DIM, (h + 1) * HEAD_DIM)
        q, k, v = (qkv_ref[c, :, cols] for c in range(3))
        dm = d_mixed[:, cols]
        probs = jnp.exp2(dot(k, q, NT) * (scale * LOG2E) - lse_ref[h : h + 1, :])
        d_probs = dot(v, dm, NT)
        dqkv_ref[2, :, cols] = dot(probs.astype(bf16), dm).astype(bf16)
        delta = jnp.sum(d_probs * probs, axis=0, keepdims=True)
        d_scores = (probs * (d_probs - delta)).astype(bf16)
        dqkv_ref[1, :, cols] = (dot(d_scores, q) * scale).astype(bf16)
        dqkv_ref[0, :, cols] = (dot(k, d_scores, TN) * scale).T.astype(bf16)
    for c in range(3):
        grad = dot(dqkv_ref[c], a_ref[...], TN)
        if added:
            grads[c][...] = (grad + got_ref[c].astype(f32)).astype(bf16)
        else:
            grads[0][c] = grad.astype(bf16)


def attend_back(a, d, w, qkv, lse, got=None):
    length, width = a.shape
    local = w.shape[0]
    heads = local // HEAD_DIM
    added = got is not None
    one = sds((local, width), bf16)
    outs = pl.pallas_call(
        functools.partial(attend_back_kernel, int(added)),
        in_specs=whole(5 + added),
        out_specs=whole(4 if added else 2),
        out_shape=[sds((3, length, local), bf16)] + ([one] * 3 if added else [sds((3, local, width), bf16)]),
        compiler_params=params(20),
        cost_estimate=cost(8 * length * width * local + 10 * heads * length * length * HEAD_DIM * 4, 7e6),
        name="attend_back",
    )(a, d, w, qkv, lse, *([got] if added else []))
    return outs[0], (list(outs[1:]) if added else outs[1])


def join_kernel(n, axes, at_ref, *refs):
    quarters, outs = refs[:4], refs[4:]
    width = quarters[0].shape[1]
    for p, quarter in enumerate(quarters):
        at = pl.multiple_of(at_ref[p] * width, width)
        i = 0
        for out, axis in zip(outs, axes, strict=True):
            if axis == 3:
                for c in range(3):
                    out[c, pl.ds(at, width), :] = quarter[i + c]
                i += 3
            elif axis == 0:
                out[pl.ds(at, width), :] = quarter[i]
                i += 1
            else:
                out[:, pl.ds(at, width)] = quarter[i]
                i += 1


def join(at, quarters, likes, axes):
    return pl.pallas_call(
        functools.partial(join_kernel, len(likes), tuple(axes)),
        in_specs=[pl.BlockSpec(memory_space=pltpu.SMEM)] + whole(4),
        out_specs=whole(len(likes)),
        out_shape=[sds(v.shape, v.dtype) for v in likes],
        compiler_params=params(12),
        cost_estimate=cost(0, 4e6),
        name="join",
    )(at, *quarters)


def finish_kernel(turned, slot, first, at_ref, mine_ref, other_ref, *refs):
    out_ref = refs[-1]
    rows = mine_ref.shape[-2]
    for at, ref in ((at_ref[0], mine_ref), (1 - at_ref[0], other_ref)):
        place = pl.ds(pl.multiple_of(at * rows, rows), rows)
        v = ref[...].astype(f32)
        if turned:
            out_ref[0, :, place] = v.T
        else:
            out_ref[place, :] = v


def finish(at, mine, other, turned, into=None, slot=0, slots=1):
    rows, width = mine.shape
    shape = (slots, width, 2 * rows) if turned else (2 * rows, width)
    out_spec = pl.BlockSpec((1, width, 2 * rows), lambda i: (slot, 0, 0)) if turned else pl.BlockSpec(shape, lambda i: (0, 0))
    spec = pl.BlockSpec((rows, width), lambda i: (0, 0))
    return pl.pallas_call(
        functools.partial(finish_kernel, turned, slot, into is None),
        grid=(1,),
        in_specs=[pl.BlockSpec(memory_space=pltpu.SMEM), spec, spec] + ([pl.BlockSpec(memory_space=pl.ANY)] if into is not None else []),
        out_specs=out_spec,
        out_shape=sds(shape, f32),
        input_output_aliases={3: 0} if into is not None else {},
        compiler_params=params(12),
        cost_estimate=cost(0, 2e6),
        name="finish",
    )(at, mine, other, *([into] if into is not None else []))


def input_back_kernel(n, *refs):
    d_qkv, w = refs[:n], refs[n : 2 * n]
    x_ref, dres_ref, g_ref, out_ref, gain_ref = refs[2 * n :]
    total = None
    for j in range(n):
        for c in range(3):
            part = dot(d_qkv[j][c], w[j][c], NT)
            total = part if total is None else total + part
    back, gain = norm_back(total, x_ref[...], g_ref[...])
    out_ref[...] = dres_ref[...] + back

    @pl.when(pl.program_id(0) == 0)
    def _():
        gain_ref[...] = jnp.zeros_like(gain_ref)

    gain_ref[...] += gain


def input_back(d_qkv, w, x, d_resid, gain, block=128):
    n = len(w)
    length, width = x.shape
    local = w[0].shape[2]
    spec = rows_spec(block, width)
    part = pl.BlockSpec((3, block, local), lambda i: (0, i, 0))
    return pl.pallas_call(
        functools.partial(input_back_kernel, n),
        grid=(length // block,),
        in_specs=[part] * n + [fixed_spec((3, width, local))] * n + [spec, spec, fixed_spec((1, width))],
        out_specs=[spec, pl.BlockSpec((8, width), lambda i: (0, 0))],
        out_shape=[sds(x.shape, f32), sds((8, width), f32)],
        compiler_params=params(),
        cost_estimate=cost(6 * length * width * local * n, 15e6),
        name="input_back",
    )(*d_qkv, *w, x, d_resid, gain)


def swap(axis, size, bit):
    pairs = [(i, i ^ bit) for i in range(size)]
    return lambda v: lax.ppermute(v, axis, pairs)


def bits_of(size):
    return [1 << b for b in reversed(range(size.bit_length() - 1))]


class Run:
    def __init__(self):
        self.token = None

    def tie(self, v):
        if self.token is None:
            return v
        return lax.optimization_barrier((v, self.token))[0]

    def compute(self, step, first, *rest):
        outs = step(self.tie(first), *rest)
        self.token = jax.tree.leaves(outs)[0]
        return outs

    def send(self, move, v):
        v = self.tie(v)
        self.token = v
        return move(v)


def half_rows(v, at):
    rows = v.shape[-2] // 2
    return lax.dynamic_slice_in_dim(v, at * rows, rows, v.ndim - 2)


ORDER = (
    "sl_q", "xp_q", "prep", "att0", "xr_q", "c0_q", "c0_ou", "sl_ou", "xp_ou", "xr_ou", "c0_d", "y_q", "att2",
    "sl_d", "xp_d", "z_q", "xr_d", "y_ou", "as_q", "cx_q", "z_ou", "att1", "y_d", "att3", "z_d", "as_ou",
    "cx_ou", "as_d", "cx_d", "proj", "mlpR", "cF1", "mlpP", "aF1", "cF0", "F.zx", "mlpback", "aF0", "F.zo",
    "ab3", "F.ax", "F.x", "cQ1", "gout", "cO", "ab2", "ab1", "Qa.x", "Qb.x", "cQ0", "F.ao", "F.a1", "F.y",
    "Qc.x", "ab0", "aO", "O.x", "Qa.a1", "Qa.y", "mlpout", "F.a2", "F.m", "inback", "Qb.a1", "Qb.y", "Qa.a2",
    "Qa.z1", "g0", "Qb.a2", "Qb.z1", "Qc.a1", "Qc.y", "Qa.a3", "g1", "Qa.z2", "Qb.a3", "Qb.z2", "Qc.a2", "Qc.z1",
    "O.a1", "O.y", "g2", "Qa.a4", "Qa.z3", "Qc.a3", "Qc.z2", "Qb.a4", "Qb.z3", "O.a2", "O.z1", "Qa.a5", "Qa.w",
    "Qc.a4", "Qc.z3", "F.a3", "F.w", "O.a3", "O.z2", "Qb.a5", "Qa.f", "Qb.w", "Qc.a5", "Qc.w", "O.a4", "O.z3",
    "g3", "O.a5", "O.w", "Qb.f", "Qc.f", "F.f", "O.f",
)
GROUPS = {"q": ("qkv",), "ou": ("out", "up"), "d": ("down",)}
CHUNKS = {"F": ("z", "F", None), "O": ("x", "O", 0), "Qa": ("x", "Q", 0), "Qb": ("x", "Q", 1), "Qc": ("x", "Q", 2)}
AXES = {"qkv": 3, "out": 1, "up": 0, "down": 1}


def per_device(
    sizes,
    inputs,
    norm1_gain,
    weight_qkv,
    weight_out,
    norm2_gain,
    weight_up,
    weight_down,
    cotangent,
):
    n_rep, n_dp, n_mp = sizes["rep"], sizes["dp"], sizes["mp"]
    if n_mp != 4 or n_rep != 2 or n_dp & (n_dp - 1) or n_dp < 2:
        raise ValueError("unsupported mesh")
    shape = inputs.shape
    x = inputs.reshape(shape[-2:])
    cot = cotangent.reshape(shape[-2:])
    gain1, gain2 = norm1_gain.reshape(1, -1), norm2_gain.reshape(1, -1)
    width = x.shape[1]
    run = Run()
    dp_at = lax.axis_index("dp")
    rep_at = lax.axis_index("rep")
    near_at = dp_at % 2
    line = n_dp == 4
    outer = (dp_at == 0) | (dp_at == n_dp - 1)
    line_at = jnp.where(outer, 0, 1)
    quarter_at = jnp.stack([rep_at, 1 - rep_at, 2 + near_at, 3 - near_at]).astype(jnp.int32)
    rep_word = rep_at.reshape(1).astype(jnp.int32)
    line_word = line_at.reshape(1).astype(jnp.int32)

    core = swap("mp", n_mp, 1)
    far = swap("mp", n_mp, 2)
    rep = swap("rep", n_rep, 1)
    near = swap("dp", n_dp, 1)
    own = {"qkv": weight_qkv, "out": weight_out, "up": weight_up, "down": weight_down}
    w = {k: [v, None, None, None] for k, v in own.items()}
    env = {}

    def gather_task(kind, g):
        names = GROUPS[g]
        if kind == "c0":
            for k in names:
                w[k][2] = run.send(core, own[k])
        elif kind == "sl":

            def cut(first, *rest):
                return tuple(
                    jnp.concatenate([lax.dynamic_slice_in_dim(v, at * (width // 4), width // 4, 0 if AXES[k] == 0 else 1).reshape(-1, width // 4, width // 4) for k, v in zip(names, (first, *rest))])
                    for at in (rep_at, 2 + near_at)
                )

            env["p", g], env["r", g] = run.compute(cut, *[own[k] for k in names])
        elif kind == "xp":
            env["px", g] = run.send(far, env["p", g])
        elif kind == "xr":
            env["rx", g] = run.send(far, env["r", g])
        elif kind == "y":
            env["py", g] = run.send(rep, env["px", g])
        elif kind == "z":
            env["rz", g] = run.send(near, env["rx", g])
        elif kind == "as":
            outs = run.compute(
                lambda a, *rest: join(quarter_at, (a, *rest), [own[k] for k in names], [AXES[k] for k in names]),
                env["px", g], env["py", g], env["rx", g], env["rz", g],
            )
            for k, v in zip(names, outs, strict=True):
                w[k][1] = v
        elif kind == "cx":
            for k in names:
                w[k][3] = run.send(core, w[k][1])

    def over_dp(v):
        for bit in bits_of(n_dp):
            v = v + run.send(swap("dp", n_dp, bit), v)
        return v

    def chunk_task(name, stage):
        mode, source, index = CHUNKS[name]
        c = env.setdefault(("chunk", name), {})

        def part(i):
            return env[source, i] if index is None else env[source, i][index]

        if mode == "z" and not line:
            mode = "zx"
        if mode == "x":
            if stage == "x":
                c["x"] = run.send(far, part(1))
            elif stage == "a1":

                def split(k, g):
                    return half_rows(k, 1 - rep_at) + half_rows(g, 1 - rep_at), half_rows(k, rep_at) + half_rows(g, rep_at)

                c["give"], c["v"] = run.compute(split, part(0), c["x"])
            elif stage == "y":
                c["y"] = run.send(rep, c["give"])
            elif stage == "a2":
                c["v"] = run.compute(jnp.add, c["v"], c["y"])
            elif stage == "z1" and line:
                c["z1"] = run.send(lambda v: lax.ppermute(v, "dp", [(0, 1), (3, 2)]), c["v"])
            elif stage == "a3" and line:
                c["v"] = run.compute(jnp.add, c["v"], c["z1"])
            elif stage == "z2" and line:
                c["z2"] = run.send(lambda v: lax.ppermute(v, "dp", [(1, 2), (2, 1)]), c["v"])
            elif stage == "a4":
                c["v"] = run.compute(jnp.add, c["v"], c["z2"]) if line else over_dp(c["v"])
            elif stage == "z3" and line:
                c["z3"] = run.send(lambda v: lax.ppermute(v, "dp", [(1, 0), (2, 3)]), c["v"])
            elif stage == "a5" and line:
                c["v"] = run.compute(lambda a, b: jnp.where(outer, b, a), c["v"], c["z3"])
            elif stage == "w":
                c["w"] = run.send(rep, c["v"])
            elif stage == "f":
                done(name, rep_word, c["v"], c["w"])
            return
        if stage in ("zo", "zx"):
            v = part(0 if stage == "zo" else 1)
            if mode == "z":
                give = run.compute(lambda t: half_rows(t, 1 - line_at), v)
                c[stage] = run.send(near, give)
        elif stage in ("ao", "ax"):
            v = part(0 if stage == "ao" else 1)
            c[stage] = run.compute(lambda t, g: half_rows(t, line_at) + g, v, c["z" + stage[1]]) if mode == "z" else v
        elif stage == "x":
            c["x"] = run.send(far, c["ax"])
        elif stage == "a1":
            c["v"] = run.compute(jnp.add, c["ao"], c["x"])
        elif stage == "y":
            c["y"] = run.send(rep, c["v"])
        elif stage == "a2":
            c["v"] = run.compute(jnp.add, c["v"], c["y"])
        elif stage == "m":
            c["m"] = run.send(swap("dp", n_dp, 3), c["v"]) if mode == "z" else None
        elif stage == "a3":
            c["v"] = run.compute(jnp.add, c["v"], c["m"]) if mode == "z" else over_dp(c["v"])
        elif stage == "w":
            if mode == "z":
                c["w"] = run.send(near, c["v"])
            else:
                c["v"], c["w"] = (lax.slice_in_dim(c["v"], i * (c["v"].shape[-2] // 2), (i + 1) * (c["v"].shape[-2] // 2), axis=c["v"].ndim - 2) for i in range(2))
        elif stage == "f":
            done(name, line_word if mode == "z" else jnp.zeros_like(line_word), c["v"], c["w"])

    def done(name, at, mine, other):
        if name == "F":
            mine, other = run.compute(lambda a, b: ((a[0], a[1]), (b[0], b[1])), mine, other)
            env["down"] = run.compute(lambda a, b: finish(at, a, b, False), mine[0], other[0])
            env["up"] = run.compute(lambda a, b: finish(at, a, b, True), mine[1], other[1])[0]
        elif name == "O":
            env["out"] = run.compute(lambda a, b: finish(at, a, b, False), mine, other)
        else:
            env["qkv"] = run.compute(lambda a, b: finish(at, a, b, True, env.get("qkv"), "abc".index(name[1]), 3), mine, other)

    def gain_task(i):
        axis, size, bit = [("mp", n_mp, 1), ("mp", n_mp, 2), ("rep", n_rep, 1)][i] if i < 3 else ("dp", n_dp, None)
        if i < 3:
            env["g"] = env["g"] + run.send(swap(axis, size, bit), env["g"])
        elif i == 3:
            env["g"] = over_dp(env["g"])

    def task(t):
        if t == "prep":
            env["a1"], env["dm"] = run.compute(lambda c, v, g: prep(v, c, g), cot, x, gain1)
        elif t[:3] == "att":
            j = int(t[3])
            env["att", j] = run.compute(attend, env["a1"], w["qkv"][j])
        elif t == "proj":
            env["resid"], env["a2"] = run.compute(
                lambda m, *rest: project([m, *rest[:3]], w["out"], x, gain2), *[env["att", j][1] for j in range(4)]
            )
        elif t in ("mlpP", "mlpR"):
            js = (0, 2) if t == "mlpP" else (1, 3)
            hid, dpre, grads = run.compute(lambda a: mlp(a, env["dm"], [w["up"][j] for j in js], [w["down"][j] for j in js]), env["a2"])
            for i, j in enumerate(js):
                env["hid", j], env["dpre", j], env["gF", j] = hid[i], dpre[i], grads[i]
        elif t in ("cF0", "cF1"):
            j = int(t[2])
            env["rF", j] = run.send(core, env["gF", 2 + j])
        elif t in ("aF0", "aF1"):
            j = int(t[2])
            env["F", j] = run.compute(jnp.add, env["gF", j], env["rF", j])
        elif t == "mlpback":
            env["dres"], env["datt"], env["gain2"] = run.compute(
                lambda d, *rest: mlp_back([d, *rest], w["up"], env["resid"], cot, gain2), *[env["dpre", j] for j in range(4)]
            )
        elif t == "mlpout":
            env["output"] = run.compute(lambda h, *rest: mlp_out([h, *rest], w["down"], env["resid"]), *[env["hid", j] for j in range(4)])
        elif t == "gout":
            env["gO"], env["sO"] = run.compute(lambda d: grad_out(d, [env["att", j][1] for j in range(4)]), env["datt"])
        elif t == "cO":
            env["rO"] = run.send(core, env["sO"])
        elif t == "aO":
            a, b = run.compute(lambda g, r: (g[0] + r[0], g[1] + r[1]), env["gO"], env["rO"])
            env["O", 0], env["O", 1] = [a], [b]
        elif t[:2] == "ab":
            j = int(t[2])
            got = env["rQ", j] if j < 2 else None
            env["dqkv", j], env["gQ", j] = run.compute(
                lambda d: attend_back(env["a1"], d, w["out"][j], env["att", j][0], env["att", j][2], got), env["datt"]
            )
            if j < 2:
                env["Q", j] = env["gQ", j]
        elif t in ("cQ0", "cQ1"):
            j = int(t[2])
            env["rQ", j] = run.send(core, env["gQ", 2 + j])
        elif t == "inback":
            env["gin"], part1 = run.compute(
                lambda d, *rest: input_back([d, *rest], w["qkv"], x, env["dres"], gain1), *[env["dqkv", j] for j in range(4)]
            )
            env["g"] = jnp.stack([jnp.sum(part1, axis=0), jnp.sum(env["gain2"], axis=0)])
        elif t[0] == "g" and t[1:].isdigit():
            gain_task(int(t[1:]))
        elif "_" in t:
            gather_task(*t.split("_"))
        else:
            name, stage = t.split(".")
            chunk_task(name, stage)

    for t in ORDER:
        task(t)
    return (
        env["output"].reshape(shape),
        env["gin"].reshape(shape),
        env["g"][0],
        env["qkv"],
        env["out"],
        env["g"][1],
        env["up"],
        env["down"],
    )


def solution(mesh):
    return jax.shard_map(
        functools.partial(per_device, dict(mesh.shape)),
        mesh=mesh,
        in_specs=(
            P(("rep", "mp"), "dp", None, None),
            P(),
            P(None, None, "mp"),
            P("mp", None),
            P(),
            P(None, "mp"),
            P("mp", None),
            P(("rep", "mp"), "dp", None, None),
        ),
        out_specs=(
            P(("rep", "mp"), "dp", None, None),
            P(("rep", "mp"), "dp", None, None),
            P(),
            P(None, None, "mp"),
            P("mp", None),
            P(),
            P(None, "mp"),
            P("mp", None),
        ),
        check_vma=False,
    )
```

```python
import functools

import jax
import jax.numpy as jnp
from jax import lax
from jax.experimental import pallas as pl
from jax.experimental.pallas import tpu as pltpu
from jax.sharding import PartitionSpec as P

HEAD_DIM = 128
EPS = 1e-05
LOG2E = 1.4426950408889634
GELU_A = 0.7978845608028654
GELU_B = 0.044715
f32 = jnp.float32
bf16 = jnp.bfloat16

NN = (((1,), (0,)), ((), ()))
NT = (((1,), (1,)), ((), ()))
TN = (((0,), (0,)), ((), ()))


def dot(a, b, dims=NN):
    return lax.dot_general(a, b, dims, preferred_element_type=f32)


def normed(v):
    mean = jnp.mean(v, axis=-1, keepdims=True)
    centred = v - mean
    r = lax.rsqrt(jnp.mean(centred * centred, axis=-1, keepdims=True) + EPS)
    return centred * r, r


def fold(v):
    return jnp.sum(v.reshape(-1, 8, v.shape[-1]), axis=0)


def params(mib=8):
    return pltpu.CompilerParams(vmem_limit_bytes=mib * 2**20)


def cost(flops, nbytes):
    return pl.CostEstimate(flops=int(flops), bytes_accessed=int(nbytes), transcendentals=0)


def whole(n):
    return [pl.BlockSpec(memory_space=pltpu.VMEM)] * n


def sds(shape, dtype):
    return jax.ShapeDtypeStruct(shape, dtype)


def by_rows(length, step, init=None, block=128):
    return lax.fori_loop(0, length // block, lambda i, c: step(pl.ds(pl.multiple_of(i * block, block), block), c), init)


def call(kernel, ins, outs, name, flops=0, mib=8, at=None):
    flags = [] if at is None else [at]
    nbytes = sum(v.size * v.dtype.itemsize for v in (*ins, *outs))
    return pl.pallas_call(
        kernel,
        in_specs=[pl.BlockSpec(memory_space=pltpu.SMEM)] * len(flags) + whole(len(ins)),
        out_specs=whole(len(outs)),
        out_shape=list(outs),
        compiler_params=params(mib),
        cost_estimate=cost(flops, nbytes),
        name=name,
    )(*flags, *ins)


def prep_kernel(x_ref, c_ref, g_ref, a_ref, d_ref):
    def step(rows, _):
        a_ref[rows, :] = (normed(x_ref[rows, :])[0] * g_ref[...]).astype(bf16)
        d_ref[rows, :] = c_ref[rows, :].astype(bf16)

    by_rows(x_ref.shape[0], step)


def prep(x, cot, gain):
    return call(prep_kernel, (x, cot, gain), (sds(x.shape, bf16),) * 2, "prep", 10 * x.size)


def attend_kernel(a_ref, w_ref, qkv_ref, mixed_ref, lse_ref):
    scale = HEAD_DIM**-0.5 * LOG2E
    for c in range(3):
        qkv_ref[c] = dot(a_ref[...], w_ref[c]).astype(bf16)
    for h in range(w_ref.shape[2] // HEAD_DIM):
        cols = slice(h * HEAD_DIM, (h + 1) * HEAD_DIM)
        q, k, v = (qkv_ref[c, :, cols] for c in range(3))
        scores = dot(k, q, NT)
        top = jnp.max(scores, axis=0, keepdims=True)
        expd = jnp.exp2((scores - top) * scale)
        total = jnp.sum(expd, axis=0, keepdims=True)
        mixed = dot(v, expd.astype(bf16), TN) / total
        mixed_ref[:, cols] = mixed.T.astype(bf16)
        lse_ref[h : h + 1, :] = top * scale + jnp.log2(total)


def attend(a, w):
    length, width = a.shape
    local = w.shape[2]
    heads = local // HEAD_DIM
    outs = (sds((3, length, local), bf16), sds((length, local), bf16), sds((heads, length), f32))
    return call(attend_kernel, (a, w), outs, "attend", 6 * length * width * local + 16 * heads * length * length * HEAD_DIM, 12)


def project_kernel(n, *refs):
    mixed, w = refs[:n], refs[n : 2 * n]
    x_ref, g_ref, resid_ref, a_ref = refs[2 * n :]

    def step(rows, _):
        total = dot(mixed[0][rows, :], w[0][...])
        for j in range(1, n):
            total += dot(mixed[j][rows, :], w[j][...])
        resid = x_ref[rows, :] + total
        resid_ref[rows, :] = resid
        a_ref[rows, :] = (normed(resid)[0] * g_ref[...]).astype(bf16)

    by_rows(x_ref.shape[0], step)


def project(mixed, w, x, gain):
    flops = 2 * x.size * mixed[0].shape[1] * len(mixed)
    outs = (sds(x.shape, f32), sds(x.shape, bf16))
    return call(functools.partial(project_kernel, len(mixed)), (*mixed, *w, x, gain), outs, "project", flops)


def mlp_kernel(n, *refs):
    a_ref, d_ref = refs[:2]
    up, down = refs[2 : 2 + n], refs[2 + n : 2 + 2 * n]
    outs = refs[2 + 2 * n :]
    hid, dpre, grads = outs[:n], outs[n : 2 * n], outs[2 * n :]
    for j in range(n):
        u = dot(a_ref[...], up[j][...])
        d_hidden = dot(d_ref[...], down[j][...], NT)
        sq = u * u
        t = jnp.tanh(GELU_A * u * (1.0 + GELU_B * sq))
        half = 0.5 * (1.0 + t)
        hidden = (u * half).astype(bf16)
        slope = half + 0.5 * u * (1.0 - t * t) * (GELU_A * (1.0 + 3.0 * GELU_B * sq))
        d_pre = (d_hidden * slope).astype(bf16)
        hid[j][...] = hidden
        dpre[j][...] = d_pre
        grads[j][0] = dot(hidden, d_ref[...], TN).astype(bf16)
        grads[j][1] = dot(d_pre, a_ref[...], TN).astype(bf16)


def mlp(a, d, up, down):
    n = len(up)
    length, width = a.shape
    local = up[0].shape[1]
    act, grad = sds((length, local), bf16), sds((2, local, width), bf16)
    flops = 8 * length * width * local * n
    outs = call(functools.partial(mlp_kernel, n), (a, d, *up, *down), (act,) * (2 * n) + (grad,) * n, "mlp", flops, 12)
    return outs[:n], outs[n : 2 * n], outs[2 * n :]


def norm_back(d_a, v, gain):
    xhat, r = normed(v)
    e = d_a * gain
    back = r * (e - jnp.mean(e, axis=-1, keepdims=True) - xhat * jnp.mean(e * xhat, axis=-1, keepdims=True))
    return back, fold(d_a * xhat)


def mlp_back_kernel(n, *refs):
    d_pre, up = refs[:n], refs[n : 2 * n]
    resid_ref, c_ref, g_ref, dres_ref, datt_ref, gain_ref = refs[2 * n :]

    def step(rows, gain):
        total = dot(d_pre[0][rows, :], up[0][...], NT)
        for j in range(1, n):
            total += dot(d_pre[j][rows, :], up[j][...], NT)
        back, part = norm_back(total, resid_ref[rows, :], g_ref[...])
        d_resid = c_ref[rows, :] + back
        dres_ref[rows, :] = d_resid
        datt_ref[rows, :] = d_resid.astype(bf16)
        return gain + part

    gain_ref[...] = by_rows(c_ref.shape[0], step, jnp.zeros(gain_ref.shape, f32))


def mlp_back(d_pre, up, resid, cot, gain):
    n = len(up)
    flops = 2 * resid.size * up[0].shape[1] * n
    outs = (sds(resid.shape, f32), sds(resid.shape, bf16), sds((8, resid.shape[1]), f32))
    return call(functools.partial(mlp_back_kernel, n), (*d_pre, *up, resid, cot, gain), outs, "mlp_back", flops)


def mlp_out_kernel(n, *refs):
    hid, down = refs[:n], refs[n : 2 * n]
    resid_ref, out_ref = refs[2 * n :]

    def step(rows, _):
        total = resid_ref[rows, :]
        for j in range(n):
            total += dot(hid[j][rows, :], down[j][...])
        out_ref[rows, :] = total

    by_rows(resid_ref.shape[0], step)


def mlp_out(hid, down, resid):
    n = len(down)
    flops = 2 * resid.size * down[0].shape[0] * n
    return call(functools.partial(mlp_out_kernel, n), (*hid, *down, resid), (sds(resid.shape, f32),), "mlp_out", flops)[0]


def grad_out_kernel(n, *refs):
    d_ref, mixed, kept_ref, sent_ref = refs[0], refs[1 : 1 + n], refs[1 + n], refs[2 + n]
    for j in range(n):
        into = (kept_ref, sent_ref)[j // (n // 2)]
        into[j % (n // 2)] = dot(mixed[j][...], d_ref[...], TN).astype(bf16)


def grad_out(d, mixed):
    n = len(mixed)
    length, width = d.shape
    local = mixed[0].shape[1]
    outs = (sds((n // 2, local, width), bf16),) * 2
    return call(functools.partial(grad_out_kernel, n), (d, *mixed), outs, "grad_out", 2 * length * width * local * n)


def attend_back_kernel(added, a_ref, d_ref, w_ref, qkv_ref, lse_ref, *refs):
    scale = HEAD_DIM**-0.5
    got_ref = refs[0] if added else None
    dqkv_ref, grads = refs[added], refs[added + 1 :]
    d_mixed = dot(d_ref[...], w_ref[...], NT).astype(bf16)
    for h in range(w_ref.shape[0] // HEAD_DIM):
        cols = slice(h * HEAD_DIM, (h + 1) * HEAD_DIM)
        q, k, v = (qkv_ref[c, :, cols] for c in range(3))
        dm = d_mixed[:, cols]
        probs = jnp.exp2(dot(k, q, NT) * (scale * LOG2E) - lse_ref[h : h + 1, :])
        d_probs = dot(v, dm, NT)
        dqkv_ref[2, :, cols] = dot(probs.astype(bf16), dm).astype(bf16)
        delta = jnp.sum(d_probs * probs, axis=0, keepdims=True)
        d_scores = (probs * (d_probs - delta)).astype(bf16)
        dqkv_ref[1, :, cols] = (dot(d_scores, q) * scale).astype(bf16)
        dqkv_ref[0, :, cols] = (dot(k, d_scores, TN) * scale).T.astype(bf16)
    for c in range(3):
        grad = dot(dqkv_ref[c], a_ref[...], TN)
        if added:
            grads[c][...] = (grad + got_ref[c].astype(f32)).astype(bf16)
        else:
            grads[0][c] = grad.astype(bf16)


def attend_back(a, d, w, qkv, lse, got=None):
    length, width = a.shape
    local = w.shape[0]
    heads = local // HEAD_DIM
    added = got is not None
    one = sds((local, width), bf16)
    outs = call(
        functools.partial(attend_back_kernel, int(added)),
        (a, d, w, qkv, lse, *([got] if added else [])),
        (sds((3, length, local), bf16), *([one] * 3 if added else [sds((3, local, width), bf16)])),
        "attend_back",
        8 * length * width * local + 40 * heads * length * length * HEAD_DIM,
        12,
    )
    return outs[0], (list(outs[1:]) if added else outs[1])


def join_kernel(n, axes, at_ref, *refs):
    quarters, outs = refs[:4], refs[4:]
    width = quarters[0].shape[1]
    for p, quarter in enumerate(quarters):
        at = pl.multiple_of(at_ref[p] * width, width)
        i = 0
        for out, axis in zip(outs, axes, strict=True):
            if axis == 3:
                for c in range(3):
                    out[c, pl.ds(at, width), :] = quarter[i + c]
                i += 3
            elif axis == 0:
                out[pl.ds(at, width), :] = quarter[i]
                i += 1
            else:
                out[:, pl.ds(at, width)] = quarter[i]
                i += 1


def join(at, quarters, likes, axes):
    return call(functools.partial(join_kernel, len(likes), tuple(axes)), quarters, [sds(v.shape, v.dtype) for v in likes], "join", mib=4, at=at)


def cut_kernel(axes, at_ref, *refs):
    n = len(axes)
    for out, p in zip(refs[n:], (0, 2), strict=True):
        size = out.shape[1]
        place = pl.ds(pl.multiple_of(at_ref[p] * size, size), size)
        i = 0
        for v, axis in zip(refs[:n], axes, strict=True):
            if axis == 3:
                for c in range(3):
                    out[i + c] = v[c, place, :]
                i += 3
            else:
                out[i] = v[place, :] if axis == 0 else v[:, place]
                i += 1


def cut(at, arrays, axes):
    size = max(arrays[0].shape) // 4
    outs = (sds((sum(v.size for v in arrays) // (4 * size * size), size, size), bf16),) * 2
    return call(functools.partial(cut_kernel, tuple(axes)), arrays, outs, "cut", mib=4, at=at)


def half_of(ref, at, rows):
    place = pl.ds(pl.multiple_of(at * rows, rows), rows)
    return ref[place, :] if len(ref.shape) == 2 else ref[:, place, :]


def add_kernel(a_ref, b_ref, o_ref):
    o_ref[...] = a_ref[...] + b_ref[...]


def add(a, b):
    return call(add_kernel, (a, b), (sds(a.shape, a.dtype),), "add", a.size, 4)[0]


def split_add_kernel(at_ref, a_ref, b_ref, give_ref, keep_ref):
    rows = give_ref.shape[-2]
    for at, out in ((1 - at_ref[0], give_ref), (at_ref[0], keep_ref)):
        out[...] = half_of(a_ref, at, rows) + half_of(b_ref, at, rows)


def add_pair_kernel(a_ref, b_ref, x_ref, y_ref):
    for j, out in enumerate((x_ref, y_ref)):
        out[...] = a_ref[j] + b_ref[j]


def add_pair(a, b):
    return call(add_pair_kernel, (a, b), (sds(a.shape[1:], a.dtype),) * 2, "add", a.size, 4)


def halved(v):
    return sds((*v.shape[:-2], v.shape[-2] // 2, v.shape[-1]), v.dtype)


def split_add(at, a, b):
    return call(split_add_kernel, (a, b), (halved(a),) * 2, "split_add", a.size, 4, at)


def half_kernel(at_ref, a_ref, o_ref):
    o_ref[...] = half_of(a_ref, 1 - at_ref[4], o_ref.shape[-2])


def half(at, a):
    return call(half_kernel, (a,), (halved(a),), "half", a.size, 4, at)[0]


def half_add_kernel(at_ref, a_ref, b_ref, o_ref):
    o_ref[...] = half_of(a_ref, at_ref[4], o_ref.shape[-2]) + b_ref[...]


def half_add(at, a, b):
    return call(half_add_kernel, (a, b), (halved(a),), "half_add", a.size, 4, at)[0]


def pick_kernel(at_ref, a_ref, b_ref, o_ref):
    @pl.when(at_ref[5] == 1)
    def _():
        o_ref[...] = b_ref[...]

    @pl.when(at_ref[5] == 0)
    def _():
        o_ref[...] = a_ref[...]


def pick(at, a, b):
    return call(pick_kernel, (a, b), (sds(a.shape, a.dtype),), "pick", a.size, 4, at)[0]


def finish_kernel(flag, turned, index, at_ref, mine_ref, other_ref, *refs):
    out_ref = refs[-1]
    rows = mine_ref.shape[-2]
    for at, ref in ((at_ref[flag], mine_ref), (1 - at_ref[flag], other_ref)):
        place = pl.ds(pl.multiple_of(at * rows, rows), rows)
        v = (ref[...] if index is None else ref[index]).astype(f32)
        if turned:
            out_ref[0, :, place] = v.T
        else:
            out_ref[place, :] = v


def finish(at, flag, mine, other, turned, index=None, into=None, slot=0, slots=1):
    rows, width = mine.shape[-2:]
    shape = (slots, width, 2 * rows) if turned else (2 * rows, width)
    out_spec = pl.BlockSpec((1, width, 2 * rows), lambda i: (slot, 0, 0)) if turned else pl.BlockSpec(shape, lambda i: (0, 0))
    return pl.pallas_call(
        functools.partial(finish_kernel, flag, turned, index),
        grid=(1,),
        in_specs=[pl.BlockSpec(memory_space=pltpu.SMEM)] + whole(2) + ([pl.BlockSpec(memory_space=pl.ANY)] if into is not None else []),
        out_specs=out_spec,
        out_shape=sds(shape, f32),
        input_output_aliases={3: 0} if into is not None else {},
        compiler_params=params(6),
        cost_estimate=cost(0, 2e6),
        name="finish",
    )(at, mine, other, *([into] if into is not None else []))


def input_back_kernel(n, *refs):
    d_qkv, w = refs[:n], refs[n : 2 * n]
    x_ref, dres_ref, g_ref, other_ref, out_ref, gains_ref = refs[2 * n :]

    def step(rows, gain):
        total = None
        for j in range(n):
            for c in range(3):
                part = dot(d_qkv[j][c, rows, :], w[j][c], NT)
                total = part if total is None else total + part
        back, part = norm_back(total, x_ref[rows, :], g_ref[...])
        out_ref[rows, :] = dres_ref[rows, :] + back
        return gain + part

    gain = by_rows(x_ref.shape[0], step, jnp.zeros(other_ref.shape, f32))
    gains_ref[0:1, :] = jnp.sum(gain, axis=0, keepdims=True)
    gains_ref[1:2, :] = jnp.sum(other_ref[...], axis=0, keepdims=True)


def input_back(d_qkv, w, x, d_resid, gain, other):
    n = len(w)
    flops = 6 * x.size * w[0].shape[2] * n
    outs = (sds(x.shape, f32), sds((2, x.shape[1]), f32))
    return call(functools.partial(input_back_kernel, n), (*d_qkv, *w, x, d_resid, gain, other), outs, "input_back", flops, 12)


def swap(axis, size, bit):
    pairs = [(i, i ^ bit) for i in range(size)]
    return lambda v: lax.ppermute(v, axis, pairs)


def bits_of(size):
    return [1 << b for b in reversed(range(size.bit_length() - 1))]


class Run:
    def __init__(self):
        self.token = None

    def tie(self, v):
        if self.token is None:
            return v
        return lax.optimization_barrier((v, self.token))[0]

    def compute(self, step, first, *rest):
        outs = step(self.tie(first), *rest)
        self.token = jax.tree.leaves(outs)[0]
        return outs

    def send(self, move, v):
        v = self.tie(v)
        self.token = v
        return move(v)


class Names:
    def __getattr__(self, name):
        return name


N = Names()
ORDER = (
    N.sl_q, N.xp_q, N.prep, N.att0, N.xr_q, N.c0_q, N.c0_ou, N.sl_ou, N.xp_ou, N.xr_ou, N.c0_d, N.y_q, N.att2,
    N.sl_d, N.xp_d, N.z_q, N.xr_d, N.y_ou, N.as_q, N.cx_q, N.z_ou, N.att1, N.y_d, N.att3, N.z_d, N.as_ou,
    N.cx_ou, N.as_d, N.cx_d, N.proj, N.mlpR, N.cF1, N.mlpP, N.aF1, N.cF0, N.F_zx, N.mlpback, N.aF0, N.F_zo,
    N.ab3, N.F_ax, N.F_x, N.cQ1, N.gout, N.cO, N.ab2, N.ab1, N.Qa_x, N.Qb_x, N.cQ0, N.F_ao, N.F_a1, N.F_y,
    N.Qc_x, N.ab0, N.aO, N.O_x, N.Qa_a1, N.Qa_y, N.mlpout, N.F_a2, N.F_m, N.inback, N.Qb_a1, N.Qb_y, N.Qa_a2,
    N.Qa_z1, N.g0, N.Qb_a2, N.Qb_z1, N.Qc_a1, N.Qc_y, N.Qa_a3, N.g1, N.Qa_z2, N.Qb_a3, N.Qb_z2, N.Qc_a2, N.Qc_z1,
    N.O_a1, N.O_y, N.g2, N.Qa_a4, N.Qa_z3, N.Qc_a3, N.Qc_z2, N.Qb_a4, N.Qb_z3, N.O_a2, N.O_z1, N.Qa_a5, N.Qa_w,
    N.Qc_a4, N.Qc_z3, N.F_a3, N.F_w, N.O_a3, N.O_z2, N.Qb_a5, N.Qa_f, N.Qb_w, N.Qc_a5, N.Qc_w, N.O_a4, N.O_z3,
    N.g3, N.O_a5, N.O_w, N.Qb_f, N.Qc_f, N.F_f, N.O_f,
)
GROUPS = {"q": ("qkv",), "ou": ("out", "up"), "d": ("down",)}
CHUNKS = {"F": ("z", "F", None), "O": ("x", "O", 0), "Qa": ("x", "Q", 0), "Qb": ("x", "Q", 1), "Qc": ("x", "Q", 2)}
AXES = {"qkv": 3, "out": 1, "up": 0, "down": 1}


def per_device(
    sizes,
    inputs,
    norm1_gain,
    weight_qkv,
    weight_out,
    norm2_gain,
    weight_up,
    weight_down,
    cotangent,
):
    n_rep, n_dp, n_mp = sizes["rep"], sizes["dp"], sizes["mp"]
    if n_mp != 4 or n_rep != 2 or n_dp & (n_dp - 1) or n_dp < 2:
        raise ValueError("unsupported mesh")
    shape = inputs.shape
    x = inputs.reshape(shape[-2:])
    cot = cotangent.reshape(shape[-2:])
    gain1, gain2 = norm1_gain.reshape(1, -1), norm2_gain.reshape(1, -1)
    width = x.shape[1]
    run = Run()
    dp_at = lax.axis_index("dp")
    rep_at = lax.axis_index("rep")
    near_at = dp_at % 2
    line = n_dp == 4
    outer = (dp_at == 0) | (dp_at == n_dp - 1)
    line_at = jnp.where(outer, 0, 1)
    at = jnp.stack([rep_at, 1 - rep_at, 2 + near_at, 3 - near_at, line_at, outer.astype(jnp.int32), jnp.zeros_like(line_at)]).astype(jnp.int32)

    core = swap("mp", n_mp, 1)
    far = swap("mp", n_mp, 2)
    rep = swap("rep", n_rep, 1)
    near = swap("dp", n_dp, 1)
    own = {"qkv": weight_qkv, "out": weight_out, "up": weight_up, "down": weight_down}
    w = {k: [v, None, None, None] for k, v in own.items()}
    env = {}

    def gather_task(kind, g):
        names = GROUPS[g]
        if kind == "c0":
            for k in names:
                w[k][2] = run.send(core, own[k])
        elif kind == "sl":
            env["p", g], env["r", g] = run.compute(lambda *v: cut(at, v, [AXES[k] for k in names]), *[own[k] for k in names])
        elif kind == "xp":
            env["px", g] = run.send(far, env["p", g])
        elif kind == "xr":
            env["rx", g] = run.send(far, env["r", g])
        elif kind == "y":
            env["py", g] = run.send(rep, env["px", g])
        elif kind == "z":
            env["rz", g] = run.send(near, env["rx", g])
        elif kind == "as":
            outs = run.compute(
                lambda *v: join(at, v, [own[k] for k in names], [AXES[k] for k in names]),
                env["px", g], env["py", g], env["rx", g], env["rz", g],
            )
            for k, v in zip(names, outs, strict=True):
                w[k][1] = v
        elif kind == "cx":
            for k in names:
                w[k][3] = run.send(core, w[k][1])

    def over_dp(v):
        for bit in bits_of(n_dp):
            v = run.compute(add, v, run.send(swap("dp", n_dp, bit), v))
        return v

    def chunk_task(name, stage):
        mode, source, index = CHUNKS[name]
        c = env.setdefault(("chunk", name), {})

        def part(i):
            return env[source, i] if index is None else env[source, i][index]

        if mode == "z" and not line:
            mode = "zx"
        if mode == "x":
            if stage == "x":
                c["x"] = run.send(far, part(1))
            elif stage == "a1":
                c["give"], c["v"] = run.compute(lambda *v: split_add(at, *v), part(0), c["x"])
            elif stage == "y":
                c["y"] = run.send(rep, c["give"])
            elif stage == "a2":
                c["v"] = run.compute(add, c["v"], c["y"])
            elif stage == "z1" and line:
                c["z1"] = run.send(lambda v: lax.ppermute(v, "dp", [(0, 1), (3, 2)]), c["v"])
            elif stage == "a3" and line:
                c["v"] = run.compute(add, c["v"], c["z1"])
            elif stage == "z2" and line:
                c["z2"] = run.send(lambda v: lax.ppermute(v, "dp", [(1, 2), (2, 1)]), c["v"])
            elif stage == "a4":
                c["v"] = run.compute(add, c["v"], c["z2"]) if line else over_dp(c["v"])
            elif stage == "z3" and line:
                c["z3"] = run.send(lambda v: lax.ppermute(v, "dp", [(1, 0), (2, 3)]), c["v"])
            elif stage == "a5" and line:
                c["v"] = run.compute(lambda *v: pick(at, *v), c["v"], c["z3"])
            elif stage == "w":
                c["w"] = run.send(rep, c["v"])
            elif stage == "f":
                done(name, 0, c["v"], c["w"])
            return
        if stage in ("zo", "zx"):
            v = part(0 if stage == "zo" else 1)
            if mode == "z":
                give = run.compute(lambda t: half(at, t), v)
                c[stage] = run.send(near, give)
        elif stage in ("ao", "ax"):
            v = part(0 if stage == "ao" else 1)
            c[stage] = run.compute(lambda *t: half_add(at, *t), v, c["z" + stage[1]]) if mode == "z" else v
        elif stage == "x":
            c["x"] = run.send(far, c["ax"])
        elif stage == "a1":
            c["v"] = run.compute(add, c["ao"], c["x"])
        elif stage == "y":
            c["y"] = run.send(rep, c["v"])
        elif stage == "a2":
            c["v"] = run.compute(add, c["v"], c["y"])
        elif stage == "m":
            c["m"] = run.send(swap("dp", n_dp, 3), c["v"]) if mode == "z" else None
        elif stage == "a3":
            c["v"] = run.compute(add, c["v"], c["m"]) if mode == "z" else over_dp(c["v"])
        elif stage == "w":
            if mode == "z":
                c["w"] = run.send(near, c["v"])
            else:
                c["v"], c["w"] = (lax.slice_in_dim(c["v"], i * (c["v"].shape[-2] // 2), (i + 1) * (c["v"].shape[-2] // 2), axis=c["v"].ndim - 2) for i in range(2))
        elif stage == "f":
            done(name, 4 if mode == "z" else 6, c["v"], c["w"])

    def done(name, flag, mine, other):
        if name == "F":
            env["down"] = run.compute(lambda a, b: finish(at, flag, a, b, False, 0), mine, other)
            env["up"] = run.compute(lambda a, b: finish(at, flag, a, b, True, 1), mine, other)[0]
        elif name == "O":
            env["out"] = run.compute(lambda a, b: finish(at, flag, a, b, False), mine, other)
        else:
            slot = "abc".index(name[1])
            env["qkv"] = run.compute(lambda a, b: finish(at, flag, a, b, True, None, env.get("qkv"), slot, 3), mine, other)

    def gain_task(i):
        axis, size, bit = [("mp", n_mp, 1), ("mp", n_mp, 2), ("rep", n_rep, 1)][i] if i < 3 else ("dp", n_dp, None)
        if i < 3:
            env["g"] = run.compute(add, env["g"], run.send(swap(axis, size, bit), env["g"]))
        elif i == 3:
            env["g"] = over_dp(env["g"])

    def task(t):
        if t == "prep":
            env["a1"], env["dm"] = run.compute(lambda c, v, g: prep(v, c, g), cot, x, gain1)
        elif t[:3] == "att":
            j = int(t[3])
            env["att", j] = run.compute(attend, env["a1"], w["qkv"][j])
        elif t == "proj":
            env["resid"], env["a2"] = run.compute(
                lambda m, *rest: project([m, *rest[:3]], w["out"], x, gain2), *[env["att", j][1] for j in range(4)]
            )
        elif t in ("mlpP", "mlpR"):
            js = (0, 2) if t == "mlpP" else (1, 3)
            hid, dpre, grads = run.compute(lambda a: mlp(a, env["dm"], [w["up"][j] for j in js], [w["down"][j] for j in js]), env["a2"])
            for i, j in enumerate(js):
                env["hid", j], env["dpre", j], env["gF", j] = hid[i], dpre[i], grads[i]
        elif t in ("cF0", "cF1"):
            j = int(t[2])
            env["rF", j] = run.send(core, env["gF", 2 + j])
        elif t in ("aF0", "aF1"):
            j = int(t[2])
            env["F", j] = run.compute(add, env["gF", j], env["rF", j])
        elif t == "mlpback":
            env["dres"], env["datt"], env["gain2"] = run.compute(
                lambda d, *rest: mlp_back([d, *rest], w["up"], env["resid"], cot, gain2), *[env["dpre", j] for j in range(4)]
            )
        elif t == "mlpout":
            env["output"] = run.compute(lambda h, *rest: mlp_out([h, *rest], w["down"], env["resid"]), *[env["hid", j] for j in range(4)])
        elif t == "gout":
            env["gO"], env["sO"] = run.compute(lambda d: grad_out(d, [env["att", j][1] for j in range(4)]), env["datt"])
        elif t == "cO":
            env["rO"] = run.send(core, env["sO"])
        elif t == "aO":
            env["O", 0], env["O", 1] = ([v] for v in run.compute(add_pair, env["gO"], env["rO"]))
        elif t[:2] == "ab":
            j = int(t[2])
            got = env["rQ", j] if j < 2 else None
            env["dqkv", j], env["gQ", j] = run.compute(
                lambda d: attend_back(env["a1"], d, w["out"][j], env["att", j][0], env["att", j][2], got), env["datt"]
            )
            if j < 2:
                env["Q", j] = env["gQ", j]
        elif t in ("cQ0", "cQ1"):
            j = int(t[2])
            env["rQ", j] = run.send(core, env["gQ", 2 + j])
        elif t == "inback":
            env["gin"], env["g"] = run.compute(
                lambda d, *rest: input_back([d, *rest], w["qkv"], x, env["dres"], gain1, env["gain2"]), *[env["dqkv", j] for j in range(4)]
            )
        elif t[0] == "g" and t[1:].isdigit():
            gain_task(int(t[1:]))
        elif t.split("_")[1] in GROUPS:
            gather_task(*t.split("_"))
        else:
            chunk_task(*t.split("_"))

    for t in ORDER:
        task(t)
    return (
        env["output"].reshape(shape),
        env["gin"].reshape(shape),
        env["g"][0],
        env["qkv"],
        env["out"],
        env["g"][1],
        env["up"],
        env["down"],
    )


def solution(mesh):
    return jax.shard_map(
        functools.partial(per_device, dict(mesh.shape)),
        mesh=mesh,
        in_specs=(
            P(("rep", "mp"), "dp", None, None),
            P(),
            P(None, None, "mp"),
            P("mp", None),
            P(),
            P(None, "mp"),
            P("mp", None),
            P(("rep", "mp"), "dp", None, None),
        ),
        out_specs=(
            P(("rep", "mp"), "dp", None, None),
            P(("rep", "mp"), "dp", None, None),
            P(),
            P(None, None, "mp"),
            P("mp", None),
            P(),
            P(None, "mp"),
            P("mp", None),
        ),
        check_vma=False,
    )
```

```python
import functools

import jax
import jax.numpy as jnp
from jax import lax
from jax.experimental import pallas as pl
from jax.experimental.pallas import tpu as pltpu
from jax.sharding import PartitionSpec as P

HEAD_DIM = 128
EPS = 1e-05
LOG2E = 1.4426950408889634
GELU_A = 0.7978845608028654
GELU_B = 0.044715
f32 = jnp.float32
bf16 = jnp.bfloat16

NN = (((1,), (0,)), ((), ()))
NT = (((1,), (1,)), ((), ()))
TN = (((0,), (0,)), ((), ()))


def dot(a, b, dims=NN):
    return lax.dot_general(a, b, dims, preferred_element_type=f32)


def normed(v):
    mean = jnp.mean(v, axis=-1, keepdims=True)
    centred = v - mean
    r = lax.rsqrt(jnp.mean(centred * centred, axis=-1, keepdims=True) + EPS)
    return centred * r, r


def fold(v):
    return jnp.sum(v.reshape(-1, 8, v.shape[-1]), axis=0)


def params(mib=8):
    return pltpu.CompilerParams(vmem_limit_bytes=mib * 2**20)


def cost(flops, nbytes):
    return pl.CostEstimate(flops=1, bytes_accessed=1, transcendentals=0)


def whole(n):
    return [pl.BlockSpec(memory_space=pltpu.VMEM)] * n


def sds(shape, dtype):
    return jax.ShapeDtypeStruct(shape, dtype)


def by_rows(length, step, init=None, block=512):
    return lax.fori_loop(0, length // block, lambda i, c: step(pl.ds(pl.multiple_of(i * block, block), block), c), init)


def call(kernel, ins, outs, name, flops=0, mib=8, at=None):
    flags = [] if at is None else [at]
    nbytes = sum(v.size * v.dtype.itemsize for v in (*ins, *outs))
    return pl.pallas_call(
        kernel,
        in_specs=[pl.BlockSpec(memory_space=pltpu.SMEM)] * len(flags) + whole(len(ins)),
        out_specs=whole(len(outs)),
        out_shape=list(outs),
        compiler_params=params(mib),
        cost_estimate=cost(flops, nbytes),
        name=name,
    )(*flags, *ins)


def prep_kernel(x_ref, c_ref, g_ref, a_ref, d_ref):
    def step(rows, _):
        a_ref[rows, :] = (normed(x_ref[rows, :])[0] * g_ref[...]).astype(bf16)
        d_ref[rows, :] = c_ref[rows, :].astype(bf16)

    by_rows(x_ref.shape[0], step)


def prep(x, cot, gain):
    return call(prep_kernel, (x, cot, gain), (sds(x.shape, bf16),) * 2, "prep", 10 * x.size)


def attend_kernel(a_ref, w_ref, qkv_ref, mixed_ref, lse_ref):
    scale = HEAD_DIM**-0.5 * LOG2E
    for c in range(3):
        qkv_ref[c] = dot(a_ref[...], w_ref[c]).astype(bf16)
    for h in range(w_ref.shape[2] // HEAD_DIM):
        cols = slice(h * HEAD_DIM, (h + 1) * HEAD_DIM)
        q, k, v = (qkv_ref[c, :, cols] for c in range(3))
        scores = dot(k, q, NT)
        top = jnp.max(scores, axis=0, keepdims=True)
        expd = jnp.exp2((scores - top) * scale)
        total = jnp.sum(expd, axis=0, keepdims=True)
        mixed = dot(v, expd.astype(bf16), TN) / total
        mixed_ref[:, cols] = mixed.T.astype(bf16)
        lse_ref[h : h + 1, :] = top * scale + jnp.log2(total)


def attend(a, w):
    length, width = a.shape
    local = w.shape[2]
    heads = local // HEAD_DIM
    outs = (sds((3, length, local), bf16), sds((length, local), bf16), sds((heads, length), f32))
    return call(attend_kernel, (a, w), outs, "attend", 6 * length * width * local + 16 * heads * length * length * HEAD_DIM, 12)


def project_kernel(n, *refs):
    mixed, w = refs[:n], refs[n : 2 * n]
    x_ref, g_ref, resid_ref, a_ref = refs[2 * n :]

    def step(rows, _):
        total = dot(mixed[0][rows, :], w[0][...])
        for j in range(1, n):
            total += dot(mixed[j][rows, :], w[j][...])
        resid = x_ref[rows, :] + total
        resid_ref[rows, :] = resid
        a_ref[rows, :] = (normed(resid)[0] * g_ref[...]).astype(bf16)

    by_rows(x_ref.shape[0], step)


def project(mixed, w, x, gain):
    flops = 2 * x.size * mixed[0].shape[1] * len(mixed)
    outs = (sds(x.shape, f32), sds(x.shape, bf16))
    return call(functools.partial(project_kernel, len(mixed)), (*mixed, *w, x, gain), outs, "project", flops)


def mlp_kernel(n, *refs):
    a_ref, d_ref = refs[:2]
    up, down = refs[2 : 2 + n], refs[2 + n : 2 + 2 * n]
    outs = refs[2 + 2 * n :]
    hid, dpre, grads = outs[:n], outs[n : 2 * n], outs[2 * n :]
    for j in range(n):
        u = dot(a_ref[...], up[j][...])
        d_hidden = dot(d_ref[...], down[j][...], NT)
        sq = u * u
        t = jnp.tanh(GELU_A * u * (1.0 + GELU_B * sq))
        half = 0.5 * (1.0 + t)
        hidden = (u * half).astype(bf16)
        slope = half + 0.5 * u * (1.0 - t * t) * (GELU_A * (1.0 + 3.0 * GELU_B * sq))
        d_pre = (d_hidden * slope).astype(bf16)
        hid[j][...] = hidden
        dpre[j][...] = d_pre
        grads[j][0] = dot(hidden, d_ref[...], TN).astype(bf16)
        grads[j][1] = dot(d_pre, a_ref[...], TN).astype(bf16)


def mlp(a, d, up, down):
    n = len(up)
    length, width = a.shape
    local = up[0].shape[1]
    act, grad = sds((length, local), bf16), sds((2, local, width), bf16)
    flops = 8 * length * width * local * n
    outs = call(functools.partial(mlp_kernel, n), (a, d, *up, *down), (act,) * (2 * n) + (grad,) * n, "mlp", flops, 12)
    return outs[:n], outs[n : 2 * n], outs[2 * n :]


def norm_back(d_a, v, gain):
    xhat, r = normed(v)
    e = d_a * gain
    back = r * (e - jnp.mean(e, axis=-1, keepdims=True) - xhat * jnp.mean(e * xhat, axis=-1, keepdims=True))
    return back, fold(d_a * xhat)


def mlp_back_kernel(n, *refs):
    d_pre, up = refs[:n], refs[n : 2 * n]
    resid_ref, c_ref, g_ref, dres_ref, datt_ref, gain_ref = refs[2 * n :]

    def step(rows, gain):
        total = dot(d_pre[0][rows, :], up[0][...], NT)
        for j in range(1, n):
            total += dot(d_pre[j][rows, :], up[j][...], NT)
        back, part = norm_back(total, resid_ref[rows, :], g_ref[...])
        d_resid = c_ref[rows, :] + back
        dres_ref[rows, :] = d_resid
        datt_ref[rows, :] = d_resid.astype(bf16)
        return gain + part

    gain_ref[...] = by_rows(c_ref.shape[0], step, jnp.zeros(gain_ref.shape, f32))


def mlp_back(d_pre, up, resid, cot, gain):
    n = len(up)
    flops = 2 * resid.size * up[0].shape[1] * n
    outs = (sds(resid.shape, f32), sds(resid.shape, bf16), sds((8, resid.shape[1]), f32))
    return call(functools.partial(mlp_back_kernel, n), (*d_pre, *up, resid, cot, gain), outs, "mlp_back", flops)


def mlp_out_kernel(n, *refs):
    hid, down = refs[:n], refs[n : 2 * n]
    resid_ref, out_ref = refs[2 * n :]

    def step(rows, _):
        total = resid_ref[rows, :]
        for j in range(n):
            total += dot(hid[j][rows, :], down[j][...])
        out_ref[rows, :] = total

    by_rows(resid_ref.shape[0], step)


def mlp_out(hid, down, resid):
    n = len(down)
    flops = 2 * resid.size * down[0].shape[0] * n
    return call(functools.partial(mlp_out_kernel, n), (*hid, *down, resid), (sds(resid.shape, f32),), "mlp_out", flops)[0]


def grad_out_kernel(n, *refs):
    d_ref, mixed, kept_ref, sent_ref = refs[0], refs[1 : 1 + n], refs[1 + n], refs[2 + n]
    for j in range(n):
        into = (kept_ref, sent_ref)[j // (n // 2)]
        into[j % (n // 2)] = dot(mixed[j][...], d_ref[...], TN).astype(bf16)


def grad_out(d, mixed):
    n = len(mixed)
    length, width = d.shape
    local = mixed[0].shape[1]
    outs = (sds((n // 2, local, width), bf16),) * 2
    return call(functools.partial(grad_out_kernel, n), (d, *mixed), outs, "grad_out", 2 * length * width * local * n)


def attend_back_kernel(added, a_ref, d_ref, w_ref, qkv_ref, lse_ref, *refs):
    scale = HEAD_DIM**-0.5
    got_ref = refs[0] if added else None
    dqkv_ref, grads = refs[added], refs[added + 1 :]
    d_mixed = dot(d_ref[...], w_ref[...], NT).astype(bf16)
    for h in range(w_ref.shape[0] // HEAD_DIM):
        cols = slice(h * HEAD_DIM, (h + 1) * HEAD_DIM)
        q, k, v = (qkv_ref[c, :, cols] for c in range(3))
        dm = d_mixed[:, cols]
        probs = jnp.exp2(dot(k, q, NT) * (scale * LOG2E) - lse_ref[h : h + 1, :])
        d_probs = dot(v, dm, NT)
        dqkv_ref[2, :, cols] = dot(probs.astype(bf16), dm).astype(bf16)
        delta = jnp.sum(d_probs * probs, axis=0, keepdims=True)
        d_scores = (probs * (d_probs - delta)).astype(bf16)
        dqkv_ref[1, :, cols] = (dot(d_scores, q) * scale).astype(bf16)
        dqkv_ref[0, :, cols] = (dot(k, d_scores, TN) * scale).T.astype(bf16)
    for c in range(3):
        grad = dot(dqkv_ref[c], a_ref[...], TN)
        if added:
            grads[c][...] = (grad + got_ref[c].astype(f32)).astype(bf16)
        else:
            grads[0][c] = grad.astype(bf16)


def attend_back(a, d, w, qkv, lse, got=None):
    length, width = a.shape
    local = w.shape[0]
    heads = local // HEAD_DIM
    added = got is not None
    one = sds((local, width), bf16)
    outs = call(
        functools.partial(attend_back_kernel, int(added)),
        (a, d, w, qkv, lse, *([got] if added else [])),
        (sds((3, length, local), bf16), *([one] * 3 if added else [sds((3, local, width), bf16)])),
        "attend_back",
        8 * length * width * local + 40 * heads * length * length * HEAD_DIM,
        12,
    )
    return outs[0], (list(outs[1:]) if added else outs[1])


def join_kernel(n, axes, at_ref, *refs):
    quarters, outs = refs[:4], refs[4:]
    width = quarters[0].shape[1]
    for p, quarter in enumerate(quarters):
        at = pl.multiple_of(at_ref[p] * width, width)
        i = 0
        for out, axis in zip(outs, axes, strict=True):
            if axis == 3:
                for c in range(3):
                    out[c, pl.ds(at, width), :] = quarter[i + c]
                i += 3
            elif axis == 0:
                out[pl.ds(at, width), :] = quarter[i]
                i += 1
            else:
                out[:, pl.ds(at, width)] = quarter[i]
                i += 1


def join(at, quarters, likes, axes):
    return call(functools.partial(join_kernel, len(likes), tuple(axes)), quarters, [sds(v.shape, v.dtype) for v in likes], "join", mib=4, at=at)


def cut_kernel(axes, at_ref, *refs):
    n = len(axes)
    for out, p in zip(refs[n:], (0, 2), strict=True):
        size = out.shape[1]
        place = pl.ds(pl.multiple_of(at_ref[p] * size, size), size)
        i = 0
        for v, axis in zip(refs[:n], axes, strict=True):
            if axis == 3:
                for c in range(3):
                    out[i + c] = v[c, place, :]
                i += 3
            else:
                out[i] = v[place, :] if axis == 0 else v[:, place]
                i += 1


def cut(at, arrays, axes):
    size = max(arrays[0].shape) // 4
    outs = (sds((sum(v.size for v in arrays) // (4 * size * size), size, size), bf16),) * 2
    return call(functools.partial(cut_kernel, tuple(axes)), arrays, outs, "cut", mib=4, at=at)


def half_of(ref, at, rows):
    place = pl.ds(pl.multiple_of(at * rows, rows), rows)
    return ref[place, :] if len(ref.shape) == 2 else ref[:, place, :]


def add_kernel(a_ref, b_ref, o_ref):
    o_ref[...] = a_ref[...] + b_ref[...]


def add(a, b):
    return call(add_kernel, (a, b), (sds(a.shape, a.dtype),), "add", a.size, 4)[0]


def split_add_kernel(at_ref, a_ref, b_ref, give_ref, keep_ref):
    rows = give_ref.shape[-2]
    for at, out in ((1 - at_ref[0], give_ref), (at_ref[0], keep_ref)):
        out[...] = half_of(a_ref, at, rows) + half_of(b_ref, at, rows)


def add_pair_kernel(a_ref, b_ref, x_ref, y_ref):
    for j, out in enumerate((x_ref, y_ref)):
        out[...] = a_ref[j] + b_ref[j]


def add_pair(a, b):
    return call(add_pair_kernel, (a, b), (sds(a.shape[1:], a.dtype),) * 2, "add", a.size, 4)


def halved(v):
    return sds((*v.shape[:-2], v.shape[-2] // 2, v.shape[-1]), v.dtype)


def split_add(at, a, b):
    return call(split_add_kernel, (a, b), (halved(a),) * 2, "split_add", a.size, 4, at)


def half_kernel(at_ref, a_ref, o_ref):
    o_ref[...] = half_of(a_ref, 1 - at_ref[4], o_ref.shape[-2])


def half(at, a):
    return call(half_kernel, (a,), (halved(a),), "half", a.size, 4, at)[0]


def half_add_kernel(at_ref, a_ref, b_ref, o_ref):
    o_ref[...] = half_of(a_ref, at_ref[4], o_ref.shape[-2]) + b_ref[...]


def half_add(at, a, b):
    return call(half_add_kernel, (a, b), (halved(a),), "half_add", a.size, 4, at)[0]


def pick_kernel(at_ref, a_ref, b_ref, o_ref):
    @pl.when(at_ref[5] == 1)
    def _():
        o_ref[...] = b_ref[...]

    @pl.when(at_ref[5] == 0)
    def _():
        o_ref[...] = a_ref[...]


def pick(at, a, b):
    return call(pick_kernel, (a, b), (sds(a.shape, a.dtype),), "pick", a.size, 4, at)[0]


def finish_kernel(flag, turned, index, at_ref, mine_ref, other_ref, *refs):
    out_ref = refs[-1]
    rows = mine_ref.shape[-2]
    for at, ref in ((at_ref[flag], mine_ref), (1 - at_ref[flag], other_ref)):
        place = pl.ds(pl.multiple_of(at * rows, rows), rows)
        v = (ref[...] if index is None else ref[index]).astype(f32)
        if turned:
            out_ref[0, :, place] = v.T
        else:
            out_ref[place, :] = v


def finish(at, flag, mine, other, turned, index=None, into=None, slot=0, slots=1):
    rows, width = mine.shape[-2:]
    shape = (slots, width, 2 * rows) if turned else (2 * rows, width)
    out_spec = pl.BlockSpec((1, width, 2 * rows), lambda i: (slot, 0, 0)) if turned else pl.BlockSpec(shape, lambda i: (0, 0))
    return pl.pallas_call(
        functools.partial(finish_kernel, flag, turned, index),
        grid=(1,),
        in_specs=[pl.BlockSpec(memory_space=pltpu.SMEM)] + whole(2) + ([pl.BlockSpec(memory_space=pl.ANY)] if into is not None else []),
        out_specs=out_spec,
        out_shape=sds(shape, f32),
        input_output_aliases={3: 0} if into is not None else {},
        compiler_params=params(6),
        cost_estimate=cost(0, 2e6),
        name="finish",
    )(at, mine, other, *([into] if into is not None else []))


def input_back_kernel(n, *refs):
    d_qkv, w = refs[:n], refs[n : 2 * n]
    x_ref, dres_ref, g_ref, other_ref, out_ref, gains_ref = refs[2 * n :]

    def step(rows, gain):
        total = None
        for j in range(n):
            for c in range(3):
                part = dot(d_qkv[j][c, rows, :], w[j][c], NT)
                total = part if total is None else total + part
        back, part = norm_back(total, x_ref[rows, :], g_ref[...])
        out_ref[rows, :] = dres_ref[rows, :] + back
        return gain + part

    gain = by_rows(x_ref.shape[0], step, jnp.zeros(other_ref.shape, f32))
    gains_ref[0:1, :] = jnp.sum(gain, axis=0, keepdims=True)
    gains_ref[1:2, :] = jnp.sum(other_ref[...], axis=0, keepdims=True)


def input_back(d_qkv, w, x, d_resid, gain, other):
    n = len(w)
    flops = 6 * x.size * w[0].shape[2] * n
    outs = (sds(x.shape, f32), sds((2, x.shape[1]), f32))
    return call(functools.partial(input_back_kernel, n), (*d_qkv, *w, x, d_resid, gain, other), outs, "input_back", flops, 12)


def swap(axis, size, bit):
    pairs = [(i, i ^ bit) for i in range(size)]
    return lambda v: lax.ppermute(v, axis, pairs)


def bits_of(size):
    return [1 << b for b in reversed(range(size.bit_length() - 1))]


class Run:
    def __init__(self):
        self.token = None

    def tie(self, v):
        if self.token is None:
            return v
        return lax.optimization_barrier((v, self.token))[0]

    def compute(self, step, first, *rest):
        outs = step(self.tie(first), *rest)
        self.token = jax.tree.leaves(outs)[0]
        return outs

    def send(self, move, v):
        v = self.tie(v)
        self.token = v
        return move(v)


class Names:
    def __getattr__(self, name):
        return name


N = Names()
ORDER = (
    N.sl_q, N.xp_q, N.xr_q, N.c0_q, N.sl_ou, N.sl_d, N.c0_d, N.prep, N.att0, N.xr_ou, N.xp_d, N.att2, N.z_q,
    N.xp_ou, N.y_q, N.z_ou, N.xr_d, N.y_ou, N.y_d, N.as_q, N.att1, N.c0_ou, N.z_d, N.as_ou, N.cx_ou, N.cx_q,
    N.att3, N.as_d, N.cx_d, N.proj, N.mlpP, N.cF0, N.mlpR, N.mlpback, N.ab3, N.cQ1, N.ab2, N.cF1, N.cQ0, N.ab1,
    N.Qa_x, N.gout, N.cO, N.aF1, N.F_hx, N.F_zx, N.Qb_x, N.ab0, N.Qc_x, N.aF0, N.Qa_a1, N.Qa_y, N.F_ho, N.F_zo,
    N.inback, N.F_ax, N.F_x, N.Qb_a1, N.Qb_y, N.Qa_a2, N.Qa_z1, N.F_ao, N.aO, N.Qb_a2, N.Qb_z1, N.g0, N.Qa_a3,
    N.Qa_z2, N.F_a1, N.F_y, N.O_x, N.ga0, N.Qb_a3, N.Qb_z2, N.Qa_a4, N.Qa_z3, N.Qc_a1, N.Qc_y, N.Qa_a5, N.F_a2,
    N.Qa_w, N.g1, N.F_m, N.Qb_a4, N.Qb_z3, N.mlpout, N.Qc_a2, N.Qc_z1, N.O_a1, N.O_y, N.Qa_f, N.Qc_a3, N.Qb_a5,
    N.Qc_z2, N.ga1, N.Qb_w, N.O_a2, N.g2, N.O_z1, N.F_a3, N.F_w, N.ga2, N.g3, N.Qb_f, N.ga3, N.Qc_a4, N.Qc_z3,
    N.O_a3, N.O_z2, N.Qc_a5, N.Qc_w, N.O_a4, N.O_z3, N.F_f, N.g4, N.Qc_f, N.ga4, N.O_a5, N.O_w, N.O_f,
)
GROUPS = {"q": ("qkv",), "ou": ("out", "up"), "d": ("down",)}
CHUNKS = {"F": ("z", "F", None), "O": ("x", "O", 0), "Qa": ("x", "Q", 0), "Qb": ("x", "Q", 1), "Qc": ("x", "Q", 2)}
AXES = {"qkv": 3, "out": 1, "up": 0, "down": 1}


def per_device(
    sizes,
    inputs,
    norm1_gain,
    weight_qkv,
    weight_out,
    norm2_gain,
    weight_up,
    weight_down,
    cotangent,
):
    n_rep, n_dp, n_mp = sizes["rep"], sizes["dp"], sizes["mp"]
    if n_mp != 4 or n_rep != 2 or n_dp & (n_dp - 1) or n_dp < 2:
        raise ValueError("unsupported mesh")
    shape = inputs.shape
    x = inputs.reshape(shape[-2:])
    cot = cotangent.reshape(shape[-2:])
    gain1, gain2 = norm1_gain.reshape(1, -1), norm2_gain.reshape(1, -1)
    width = x.shape[1]
    run = Run()
    dp_at = lax.axis_index("dp")
    rep_at = lax.axis_index("rep")
    near_at = dp_at % 2
    line = n_dp == 4
    outer = (dp_at == 0) | (dp_at == n_dp - 1)
    line_at = jnp.where(outer, 0, 1)
    at = jnp.stack([rep_at, 1 - rep_at, 2 + near_at, 3 - near_at, line_at, outer.astype(jnp.int32), jnp.zeros_like(line_at)]).astype(jnp.int32)

    core = swap("mp", n_mp, 1)
    far = swap("mp", n_mp, 2)
    rep = swap("rep", n_rep, 1)
    near = swap("dp", n_dp, 1)
    own = {"qkv": weight_qkv, "out": weight_out, "up": weight_up, "down": weight_down}
    w = {k: [v, None, None, None] for k, v in own.items()}
    env = {}

    def gather_task(kind, g):
        names = GROUPS[g]
        if kind == "c0":
            for k in names:
                w[k][2] = run.send(core, own[k])
        elif kind == "sl":
            env["p", g], env["r", g] = run.compute(lambda *v: cut(at, v, [AXES[k] for k in names]), *[own[k] for k in names])
        elif kind == "xp":
            env["px", g] = run.send(far, env["p", g])
        elif kind == "xr":
            env["rx", g] = run.send(far, env["r", g])
        elif kind == "y":
            env["py", g] = run.send(rep, env["px", g])
        elif kind == "z":
            env["rz", g] = run.send(near, env["rx", g])
        elif kind == "as":
            outs = run.compute(
                lambda *v: join(at, v, [own[k] for k in names], [AXES[k] for k in names]),
                env["px", g], env["py", g], env["rx", g], env["rz", g],
            )
            for k, v in zip(names, outs, strict=True):
                w[k][1] = v
        elif kind == "cx":
            for k in names:
                w[k][3] = run.send(core, w[k][1])

    def over_dp(v):
        for bit in bits_of(n_dp):
            v = run.compute(add, v, run.send(swap("dp", n_dp, bit), v))
        return v

    def chunk_task(name, stage):
        mode, source, index = CHUNKS[name]
        c = env.setdefault(("chunk", name), {})

        def part(i):
            return env[source, i] if index is None else env[source, i][index]

        if mode == "z" and not line:
            mode = "zx"
        if mode == "x":
            if stage == "x":
                c["x"] = run.send(far, part(1))
            elif stage == "a1":
                c["give"], c["v"] = run.compute(lambda *v: split_add(at, *v), part(0), c["x"])
            elif stage == "y":
                c["y"] = run.send(rep, c["give"])
            elif stage == "a2":
                c["v"] = run.compute(add, c["v"], c["y"])
            elif stage == "z1" and line:
                c["z1"] = run.send(lambda v: lax.ppermute(v, "dp", [(0, 1), (3, 2)]), c["v"])
            elif stage == "a3" and line:
                c["v"] = run.compute(add, c["v"], c["z1"])
            elif stage == "z2" and line:
                c["z2"] = run.send(lambda v: lax.ppermute(v, "dp", [(1, 2), (2, 1)]), c["v"])
            elif stage == "a4":
                c["v"] = run.compute(add, c["v"], c["z2"]) if line else over_dp(c["v"])
            elif stage == "z3" and line:
                c["z3"] = run.send(lambda v: lax.ppermute(v, "dp", [(1, 0), (2, 3)]), c["v"])
            elif stage == "a5" and line:
                c["v"] = run.compute(lambda *v: pick(at, *v), c["v"], c["z3"])
            elif stage == "w":
                c["w"] = run.send(rep, c["v"])
            elif stage == "f":
                done(name, 0, c["v"], c["w"])
            return
        if stage in ("ho", "hx"):
            if mode == "z":
                c[stage] = run.compute(lambda t: half(at, t), part(0 if stage == "ho" else 1))
        elif stage in ("zo", "zx"):
            if mode == "z":
                c[stage] = run.send(near, c["h" + stage[1]])
        elif stage in ("ao", "ax"):
            v = part(0 if stage == "ao" else 1)
            c[stage] = run.compute(lambda *t: half_add(at, *t), v, c["z" + stage[1]]) if mode == "z" else v
        elif stage == "x":
            c["x"] = run.send(far, c["ax"])
        elif stage == "a1":
            c["v"] = run.compute(add, c["ao"], c["x"])
        elif stage == "y":
            c["y"] = run.send(rep, c["v"])
        elif stage == "a2":
            c["v"] = run.compute(add, c["v"], c["y"])
        elif stage == "m":
            c["m"] = run.send(swap("dp", n_dp, 3), c["v"]) if mode == "z" else None
        elif stage == "a3":
            c["v"] = run.compute(add, c["v"], c["m"]) if mode == "z" else over_dp(c["v"])
        elif stage == "w":
            if mode == "z":
                c["w"] = run.send(near, c["v"])
            else:
                c["v"], c["w"] = (lax.slice_in_dim(c["v"], i * (c["v"].shape[-2] // 2), (i + 1) * (c["v"].shape[-2] // 2), axis=c["v"].ndim - 2) for i in range(2))
        elif stage == "f":
            done(name, 4 if mode == "z" else 6, c["v"], c["w"])

    def done(name, flag, mine, other):
        if name == "F":
            env["down"] = run.compute(lambda a, b: finish(at, flag, a, b, False, 0), mine, other)
            env["up"] = run.compute(lambda a, b: finish(at, flag, a, b, True, 1), mine, other)[0]
        elif name == "O":
            env["out"] = run.compute(lambda a, b: finish(at, flag, a, b, False), mine, other)
        else:
            slot = "abc".index(name[1])
            env["qkv"] = run.compute(lambda a, b: finish(at, flag, a, b, True, None, env.get("qkv"), slot, 3), mine, other)

    dp_bits = bits_of(n_dp)
    gain_moves = [core, far, rep] + [swap("dp", n_dp, bit) for bit in dp_bits]

    def gain_task(i):
        if i < len(gain_moves):
            env["gr"] = run.send(gain_moves[i], env["g"])

    def gain_add(i):
        if i < len(gain_moves):
            env["g"] = run.compute(add, env["g"], env["gr"])
        if i == 4:
            for j in range(5, len(gain_moves)):
                gain_task(j)
                gain_add(j)

    def task(t):
        if t == "prep":
            env["a1"], env["dm"] = run.compute(lambda c, v, g: prep(v, c, g), cot, x, gain1)
        elif t[:3] == "att":
            j = int(t[3])
            env["att", j] = run.compute(attend, env["a1"], w["qkv"][j])
        elif t == "proj":
            env["resid"], env["a2"] = run.compute(
                lambda m, *rest: project([m, *rest[:3]], w["out"], x, gain2), *[env["att", j][1] for j in range(4)]
            )
        elif t in ("mlpP", "mlpR"):
            js = (0, 2) if t == "mlpP" else (1, 3)
            hid, dpre, grads = run.compute(lambda a: mlp(a, env["dm"], [w["up"][j] for j in js], [w["down"][j] for j in js]), env["a2"])
            for i, j in enumerate(js):
                env["hid", j], env["dpre", j], env["gF", j] = hid[i], dpre[i], grads[i]
        elif t in ("cF0", "cF1"):
            j = int(t[2])
            env["rF", j] = run.send(core, env["gF", 2 + j])
        elif t in ("aF0", "aF1"):
            j = int(t[2])
            env["F", j] = run.compute(add, env["gF", j], env["rF", j])
        elif t == "mlpback":
            env["dres"], env["datt"], env["gain2"] = run.compute(
                lambda d, *rest: mlp_back([d, *rest], w["up"], env["resid"], cot, gain2), *[env["dpre", j] for j in range(4)]
            )
        elif t == "mlpout":
            env["output"] = run.compute(lambda h, *rest: mlp_out([h, *rest], w["down"], env["resid"]), *[env["hid", j] for j in range(4)])
        elif t == "gout":
            env["gO"], env["sO"] = run.compute(lambda d: grad_out(d, [env["att", j][1] for j in range(4)]), env["datt"])
        elif t == "cO":
            env["rO"] = run.send(core, env["sO"])
        elif t == "aO":
            env["O", 0], env["O", 1] = ([v] for v in run.compute(add_pair, env["gO"], env["rO"]))
        elif t[:2] == "ab":
            j = int(t[2])
            got = env["rQ", j] if j < 2 else None
            env["dqkv", j], env["gQ", j] = run.compute(
                lambda d: attend_back(env["a1"], d, w["out"][j], env["att", j][0], env["att", j][2], got), env["datt"]
            )
            if j < 2:
                env["Q", j] = env["gQ", j]
        elif t in ("cQ0", "cQ1"):
            j = int(t[2])
            env["rQ", j] = run.send(core, env["gQ", 2 + j])
        elif t == "inback":
            env["gin"], env["g"] = run.compute(
                lambda d, *rest: input_back([d, *rest], w["qkv"], x, env["dres"], gain1, env["gain2"]), *[env["dqkv", j] for j in range(4)]
            )
        elif t[0] == "g" and t[1:].isdigit():
            gain_task(int(t[1:]))
        elif t[:2] == "ga":
            gain_add(int(t[2:]))
        elif t.split("_")[1] in GROUPS:
            gather_task(*t.split("_"))
        else:
            chunk_task(*t.split("_"))

    for t in ORDER:
        task(t)
    return (
        env["output"].reshape(shape),
        env["gin"].reshape(shape),
        env["g"][0],
        env["qkv"],
        env["out"],
        env["g"][1],
        env["up"],
        env["down"],
    )


def solution(mesh):
    return jax.shard_map(
        functools.partial(per_device, dict(mesh.shape)),
        mesh=mesh,
        in_specs=(
            P(("rep", "mp"), "dp", None, None),
            P(),
            P(None, None, "mp"),
            P("mp", None),
            P(),
            P(None, "mp"),
            P("mp", None),
            P(("rep", "mp"), "dp", None, None),
        ),
        out_specs=(
            P(("rep", "mp"), "dp", None, None),
            P(("rep", "mp"), "dp", None, None),
            P(),
            P(None, None, "mp"),
            P("mp", None),
            P(),
            P(None, "mp"),
            P("mp", None),
        ),
        check_vma=False,
    )
```

```python
import functools

import jax
import jax.numpy as jnp
from jax import lax
from jax.experimental import pallas as pl
from jax.experimental.pallas import tpu as pltpu
from jax.sharding import PartitionSpec as P

HEAD_DIM = 128
EPS = 1e-05
LOG2E = 1.4426950408889634
GELU_A = 0.7978845608028654
GELU_B = 0.044715
f32 = jnp.float32
bf16 = jnp.bfloat16

NN = (((1,), (0,)), ((), ()))
NT = (((1,), (1,)), ((), ()))
TN = (((0,), (0,)), ((), ()))


def dot(a, b, dims=NN):
    return lax.dot_general(a, b, dims, preferred_element_type=f32)


def normed(v):
    mean = jnp.mean(v, axis=-1, keepdims=True)
    centred = v - mean
    r = lax.rsqrt(jnp.mean(centred * centred, axis=-1, keepdims=True) + EPS)
    return centred * r, r


def fold(v):
    return jnp.sum(v.reshape(-1, 8, v.shape[-1]), axis=0)


def params(mib=8):
    return pltpu.CompilerParams(vmem_limit_bytes=mib * 2**20)


def cost():
    return pl.CostEstimate(flops=1, bytes_accessed=1, transcendentals=0)


def whole(n):
    return [pl.BlockSpec(memory_space=pltpu.VMEM)] * n


def sds(shape, dtype):
    return jax.ShapeDtypeStruct(shape, dtype)


def by_rows(length, step, init=None, block=512):
    return lax.fori_loop(0, length // block, lambda i, c: step(pl.ds(pl.multiple_of(i * block, block), block), c), init)


def call(kernel, ins, outs, name, mib=8, at=None):
    flags = [] if at is None else [at]
    return pl.pallas_call(
        kernel,
        in_specs=[pl.BlockSpec(memory_space=pltpu.SMEM)] * len(flags) + whole(len(ins)),
        out_specs=whole(len(outs)),
        out_shape=list(outs),
        compiler_params=params(mib),
        cost_estimate=cost(),
        name=name,
    )(*flags, *ins)


def matrices(refs):
    return (lambda c: refs[0][c]) if len(refs) == 1 else (lambda c: refs[c][...])


def prep_kernel(x_ref, c_ref, g_ref, a_ref, d_ref):
    def step(rows, _):
        a_ref[rows, :] = (normed(x_ref[rows, :])[0] * g_ref[...]).astype(bf16)
        d_ref[rows, :] = c_ref[rows, :].astype(bf16)

    by_rows(x_ref.shape[0], step)


def prep(x, cot, gain):
    return call(prep_kernel, (x, cot, gain), (sds(x.shape, bf16),) * 2, "prep")


def attend_kernel(n, a_ref, *refs):
    w, (qkv_ref, mixed_ref, lse_ref) = matrices(refs[:n]), refs[n:]
    scale = HEAD_DIM**-0.5 * LOG2E
    for c in range(3):
        qkv_ref[c] = dot(a_ref[...], w(c)).astype(bf16)
    for h in range(qkv_ref.shape[2] // HEAD_DIM):
        cols = slice(h * HEAD_DIM, (h + 1) * HEAD_DIM)
        q, k, v = (qkv_ref[c, :, cols] for c in range(3))
        scores = dot(k, q, NT)
        top = jnp.max(scores, axis=0, keepdims=True)
        expd = jnp.exp2((scores - top) * scale)
        total = jnp.sum(expd, axis=0, keepdims=True)
        mixed = dot(v, expd.astype(bf16), TN) / total
        mixed_ref[:, cols] = mixed.T.astype(bf16)
        lse_ref[h : h + 1, :] = top * scale + jnp.log2(total)


def attend(a, w):
    length, local = a.shape[0], w[0].shape[-1]
    outs = (sds((3, length, local), bf16), sds((length, local), bf16), sds((local // HEAD_DIM, length), f32))
    return call(functools.partial(attend_kernel, len(w)), (a, *w), outs, "attend", 12)


def project_kernel(n, *refs):
    mixed, w = refs[:n], refs[n : 2 * n]
    x_ref, g_ref, resid_ref, a_ref = refs[2 * n :]

    def step(rows, _):
        total = dot(mixed[0][rows, :], w[0][...])
        for j in range(1, n):
            total += dot(mixed[j][rows, :], w[j][...])
        resid = x_ref[rows, :] + total
        resid_ref[rows, :] = resid
        a_ref[rows, :] = (normed(resid)[0] * g_ref[...]).astype(bf16)

    by_rows(x_ref.shape[0], step)


def project(mixed, w, x, gain):
    outs = (sds(x.shape, f32), sds(x.shape, bf16))
    return call(functools.partial(project_kernel, len(mixed)), (*mixed, *w, x, gain), outs, "project")


def mlp_kernel(n, *refs):
    a_ref, d_ref = refs[:2]
    up, down = refs[2 : 2 + n], refs[2 + n : 2 + 2 * n]
    outs = refs[2 + 2 * n :]
    hid, dpre, grads = outs[:n], outs[n : 2 * n], outs[2 * n :]
    for j in range(n):
        u = dot(a_ref[...], up[j][...])
        d_hidden = dot(d_ref[...], down[j][...], NT)
        sq = u * u
        t = jnp.tanh(GELU_A * u * (1.0 + GELU_B * sq))
        half = 0.5 * (1.0 + t)
        hidden = (u * half).astype(bf16)
        slope = half + 0.5 * u * (1.0 - t * t) * (GELU_A * (1.0 + 3.0 * GELU_B * sq))
        d_pre = (d_hidden * slope).astype(bf16)
        hid[j][...] = hidden
        dpre[j][...] = d_pre
        grads[2 * j][...] = dot(hidden, d_ref[...], TN).astype(bf16)
        grads[2 * j + 1][...] = dot(d_pre, a_ref[...], TN).astype(bf16)


def mlp(a, d, up, down):
    n = len(up)
    length, width = a.shape
    local = up[0].shape[1]
    act, grad = sds((length, local), bf16), sds((local, width), bf16)
    outs = call(functools.partial(mlp_kernel, n), (a, d, *up, *down), (act,) * (2 * n) + (grad,) * (2 * n), "mlp", 12)
    return outs[:n], outs[n : 2 * n], [outs[2 * n + 2 * j : 2 * n + 2 * j + 2] for j in range(n)]


def norm_back(d_a, v, gain):
    xhat, r = normed(v)
    e = d_a * gain
    back = r * (e - jnp.mean(e, axis=-1, keepdims=True) - xhat * jnp.mean(e * xhat, axis=-1, keepdims=True))
    return back, fold(d_a * xhat)


def mlp_back_kernel(n, *refs):
    d_pre, up = refs[:n], refs[n : 2 * n]
    resid_ref, c_ref, g_ref, dres_ref, datt_ref, gain_ref = refs[2 * n :]

    def step(rows, gain):
        total = dot(d_pre[0][rows, :], up[0][...], NT)
        for j in range(1, n):
            total += dot(d_pre[j][rows, :], up[j][...], NT)
        back, part = norm_back(total, resid_ref[rows, :], g_ref[...])
        d_resid = c_ref[rows, :] + back
        dres_ref[rows, :] = d_resid
        datt_ref[rows, :] = d_resid.astype(bf16)
        return gain + part

    gain_ref[...] = by_rows(c_ref.shape[0], step, jnp.zeros(gain_ref.shape, f32))


def mlp_back(d_pre, up, resid, cot, gain):
    n = len(up)
    outs = (sds(resid.shape, f32), sds(resid.shape, bf16), sds((8, resid.shape[1]), f32))
    return call(functools.partial(mlp_back_kernel, n), (*d_pre, *up, resid, cot, gain), outs, "mlp_back")


def mlp_out_kernel(n, *refs):
    hid, down = refs[:n], refs[n : 2 * n]
    resid_ref, out_ref = refs[2 * n :]

    def step(rows, _):
        total = resid_ref[rows, :]
        for j in range(n):
            total += dot(hid[j][rows, :], down[j][...])
        out_ref[rows, :] = total

    by_rows(resid_ref.shape[0], step)


def mlp_out(hid, down, resid):
    n = len(down)
    return call(functools.partial(mlp_out_kernel, n), (*hid, *down, resid), (sds(resid.shape, f32),), "mlp_out")[0]


def grad_out_kernel(n, d_ref, *refs):
    for mixed, out in zip(refs[:n], refs[n:], strict=True):
        out[...] = dot(mixed[...], d_ref[...], TN).astype(bf16)


def grad_out(d, mixed):
    n = len(mixed)
    outs = (sds((mixed[0].shape[1], d.shape[1]), bf16),) * n
    return call(functools.partial(grad_out_kernel, n), (d, *mixed), outs, "grad_out")


def attend_back_kernel(added, a_ref, d_ref, w_ref, qkv_ref, lse_ref, *refs):
    scale = HEAD_DIM**-0.5
    got, dqkv_ref, grads = refs[:added], refs[added], refs[added + 1 :]
    d_mixed = dot(d_ref[...], w_ref[...], NT).astype(bf16)
    for h in range(w_ref.shape[0] // HEAD_DIM):
        cols = slice(h * HEAD_DIM, (h + 1) * HEAD_DIM)
        q, k, v = (qkv_ref[c, :, cols] for c in range(3))
        dm = d_mixed[:, cols]
        probs = jnp.exp2(dot(k, q, NT) * (scale * LOG2E) - lse_ref[h : h + 1, :])
        d_probs = dot(v, dm, NT)
        dqkv_ref[2, :, cols] = dot(probs.astype(bf16), dm).astype(bf16)
        delta = jnp.sum(d_probs * probs, axis=0, keepdims=True)
        d_scores = (probs * (d_probs - delta)).astype(bf16)
        dqkv_ref[1, :, cols] = (dot(d_scores, q) * scale).astype(bf16)
        dqkv_ref[0, :, cols] = (dot(k, d_scores, TN) * scale).T.astype(bf16)
    for c in range(3):
        grad = dot(dqkv_ref[c], a_ref[...], TN)
        grads[c][...] = (grad + got[c][...].astype(f32) if added else grad).astype(bf16)


def attend_back(a, d, w, qkv, lse, got=()):
    length, width = a.shape
    local = w.shape[0]
    outs = (sds((3, length, local), bf16), *[sds((local, width), bf16)] * 3)
    outs = call(functools.partial(attend_back_kernel, len(got)), (a, d, w, qkv, lse, *got), outs, "attend_back", 12)
    return outs[0], outs[1:]


def join_kernel(axes, at_ref, *refs):
    quarters, outs = refs[:4], refs[4:]
    width = quarters[0].shape[1]
    for p, quarter in enumerate(quarters):
        place = pl.ds(pl.multiple_of(at_ref[p] * width, width), width)
        for i, (out, axis) in enumerate(zip(outs, axes, strict=True)):
            if axis == 0:
                out[place, :] = quarter[i]
            else:
                out[:, place] = quarter[i]


def join(at, quarters, likes, axes):
    flat = [(v.shape[-2:], 0 if axis == 3 else axis) for v, axis in zip(likes, axes, strict=True) for _ in range(v.size // (v.shape[-1] * v.shape[-2]))]
    outs = [sds(shape, bf16) for shape, _ in flat]
    return call(functools.partial(join_kernel, tuple(axis for _, axis in flat)), quarters, outs, "join", 4, at)


def cut_kernel(axes, at_ref, *refs):
    n = len(axes)
    for out, p in zip(refs[n:], (0, 2), strict=True):
        size = out.shape[1]
        place = pl.ds(pl.multiple_of(at_ref[p] * size, size), size)
        i = 0
        for v, axis in zip(refs[:n], axes, strict=True):
            if axis == 3:
                for c in range(3):
                    out[i + c] = v[c, place, :]
                i += 3
            else:
                out[i] = v[place, :] if axis == 0 else v[:, place]
                i += 1


def cut(at, arrays, axes):
    size = max(arrays[0].shape) // 4
    outs = (sds((sum(v.size for v in arrays) // (4 * size * size), size, size), bf16),) * 2
    return call(functools.partial(cut_kernel, tuple(axes)), arrays, outs, "cut", 4, at)


def half_of(ref, at, rows):
    place = pl.ds(pl.multiple_of(at * rows, rows), rows)
    return ref[place, :] if len(ref.shape) == 2 else ref[:, place, :]


def add_kernel(a_ref, b_ref, o_ref):
    o_ref[...] = a_ref[...] + b_ref[...]


def add(a, b):
    return call(add_kernel, (a, b), (sds(a.shape, a.dtype),), "add", 4)[0]


def halved(shape, n=None):
    half = (shape[-2] // 2, shape[-1])
    return sds(half if n is None else (n, *half), bf16)


def split_add_kernel(n, at_ref, *refs):
    a, b, (give_ref, keep_ref) = refs[:n], refs[n : 2 * n], refs[2 * n :]
    rows = give_ref.shape[-2]
    for at, out in ((1 - at_ref[0], give_ref), (at_ref[0], keep_ref)):
        for i in range(n):
            total = half_of(a[i], at, rows) + half_of(b[i], at, rows)
            if len(out.shape) == 2:
                out[...] = total
            else:
                out[i] = total


def split_add(at, a, b):
    n = len(a)
    outs = (halved(a[0].shape, None if n == 1 else n),) * 2
    return call(functools.partial(split_add_kernel, n), (*a, *b), outs, "split_add", 4, at)


EXTRA = 16


def pack_kernel(*refs):
    gains, got_gains, outs = refs[4], refs[5], refs[6:]
    total = (gains[...] + got_gains[...]).astype(bf16)
    for a, b, out in zip(refs[:2], refs[2:4], outs, strict=True):
        rows = a.shape[0]
        out[0:rows, :] = a[...] + b[...]
        out[rows : rows + EXTRA, :] = jnp.concatenate([total, jnp.zeros((EXTRA - total.shape[0], total.shape[1]), bf16)])


def pack(kept, sent, got, gains, got_gains):
    rows, width = kept.shape
    return call(pack_kernel, (kept, sent, *got, gains, got_gains), (sds((rows + EXTRA, width), bf16),) * 2, "pack", 4)


def split_packed_kernel(at_ref, a_ref, b_ref, give_ref, keep_ref):
    rows = give_ref.shape[0] - EXTRA
    extra = slice(2 * rows, 2 * rows + EXTRA)
    gains = a_ref[extra, :] + b_ref[extra, :]
    for at, out in ((1 - at_ref[0], give_ref), (at_ref[0], keep_ref)):
        out[0:rows, :] = half_of(a_ref, at, rows) + half_of(b_ref, at, rows)
        out[rows : rows + EXTRA, :] = gains


def split_packed(at, a, b):
    shape = ((a.shape[0] - EXTRA) // 2 + EXTRA, a.shape[1])
    return call(split_packed_kernel, (a, b), (sds(shape, bf16),) * 2, "split_add", 4, at)


def finish_packed_kernel(at_ref, mine_ref, other_ref, out_ref, gain1_ref, gain2_ref):
    rows = out_ref.shape[0] // 2
    for at, ref in ((at_ref[0], mine_ref), (1 - at_ref[0], other_ref)):
        out_ref[pl.ds(pl.multiple_of(at * rows, rows), rows), :] = ref[0:rows, :].astype(f32)
    gains = mine_ref[rows : rows + EXTRA, :].astype(f32)
    gain1_ref[...] = gains[0:1, :]
    gain2_ref[...] = gains[1:2, :]


def finish_packed(at, mine, other):
    rows, width = 2 * (mine.shape[0] - EXTRA), mine.shape[1]
    outs = (sds((rows, width), f32), sds((1, width), f32), sds((1, width), f32))
    return call(finish_packed_kernel, (mine, other), outs, "finish", 6, at)


def pick_kernel(at_ref, a_ref, b_ref, o_ref):
    @pl.when(at_ref[4] == 1)
    def _():
        o_ref[...] = b_ref[...]

    @pl.when(at_ref[4] == 0)
    def _():
        o_ref[...] = a_ref[...]


def pick(at, a, b):
    return call(pick_kernel, (a, b), (sds(a.shape, a.dtype),), "pick", 4, at)[0]


def placed(ref, at, index=None):
    rows = ref.shape[-2]
    return pl.ds(pl.multiple_of(at * rows, rows), rows), (ref[...] if index is None else ref[index]).astype(f32)


def finish_kernel(turned, at_ref, mine_ref, other_ref, *outs):
    for at, ref in ((at_ref[0], mine_ref), (1 - at_ref[0], other_ref)):
        for i, (out, turn) in enumerate(zip(outs, turned, strict=True)):
            place, v = placed(ref, at, i if len(turned) > 1 else None)
            if turn:
                out[:, place] = v.T
            else:
                out[place, :] = v


def finish(at, mine, other, turned):
    rows, width = 2 * mine.shape[-2], mine.shape[-1]
    outs = [sds((width, rows) if turn else (rows, width), f32) for turn in turned]
    return call(functools.partial(finish_kernel, turned), (mine, other), outs, "finish", 6, at)


def finish_slot_kernel(at_ref, mine_ref, other_ref, *refs):
    for at, ref in ((at_ref[0], mine_ref), (1 - at_ref[0], other_ref)):
        place, v = placed(ref, at)
        refs[-1][0, :, place] = v.T


def finish_slot(at, mine, other, slot, slots, into):
    rows, width = mine.shape
    spec = pl.BlockSpec(memory_space=pltpu.VMEM)
    return pl.pallas_call(
        finish_slot_kernel,
        grid=(1,),
        in_specs=[pl.BlockSpec(memory_space=pltpu.SMEM), spec, spec] + [pl.BlockSpec(memory_space=pl.ANY)] * (into is not None),
        out_specs=pl.BlockSpec((1, width, 2 * rows), lambda i: (slot, 0, 0)),
        out_shape=sds((slots, width, 2 * rows), f32),
        input_output_aliases={} if into is None else {3: 0},
        compiler_params=params(6),
        cost_estimate=cost(),
        name="finish",
    )(at, mine, other, *([] if into is None else [into]))


def input_back_kernel(n, counts, *refs):
    d_qkv, refs = refs[:n], refs[n:]
    w = []
    for count in counts:
        w.append(matrices(refs[:count]))
        refs = refs[count:]
    x_ref, dres_ref, g_ref, other_ref, out_ref, gains_ref = refs

    def step(rows, gain):
        total = None
        for j in range(n):
            for c in range(3):
                part = dot(d_qkv[j][c, rows, :], w[j](c), NT)
                total = part if total is None else total + part
        back, part = norm_back(total, x_ref[rows, :], g_ref[...])
        out_ref[rows, :] = dres_ref[rows, :] + back
        return gain + part

    gain = by_rows(x_ref.shape[0], step, jnp.zeros(other_ref.shape, f32))
    gains_ref[0:1, :] = jnp.sum(gain, axis=0, keepdims=True)
    gains_ref[1:2, :] = jnp.sum(other_ref[...], axis=0, keepdims=True)


def input_back(d_qkv, w, x, d_resid, gain, other):
    outs = (sds(x.shape, f32), sds((2, x.shape[1]), f32))
    kernel = functools.partial(input_back_kernel, len(w), tuple(len(v) for v in w))
    return call(kernel, (*d_qkv, *[m for v in w for m in v], x, d_resid, gain, other), outs, "input_back", 12)


def swap(axis, size, bit):
    pairs = [(i, i ^ bit) for i in range(size)]
    return lambda v: lax.ppermute(v, axis, pairs)


def bits_of(size):
    return [1 << b for b in reversed(range(size.bit_length() - 1))]


class Run:
    def __init__(self):
        self.token = None

    def tie(self, v):
        if self.token is None:
            return v
        return lax.optimization_barrier((v, self.token))[0]

    def compute(self, step, first, *rest):
        outs = step(self.tie(first), *rest)
        self.token = jax.tree.leaves(outs)[0]
        return outs

    def send(self, move, v):
        v = self.tie(v)
        self.token = v
        return move(v)


class Names:
    def __getattr__(self, name):
        return name


N = Names()
ORDER = (
    N.x_d, N.c0_ou, N.sl_q, N.xp_q, N.c0_q, N.prep, N.sl_ou, N.xr_q, N.y_q, N.xr_ou, N.xp_ou, N.att0, N.z_q,
    N.z_ou, N.att2, N.as_q, N.y_ou, N.cx_q, N.att1, N.as_ou, N.cx_ou, N.cx_d, N.att3, N.c0_d, N.proj, N.mlpR,
    N.cF1, N.mlpP, N.cF0, N.aF1, N.F_yx, N.mlpback, N.gout, N.aF0, N.ab3, N.cQ1, N.F_yo, N.F_ax, N.F_x, N.ab1,
    N.Qb_x, N.cO, N.ab2, N.Qc_x, N.cQ0, N.Qa_x, N.F_ao, N.F_a2, N.F_z1, N.ab0, N.inback, N.g0, N.Qa_a1, N.aO,
    N.O_x, N.F_a3, N.F_z2, N.Qa_y, N.Qa_a2, N.Qa_z1, N.Qb_a1, N.Qb_y, N.F_a4, N.Qa_a3, N.F_z3, N.Qb_a2, N.Qa_z2,
    N.Qb_z1, N.O_a1, N.O_y, N.Qb_a3, N.Qb_z2, N.F_a5, N.O_a2, N.Qa_a4, N.O_z1, N.Qa_z3, N.Qc_a1, N.Qc_y, N.Qb_a4,
    N.F_w, N.Qc_a2, N.Qc_z1, N.O_a3, N.Qa_a5, N.Qb_z3, N.O_z2, N.Qc_a3, N.Qa_w, N.Qc_z2, N.O_a4, N.F_f, N.Qb_a5,
    N.Qb_w, N.O_z3, N.Qc_a4, N.Qa_f, N.Qc_z3, N.O_a5, N.O_w, N.Qb_f, N.mlpout, N.Qc_a5, N.Qc_w, N.O_f, N.Qc_f,
)
GROUPS = {"q": ("qkv",), "ou": ("out", "up"), "d": ("down",)}
CHUNKS = {"F": "F", "O": "O", "Qa": "Q", "Qb": "Q", "Qc": "Q"}
AXES = {"qkv": 3, "out": 1, "up": 0, "down": 1}


def per_device(
    sizes,
    inputs,
    norm1_gain,
    weight_qkv,
    weight_out,
    norm2_gain,
    weight_up,
    weight_down,
    cotangent,
):
    n_rep, n_dp, n_mp = sizes["rep"], sizes["dp"], sizes["mp"]
    if n_mp != 4 or n_rep != 2 or n_dp & (n_dp - 1) or n_dp < 2:
        raise ValueError("unsupported mesh")
    shape = inputs.shape
    x = inputs.reshape(shape[-2:])
    cot = cotangent.reshape(shape[-2:])
    gain1, gain2 = norm1_gain.reshape(1, -1), norm2_gain.reshape(1, -1)
    width = x.shape[1]
    run = Run()
    dp_at = lax.axis_index("dp")
    rep_at = lax.axis_index("rep")
    near_at = dp_at % 2
    line = n_dp == 4
    outer = (dp_at == 0) | (dp_at == n_dp - 1)
    at = jnp.stack([rep_at, 1 - rep_at, 2 + near_at, 3 - near_at, outer.astype(jnp.int32)]).astype(jnp.int32)

    core = swap("mp", n_mp, 1)
    far = swap("mp", n_mp, 2)
    rep = swap("rep", n_rep, 1)
    near = swap("dp", n_dp, 1)
    own = {"qkv": weight_qkv, "out": weight_out, "up": weight_up, "down": weight_down}
    w = {k: [[v], None, None, None] for k, v in own.items()}
    env = {}

    def gather_task(kind, g):
        names = GROUPS[g]
        if kind == "c0":
            for k in names:
                w[k][2] = [run.send(core, own[k])]
        elif kind == "x":
            for k in names:
                w[k][1] = [run.send(far, own[k])]
        elif kind == "sl":
            env["p", g], env["r", g] = run.compute(lambda *v: cut(at, v, [AXES[k] for k in names]), *[own[k] for k in names])
        elif kind == "xp":
            env["px", g] = run.send(far, env["p", g])
        elif kind == "xr":
            env["rx", g] = run.send(far, env["r", g])
        elif kind == "y":
            env["py", g] = run.send(rep, env["px", g])
        elif kind == "z":
            env["rz", g] = run.send(near, env["rx", g])
        elif kind == "as":
            outs = run.compute(
                lambda *v: join(at, v, [own[k] for k in names], [AXES[k] for k in names]),
                env["px", g], env["py", g], env["rx", g], env["rz", g],
            )
            for k in names:
                n = 3 if AXES[k] == 3 else 1
                w[k][1], outs = outs[:n], outs[n:]
        elif kind == "cx":
            for k in names:
                w[k][3] = [run.send(core, v) for v in w[k][1]]

    def one(k):
        return [v[0] for v in w[k]]

    def over_dp(v):
        for bit in bits_of(n_dp):
            v = run.compute(add, v, run.send(swap("dp", n_dp, bit), v))
        return v

    def chunk_task(name, stage):
        source = CHUNKS[name]
        c = env.setdefault(("chunk", name), {})

        def z(pairs):
            return lambda v: lax.ppermute(v, "dp", pairs)

        if stage == "f":
            done(name, c["v"], c["w"])
        elif stage == "w":
            c["w"] = run.send(rep, c["v"])
        elif stage == "z1" and line:
            c["z"] = run.send(z([(0, 1), (3, 2)]), c["v"])
        elif stage == "z2" and line:
            c["z"] = run.send(z([(1, 2), (2, 1)]), c["v"])
        elif stage == "z3" and line:
            c["z"] = run.send(z([(1, 0), (2, 3)]), c["v"])
        elif stage == "a3" and line:
            c["v"] = run.compute(add, c["v"], c["z"])
        elif stage == "a4":
            c["v"] = run.compute(add, c["v"], c["z"]) if line else over_dp(c["v"])
        elif stage == "a5" and line:
            c["v"] = run.compute(lambda *v: pick(at, *v), c["v"], c["z"])
        elif source in ("Q", "O"):

            def part(j):
                return env["O"][j] if source == "O" else env["gQ", j]["abc".index(name[1])]

            if stage == "x":
                c["x"] = run.send(far, part(1))
            elif stage == "a1":
                step = (lambda *v: split_packed(at, *v)) if source == "O" else (lambda a, b: split_add(at, [a], [b]))
                c["give"], c["v"] = run.compute(step, part(0), c["x"])
            elif stage == "y":
                c["y"] = run.send(rep, c["give"])
            elif stage == "a2":
                c["v"] = run.compute(add, c["v"], c["y"])
        elif source == "F":
            if stage in ("yo", "yx"):
                c[stage] = run.send(rep, env["F", "ox".index(stage[1])][0])
            elif stage in ("ao", "ax"):
                c[stage] = run.compute(add, env["F", "ox".index(stage[1])][1], c["y" + stage[1]])
            elif stage == "x":
                c["x"] = run.send(far, c["ax"])
            elif stage == "a2":
                c["v"] = run.compute(add, c["ao"], c["x"])

    def done(name, mine, other):
        if name == "F":
            env["down"], env["up"] = run.compute(lambda *v: finish(at, *v, (False, True)), mine, other)
        elif name == "O":
            env["out"], env["gain1"], env["gain2"] = run.compute(lambda *v: finish_packed(at, *v), mine, other)
        else:
            env["qkv"] = run.compute(lambda *v: finish_slot(at, *v, "abc".index(name[1]), 3, env.get("qkv")), mine, other)

    def task(t):
        if t == "prep":
            env["a1"], env["dm"] = run.compute(lambda c, v, g: prep(v, c, g), cot, x, gain1)
        elif t[:3] == "att":
            j = int(t[3])
            env["att", j] = run.compute(attend, env["a1"], w["qkv"][j])
        elif t == "proj":
            env["resid"], env["a2"] = run.compute(lambda *m: project(m, one("out"), x, gain2), *[env["att", j][1] for j in range(4)])
        elif t in ("mlpP", "mlpR"):
            js = (0, 2) if t == "mlpP" else (1, 3)
            hid, dpre, grads = run.compute(lambda a: mlp(a, env["dm"], [w["up"][j][0] for j in js], [w["down"][j][0] for j in js]), env["a2"])
            for i, j in enumerate(js):
                env["hid", j], env["dpre", j], env["gF", j] = hid[i], dpre[i], grads[i]
        elif t in ("cF0", "cF1"):
            j = int(t[2])
            env["rF", j] = [run.send(core, v) for v in env["gF", 2 + j]]
        elif t in ("aF0", "aF1"):
            j = int(t[2])
            env["F", j] = run.compute(lambda v, *r: split_add(at, [v, r[0]], r[1:]), *env["gF", j], *env["rF", j])
        elif t == "mlpback":
            env["dres"], env["datt"], env["part2"] = run.compute(
                lambda *d: mlp_back(d, one("up"), env["resid"], cot, gain2), *[env["dpre", j] for j in range(4)]
            )
        elif t == "mlpout":
            env["output"] = run.compute(lambda *h: mlp_out(h, one("down"), env["resid"]), *[env["hid", j] for j in range(4)])
        elif t == "gout":
            env["gO"] = run.compute(lambda d: grad_out(d, [env["att", j][1] for j in range(4)]), env["datt"])
        elif t == "cO":
            env["rO"] = [run.send(core, v) for v in env["gO"][2:]]
        elif t == "aO":
            env["O"] = run.compute(lambda *v: pack(*v, env["rO"], env["g"], env["gr"]), *env["gO"][:2])
        elif t[:2] == "ab":
            j = int(t[2])
            got = env["rQ", j] if j < 2 else ()
            env["dqkv", j], env["gQ", j] = run.compute(
                lambda d: attend_back(env["a1"], d, w["out"][j][0], env["att", j][0], env["att", j][2], got), env["datt"]
            )
        elif t in ("cQ0", "cQ1"):
            j = int(t[2])
            env["rQ", j] = [run.send(core, v) for v in env["gQ", 2 + j]]
        elif t == "inback":
            env["gin"], env["g"] = run.compute(
                lambda *d: input_back(d, w["qkv"], x, env["dres"], gain1, env["part2"]), *[env["dqkv", j] for j in range(4)]
            )
        elif t == "g0":
            env["gr"] = run.send(core, env["g"])
        elif t.split("_")[1] in GROUPS:
            gather_task(*t.split("_"))
        else:
            chunk_task(*t.split("_"))

    for t in ORDER:
        task(t)
    return (
        env["output"].reshape(shape),
        env["gin"].reshape(shape),
        env["gain1"].reshape(-1),
        env["qkv"],
        env["out"],
        env["gain2"].reshape(-1),
        env["up"],
        env["down"],
    )


def solution(mesh):
    return jax.shard_map(
        functools.partial(per_device, dict(mesh.shape)),
        mesh=mesh,
        in_specs=(
            P(("rep", "mp"), "dp", None, None),
            P(),
            P(None, None, "mp"),
            P("mp", None),
            P(),
            P(None, "mp"),
            P("mp", None),
            P(("rep", "mp"), "dp", None, None),
        ),
        out_specs=(
            P(("rep", "mp"), "dp", None, None),
            P(("rep", "mp"), "dp", None, None),
            P(),
            P(None, None, "mp"),
            P("mp", None),
            P(),
            P(None, "mp"),
            P("mp", None),
        ),
        check_vma=False,
    )
```

```python
import functools

import jax
import jax.numpy as jnp
from jax import lax
from jax.experimental import pallas as pl
from jax.experimental.pallas import tpu as pltpu
from jax.sharding import PartitionSpec as P

HEAD_DIM = 128
PROJ_BLOCK = 256
GRAD_BLOCK = 512
EPS = 1e-05
LOG2E = 1.4426950408889634
GELU_A = 0.7978845608028654
GELU_B = 0.044715
f32 = jnp.float32
bf16 = jnp.bfloat16

NN = (((1,), (0,)), ((), ()))
NT = (((1,), (1,)), ((), ()))
TN = (((0,), (0,)), ((), ()))


def dot(a, b, dims=NN):
    return lax.dot_general(a, b, dims, preferred_element_type=f32)


def normed(v):
    mean = jnp.mean(v, axis=-1, keepdims=True)
    centred = v - mean
    r = lax.rsqrt(jnp.mean(centred * centred, axis=-1, keepdims=True) + EPS)
    return centred * r, r


def fold(v):
    return jnp.sum(v.reshape(-1, 8, v.shape[-1]), axis=0)


def params(mib=8):
    return pltpu.CompilerParams(vmem_limit_bytes=mib * 2**20)


def cost():
    return pl.CostEstimate(flops=1, bytes_accessed=1, transcendentals=0)


def whole(n):
    return [pl.BlockSpec(memory_space=pltpu.VMEM)] * n


def sds(shape, dtype):
    return jax.ShapeDtypeStruct(shape, dtype)


def by_rows(length, step, init=None, block=512):
    if block >= length:
        return step(slice(None), init)
    return lax.fori_loop(0, length // block, lambda i, c: step(span(i, block), c), init)


def span(i, size):
    return pl.ds(pl.multiple_of(i * size, size), size)


def loop(n, step):
    lax.fori_loop(0, n, lambda i, _: step(i), None)


def call(kernel, ins, outs, name, mib=8, at=None, scratch=()):
    flags = [] if at is None else [at]
    return pl.pallas_call(
        kernel,
        in_specs=[pl.BlockSpec(memory_space=pltpu.SMEM)] * len(flags) + whole(len(ins)),
        out_specs=whole(len(outs)),
        out_shape=list(outs),
        scratch_shapes=list(scratch),
        compiler_params=params(mib),
        cost_estimate=cost(),
        name=name,
    )(*flags, *ins)


def matrices(refs):
    return (lambda c: refs[0][c]) if len(refs) == 1 else (lambda c: refs[c][...])


def prep_kernel(x_ref, c_ref, g_ref, a_ref, d_ref):
    def step(rows, _):
        a_ref[rows, :] = (normed(x_ref[rows, :])[0] * g_ref[...]).astype(bf16)
        d_ref[rows, :] = c_ref[rows, :].astype(bf16)

    by_rows(x_ref.shape[0], step)


def prep(x, cot, gain):
    return call(prep_kernel, (x, cot, gain), (sds(x.shape, bf16),) * 2, "prep")


def attend_kernel(n, a_ref, *refs):
    w, (qkv_ref, mixed_ref, lse_ref) = matrices(refs[:n]), refs[n:]
    scale = HEAD_DIM**-0.5 * LOG2E

    def project_rows(rows, _):
        for c in range(3):
            qkv_ref[c, rows, :] = dot(a_ref[rows, :], w(c)).astype(bf16)

    def head(h):
        cols = span(h, HEAD_DIM)
        q, k, v = (qkv_ref[c, :, cols] for c in range(3))
        scores = dot(k, q, NT)
        top = jnp.max(scores, axis=0, keepdims=True)
        expd = jnp.exp2((scores - top) * scale)
        total = jnp.sum(expd, axis=0, keepdims=True)
        mixed = dot(v, expd.astype(bf16), TN) / total
        mixed_ref[:, cols] = mixed.T.astype(bf16)
        lse_ref[pl.ds(h, 1), :] = top * scale + jnp.log2(total)

    by_rows(a_ref.shape[0], project_rows, None, PROJ_BLOCK)
    loop(qkv_ref.shape[2] // HEAD_DIM, head)


def attend(a, w):
    length, local = a.shape[0], w[0].shape[-1]
    outs = (sds((3, length, local), bf16), sds((length, local), bf16), sds((local // HEAD_DIM, length), f32))
    return call(functools.partial(attend_kernel, len(w)), (a, *w), outs, "attend", 12)


def project_kernel(n, *refs):
    mixed, w = refs[:n], refs[n : 2 * n]
    x_ref, g_ref, resid_ref, a_ref = refs[2 * n :]

    def step(rows, _):
        total = dot(mixed[0][rows, :], w[0][...])
        for j in range(1, n):
            total += dot(mixed[j][rows, :], w[j][...])
        resid = x_ref[rows, :] + total
        resid_ref[rows, :] = resid
        a_ref[rows, :] = (normed(resid)[0] * g_ref[...]).astype(bf16)

    by_rows(x_ref.shape[0], step)


def project(mixed, w, x, gain):
    outs = (sds(x.shape, f32), sds(x.shape, bf16))
    return call(functools.partial(project_kernel, len(mixed)), (*mixed, *w, x, gain), outs, "project")


def mlp_kernel(n, *refs):
    a_ref, d_ref = refs[:2]
    up, down = refs[2 : 2 + n], refs[2 + n : 2 + 2 * n]
    outs = refs[2 + 2 * n :]
    hid, dpre, grads = outs[:n], outs[n : 2 * n], outs[2 * n :]
    for j in range(n):
        u = dot(a_ref[...], up[j][...])
        d_hidden = dot(d_ref[...], down[j][...], NT)
        sq = u * u
        t = jnp.tanh(GELU_A * u * (1.0 + GELU_B * sq))
        half = 0.5 * (1.0 + t)
        hidden = (u * half).astype(bf16)
        slope = half + 0.5 * u * (1.0 - t * t) * (GELU_A * (1.0 + 3.0 * GELU_B * sq))
        d_pre = (d_hidden * slope).astype(bf16)
        hid[j][...] = hidden
        dpre[j][...] = d_pre
        grads[2 * j][...] = dot(hidden, d_ref[...], TN).astype(bf16)
        grads[2 * j + 1][...] = dot(d_pre, a_ref[...], TN).astype(bf16)


def mlp(a, d, up, down):
    n = len(up)
    length, width = a.shape
    local = up[0].shape[1]
    act, grad = sds((length, local), bf16), sds((local, width), bf16)
    outs = call(functools.partial(mlp_kernel, n), (a, d, *up, *down), (act,) * (2 * n) + (grad,) * (2 * n), "mlp", 12)
    return outs[:n], outs[n : 2 * n], [outs[2 * n + 2 * j : 2 * n + 2 * j + 2] for j in range(n)]


def norm_back(d_a, v, gain):
    xhat, r = normed(v)
    e = d_a * gain
    back = r * (e - jnp.mean(e, axis=-1, keepdims=True) - xhat * jnp.mean(e * xhat, axis=-1, keepdims=True))
    return back, fold(d_a * xhat)


def mlp_back_kernel(n, *refs):
    d_pre, up = refs[:n], refs[n : 2 * n]
    resid_ref, c_ref, g_ref, dres_ref, datt_ref, gain_ref = refs[2 * n :]

    def step(rows, gain):
        total = dot(d_pre[0][rows, :], up[0][...], NT)
        for j in range(1, n):
            total += dot(d_pre[j][rows, :], up[j][...], NT)
        back, part = norm_back(total, resid_ref[rows, :], g_ref[...])
        d_resid = c_ref[rows, :] + back
        dres_ref[rows, :] = d_resid
        datt_ref[rows, :] = d_resid.astype(bf16)
        return gain + part

    gain_ref[...] = by_rows(c_ref.shape[0], step, jnp.zeros(gain_ref.shape, f32), 256)


def mlp_back(d_pre, up, resid, cot, gain):
    n = len(up)
    outs = (sds(resid.shape, f32), sds(resid.shape, bf16), sds((8, resid.shape[1]), f32))
    return call(functools.partial(mlp_back_kernel, n), (*d_pre, *up, resid, cot, gain), outs, "mlp_back")


def mlp_out_kernel(n, *refs):
    hid, down = refs[:n], refs[n : 2 * n]
    resid_ref, out_ref = refs[2 * n :]

    def step(rows, _):
        total = resid_ref[rows, :]
        for j in range(n):
            total += dot(hid[j][rows, :], down[j][...])
        out_ref[rows, :] = total

    by_rows(resid_ref.shape[0], step)


def mlp_out(hid, down, resid):
    n = len(down)
    return call(functools.partial(mlp_out_kernel, n), (*hid, *down, resid), (sds(resid.shape, f32),), "mlp_out")[0]


def grad_out_kernel(n, d_ref, *refs):
    for mixed, out in zip(refs[:n], refs[n:], strict=True):
        out[...] = dot(mixed[...], d_ref[...], TN).astype(bf16)


def grad_out(d, mixed):
    n = len(mixed)
    outs = (sds((mixed[0].shape[1], d.shape[1]), bf16),) * n
    return call(functools.partial(grad_out_kernel, n), (d, *mixed), outs, "grad_out")


def attend_back_kernel(added, a_ref, d_ref, w_ref, qkv_ref, lse_ref, *refs):
    scale = HEAD_DIM**-0.5
    got, dqkv_ref, grads, dm_ref = refs[:added], refs[added], refs[added + 1 : -1], refs[-1]
    dm_ref[...] = dot(d_ref[...], w_ref[...], NT).astype(bf16)

    def head(h):
        cols = span(h, HEAD_DIM)
        q, k, v = (qkv_ref[c, :, cols] for c in range(3))
        dm = dm_ref[:, cols]
        probs = jnp.exp2(dot(k, q, NT) * (scale * LOG2E) - lse_ref[pl.ds(h, 1), :])
        d_probs = dot(v, dm, NT)
        dqkv_ref[2, :, cols] = dot(probs.astype(bf16), dm).astype(bf16)
        delta = jnp.sum(d_probs * probs, axis=0, keepdims=True)
        d_scores = (probs * (d_probs - delta)).astype(bf16)
        dqkv_ref[1, :, cols] = (dot(d_scores, q) * scale).astype(bf16)
        dqkv_ref[0, :, cols] = (dot(k, d_scores, TN) * scale).T.astype(bf16)

    loop(w_ref.shape[0] // HEAD_DIM, head)
    size = GRAD_BLOCK

    def grad_cols(i):
        cols = span(i, size)
        for c in range(3):
            grad = dot(dqkv_ref[c], a_ref[:, cols], TN)
            grads[c][:, cols] = (grad + got[c][:, cols].astype(f32) if added else grad).astype(bf16)

    loop(a_ref.shape[1] // size, grad_cols)


def attend_back(a, d, w, qkv, lse, got=()):
    length, width = a.shape
    local = w.shape[0]
    outs = (sds((3, length, local), bf16), *[sds((local, width), bf16)] * 3)
    outs = call(functools.partial(attend_back_kernel, len(got)), (a, d, w, qkv, lse, *got), outs, "attend_back", 12, None, [pltpu.VMEM((length, local), bf16)])
    return outs[0], outs[1:]


def join_kernel(axes, at_ref, *refs):
    quarters, outs = refs[:4], refs[4:]
    width = quarters[0].shape[1]
    for p, quarter in enumerate(quarters):
        place = pl.ds(pl.multiple_of(at_ref[p] * width, width), width)
        for i, (out, axis) in enumerate(zip(outs, axes, strict=True)):
            if axis == 0:
                out[place, :] = quarter[i]
            else:
                out[:, place] = quarter[i]


def join(at, quarters, likes, axes):
    flat = [(v.shape[-2:], 0 if axis == 3 else axis) for v, axis in zip(likes, axes, strict=True) for _ in range(v.size // (v.shape[-1] * v.shape[-2]))]
    outs = [sds(shape, bf16) for shape, _ in flat]
    return call(functools.partial(join_kernel, tuple(axis for _, axis in flat)), quarters, outs, "join", 4, at)


def cut_kernel(axes, at_ref, *refs):
    n = len(axes)
    for out, p in zip(refs[n:], (0, 2), strict=True):
        size = out.shape[1]
        place = pl.ds(pl.multiple_of(at_ref[p] * size, size), size)
        i = 0
        for v, axis in zip(refs[:n], axes, strict=True):
            if axis == 3:
                for c in range(3):
                    out[i + c] = v[c, place, :]
                i += 3
            else:
                out[i] = v[place, :] if axis == 0 else v[:, place]
                i += 1


def cut(at, arrays, axes):
    size = max(arrays[0].shape) // 4
    outs = (sds((sum(v.size for v in arrays) // (4 * size * size), size, size), bf16),) * 2
    return call(functools.partial(cut_kernel, tuple(axes)), arrays, outs, "cut", 4, at)


def half_of(ref, at, rows):
    place = pl.ds(pl.multiple_of(at * rows, rows), rows)
    return ref[place, :] if len(ref.shape) == 2 else ref[:, place, :]


def add_kernel(a_ref, b_ref, o_ref):
    o_ref[...] = a_ref[...] + b_ref[...]


def add(a, b):
    return call(add_kernel, (a, b), (sds(a.shape, a.dtype),), "add", 4)[0]


def halved(shape, n=None):
    half = (shape[-2] // 2, shape[-1])
    return sds(half if n is None else (n, *half), bf16)


def split_add_kernel(n, at_ref, *refs):
    a, b, (give_ref, keep_ref) = refs[:n], refs[n : 2 * n], refs[2 * n :]
    rows = give_ref.shape[-2]
    for at, out in ((1 - at_ref[0], give_ref), (at_ref[0], keep_ref)):
        for i in range(n):
            total = half_of(a[i], at, rows) + half_of(b[i], at, rows)
            if len(out.shape) == 2:
                out[...] = total
            else:
                out[i] = total


def split_add(at, a, b):
    n = len(a)
    outs = (halved(a[0].shape, None if n == 1 else n),) * 2
    return call(functools.partial(split_add_kernel, n), (*a, *b), outs, "split_add", 4, at)


EXTRA = 16


def pack_kernel(*refs):
    gains, got_gains, outs = refs[4], refs[5], refs[6:]
    total = (gains[...] + got_gains[...]).astype(bf16)
    for a, b, out in zip(refs[:2], refs[2:4], outs, strict=True):
        rows = a.shape[0]
        out[0:rows, :] = a[...] + b[...]
        out[rows : rows + EXTRA, :] = jnp.concatenate([total, jnp.zeros((EXTRA - total.shape[0], total.shape[1]), bf16)])


def pack(kept, sent, got, gains, got_gains):
    rows, width = kept.shape
    return call(pack_kernel, (kept, sent, *got, gains, got_gains), (sds((rows + EXTRA, width), bf16),) * 2, "pack", 4)


def split_packed_kernel(at_ref, a_ref, b_ref, give_ref, keep_ref):
    rows = give_ref.shape[0] - EXTRA
    extra = slice(2 * rows, 2 * rows + EXTRA)
    gains = a_ref[extra, :] + b_ref[extra, :]
    for at, out in ((1 - at_ref[0], give_ref), (at_ref[0], keep_ref)):
        out[0:rows, :] = half_of(a_ref, at, rows) + half_of(b_ref, at, rows)
        out[rows : rows + EXTRA, :] = gains


def split_packed(at, a, b):
    shape = ((a.shape[0] - EXTRA) // 2 + EXTRA, a.shape[1])
    return call(split_packed_kernel, (a, b), (sds(shape, bf16),) * 2, "split_add", 4, at)


def finish_packed_kernel(at_ref, mine_ref, other_ref, out_ref, gain1_ref, gain2_ref):
    rows = out_ref.shape[0] // 2
    for at, ref in ((at_ref[0], mine_ref), (1 - at_ref[0], other_ref)):
        out_ref[pl.ds(pl.multiple_of(at * rows, rows), rows), :] = ref[0:rows, :].astype(f32)
    gains = mine_ref[rows : rows + EXTRA, :].astype(f32)
    gain1_ref[...] = gains[0:1, :]
    gain2_ref[...] = gains[1:2, :]


def finish_packed(at, mine, other):
    rows, width = 2 * (mine.shape[0] - EXTRA), mine.shape[1]
    outs = (sds((rows, width), f32), sds((1, width), f32), sds((1, width), f32))
    return call(finish_packed_kernel, (mine, other), outs, "finish", 6, at)


def pick_kernel(at_ref, a_ref, b_ref, o_ref):
    @pl.when(at_ref[4] == 1)
    def _():
        o_ref[...] = b_ref[...]

    @pl.when(at_ref[4] == 0)
    def _():
        o_ref[...] = a_ref[...]


def pick(at, a, b):
    return call(pick_kernel, (a, b), (sds(a.shape, a.dtype),), "pick", 4, at)[0]


def placed(ref, at, index=None):
    rows = ref.shape[-2]
    return pl.ds(pl.multiple_of(at * rows, rows), rows), (ref[...] if index is None else ref[index]).astype(f32)


def finish_kernel(turned, at_ref, mine_ref, other_ref, *outs):
    for at, ref in ((at_ref[0], mine_ref), (1 - at_ref[0], other_ref)):
        for i, (out, turn) in enumerate(zip(outs, turned, strict=True)):
            place, v = placed(ref, at, i if len(turned) > 1 else None)
            if turn:
                out[:, place] = v.T
            else:
                out[place, :] = v


def finish(at, mine, other, turned):
    rows, width = 2 * mine.shape[-2], mine.shape[-1]
    outs = [sds((width, rows) if turn else (rows, width), f32) for turn in turned]
    return call(functools.partial(finish_kernel, turned), (mine, other), outs, "finish", 6, at)


def finish_slot_kernel(at_ref, mine_ref, other_ref, *refs):
    for at, ref in ((at_ref[0], mine_ref), (1 - at_ref[0], other_ref)):
        place, v = placed(ref, at)
        refs[-1][0, :, place] = v.T


def finish_slot(at, mine, other, slot, slots, into):
    rows, width = mine.shape
    spec = pl.BlockSpec(memory_space=pltpu.VMEM)
    return pl.pallas_call(
        finish_slot_kernel,
        grid=(1,),
        in_specs=[pl.BlockSpec(memory_space=pltpu.SMEM), spec, spec] + [pl.BlockSpec(memory_space=pl.ANY)] * (into is not None),
        out_specs=pl.BlockSpec((1, width, 2 * rows), lambda i: (slot, 0, 0)),
        out_shape=sds((slots, width, 2 * rows), f32),
        input_output_aliases={} if into is None else {3: 0},
        compiler_params=params(6),
        cost_estimate=cost(),
        name="finish",
    )(at, mine, other, *([] if into is None else [into]))


def input_back_kernel(n, counts, *refs):
    d_qkv, refs = refs[:n], refs[n:]
    w = []
    for count in counts:
        w.append(matrices(refs[:count]))
        refs = refs[count:]
    x_ref, dres_ref, g_ref, other_ref, out_ref, gains_ref = refs

    def step(rows, gain):
        total = None
        for j in range(n):
            for c in range(3):
                part = dot(d_qkv[j][c, rows, :], w[j](c), NT)
                total = part if total is None else total + part
        back, part = norm_back(total, x_ref[rows, :], g_ref[...])
        out_ref[rows, :] = dres_ref[rows, :] + back
        return gain + part

    gain = by_rows(x_ref.shape[0], step, jnp.zeros(other_ref.shape, f32), 256)
    gains_ref[0:1, :] = jnp.sum(gain, axis=0, keepdims=True)
    gains_ref[1:2, :] = jnp.sum(other_ref[...], axis=0, keepdims=True)


def input_back(d_qkv, w, x, d_resid, gain, other):
    outs = (sds(x.shape, f32), sds((2, x.shape[1]), f32))
    kernel = functools.partial(input_back_kernel, len(w), tuple(len(v) for v in w))
    return call(kernel, (*d_qkv, *[m for v in w for m in v], x, d_resid, gain, other), outs, "input_back", 12)


def swap(axis, size, bit):
    pairs = [(i, i ^ bit) for i in range(size)]
    return lambda v: lax.ppermute(v, axis, pairs)


def bits_of(size):
    return [1 << b for b in reversed(range(size.bit_length() - 1))]


class Run:
    def __init__(self):
        self.token = None

    def tie(self, v):
        if self.token is None:
            return v
        return lax.optimization_barrier((v, self.token))[0]

    def compute(self, step, first, *rest):
        outs = step(self.tie(first), *rest)
        self.token = jax.tree.leaves(outs)[0]
        return outs

    def send(self, move, v):
        v = self.tie(v)
        self.token = v
        return move(v)


class Names:
    def __getattr__(self, name):
        return name


N = Names()
ORDER = (
    N.x_d, N.c0_ou, N.sl_q, N.xp_q, N.c0_q, N.prep, N.sl_ou, N.xr_q, N.y_q, N.xr_ou, N.xp_ou, N.att0, N.z_q,
    N.z_ou, N.att2, N.as_q, N.y_ou, N.cx_q, N.att1, N.as_ou, N.cx_ou, N.cx_d, N.att3, N.c0_d, N.proj, N.mlpR,
    N.cF1, N.mlpP, N.cF0, N.aF1, N.F_yx, N.mlpback, N.gout, N.aF0, N.ab3, N.cQ1, N.F_yo, N.F_ax, N.F_x, N.ab1,
    N.Qb_x, N.cO, N.ab2, N.Qc_x, N.cQ0, N.Qa_x, N.F_ao, N.F_a2, N.F_z1, N.ab0, N.inback, N.g0, N.Qa_a1, N.aO,
    N.O_x, N.F_a3, N.F_z2, N.Qa_y, N.Qa_a2, N.Qa_z1, N.Qb_a1, N.Qb_y, N.F_a4, N.Qa_a3, N.F_z3, N.Qb_a2, N.Qa_z2,
    N.Qb_z1, N.O_a1, N.O_y, N.Qb_a3, N.Qb_z2, N.F_a5, N.O_a2, N.Qa_a4, N.O_z1, N.Qa_z3, N.Qc_a1, N.Qc_y, N.Qb_a4,
    N.F_w, N.Qc_a2, N.Qc_z1, N.O_a3, N.Qa_a5, N.Qb_z3, N.O_z2, N.Qc_a3, N.Qa_w, N.Qc_z2, N.O_a4, N.F_f, N.Qb_a5,
    N.Qb_w, N.O_z3, N.Qc_a4, N.Qa_f, N.Qc_z3, N.O_a5, N.O_w, N.Qb_f, N.mlpout, N.Qc_a5, N.Qc_w, N.O_f, N.Qc_f,
)
GROUPS = {"q": ("qkv",), "ou": ("out", "up"), "d": ("down",)}
CHUNKS = {"F": "F", "O": "O", "Qa": "Q", "Qb": "Q", "Qc": "Q"}
AXES = {"qkv": 3, "out": 1, "up": 0, "down": 1}


def per_device(
    sizes,
    inputs,
    norm1_gain,
    weight_qkv,
    weight_out,
    norm2_gain,
    weight_up,
    weight_down,
    cotangent,
):
    n_rep, n_dp, n_mp = sizes["rep"], sizes["dp"], sizes["mp"]
    if n_mp != 4 or n_rep != 2 or n_dp & (n_dp - 1) or n_dp < 2:
        raise ValueError("unsupported mesh")
    shape = inputs.shape
    x = inputs.reshape(shape[-2:])
    cot = cotangent.reshape(shape[-2:])
    gain1, gain2 = norm1_gain.reshape(1, -1), norm2_gain.reshape(1, -1)
    width = x.shape[1]
    run = Run()
    dp_at = lax.axis_index("dp")
    rep_at = lax.axis_index("rep")
    near_at = dp_at % 2
    line = n_dp == 4
    outer = (dp_at == 0) | (dp_at == n_dp - 1)
    at = jnp.stack([rep_at, 1 - rep_at, 2 + near_at, 3 - near_at, outer.astype(jnp.int32)]).astype(jnp.int32)

    core = swap("mp", n_mp, 1)
    far = swap("mp", n_mp, 2)
    rep = swap("rep", n_rep, 1)
    near = swap("dp", n_dp, 1)
    own = {"qkv": weight_qkv, "out": weight_out, "up": weight_up, "down": weight_down}
    w = {k: [[v], None, None, None] for k, v in own.items()}
    env = {}

    def gather_task(kind, g):
        names = GROUPS[g]
        if kind == "c0":
            for k in names:
                w[k][2] = [run.send(core, own[k])]
        elif kind == "x":
            for k in names:
                w[k][1] = [run.send(far, own[k])]
        elif kind == "sl":
            env["p", g], env["r", g] = run.compute(lambda *v: cut(at, v, [AXES[k] for k in names]), *[own[k] for k in names])
        elif kind == "xp":
            env["px", g] = run.send(far, env["p", g])
        elif kind == "xr":
            env["rx", g] = run.send(far, env["r", g])
        elif kind == "y":
            env["py", g] = run.send(rep, env["px", g])
        elif kind == "z":
            env["rz", g] = run.send(near, env["rx", g])
        elif kind == "as":
            outs = run.compute(
                lambda *v: join(at, v, [own[k] for k in names], [AXES[k] for k in names]),
                env["px", g], env["py", g], env["rx", g], env["rz", g],
            )
            for k in names:
                n = 3 if AXES[k] == 3 else 1
                w[k][1], outs = outs[:n], outs[n:]
        elif kind == "cx":
            for k in names:
                w[k][3] = [run.send(core, v) for v in w[k][1]]

    def one(k):
        return [v[0] for v in w[k]]

    def over_dp(v):
        for bit in bits_of(n_dp):
            v = run.compute(add, v, run.send(swap("dp", n_dp, bit), v))
        return v

    def chunk_task(name, stage):
        source = CHUNKS[name]
        c = env.setdefault(("chunk", name), {})

        def z(pairs):
            return lambda v: lax.ppermute(v, "dp", pairs)

        if stage == "f":
            done(name, c["v"], c["w"])
        elif stage == "w":
            c["w"] = run.send(rep, c["v"])
        elif stage == "z1" and line:
            c["z"] = run.send(z([(0, 1), (3, 2)]), c["v"])
        elif stage == "z2" and line:
            c["z"] = run.send(z([(1, 2), (2, 1)]), c["v"])
        elif stage == "z3" and line:
            c["z"] = run.send(z([(1, 0), (2, 3)]), c["v"])
        elif stage == "a3" and line:
            c["v"] = run.compute(add, c["v"], c["z"])
        elif stage == "a4":
            c["v"] = run.compute(add, c["v"], c["z"]) if line else over_dp(c["v"])
        elif stage == "a5" and line:
            c["v"] = run.compute(lambda *v: pick(at, *v), c["v"], c["z"])
        elif source in ("Q", "O"):

            def part(j):
                return env["O"][j] if source == "O" else env["gQ", j]["abc".index(name[1])]

            if stage == "x":
                c["x"] = run.send(far, part(1))
            elif stage == "a1":
                step = (lambda *v: split_packed(at, *v)) if source == "O" else (lambda a, b: split_add(at, [a], [b]))
                c["give"], c["v"] = run.compute(step, part(0), c["x"])
            elif stage == "y":
                c["y"] = run.send(rep, c["give"])
            elif stage == "a2":
                c["v"] = run.compute(add, c["v"], c["y"])
        elif source == "F":
            if stage in ("yo", "yx"):
                c[stage] = run.send(rep, env["F", "ox".index(stage[1])][0])
            elif stage in ("ao", "ax"):
                c[stage] = run.compute(add, env["F", "ox".index(stage[1])][1], c["y" + stage[1]])
            elif stage == "x":
                c["x"] = run.send(far, c["ax"])
            elif stage == "a2":
                c["v"] = run.compute(add, c["ao"], c["x"])

    def done(name, mine, other):
        if name == "F":
            env["down"], env["up"] = run.compute(lambda *v: finish(at, *v, (False, True)), mine, other)
        elif name == "O":
            env["out"], env["gain1"], env["gain2"] = run.compute(lambda *v: finish_packed(at, *v), mine, other)
        else:
            env["qkv"] = run.compute(lambda *v: finish_slot(at, *v, "abc".index(name[1]), 3, env.get("qkv")), mine, other)

    def task(t):
        if t == "prep":
            env["a1"], env["dm"] = run.compute(lambda c, v, g: prep(v, c, g), cot, x, gain1)
        elif t[:3] == "att":
            j = int(t[3])
            env["att", j] = run.compute(attend, env["a1"], w["qkv"][j])
        elif t == "proj":
            env["resid"], env["a2"] = run.compute(lambda *m: project(m, one("out"), x, gain2), *[env["att", j][1] for j in range(4)])
        elif t in ("mlpP", "mlpR"):
            js = (0, 2) if t == "mlpP" else (1, 3)
            hid, dpre, grads = run.compute(lambda a: mlp(a, env["dm"], [w["up"][j][0] for j in js], [w["down"][j][0] for j in js]), env["a2"])
            for i, j in enumerate(js):
                env["hid", j], env["dpre", j], env["gF", j] = hid[i], dpre[i], grads[i]
        elif t in ("cF0", "cF1"):
            j = int(t[2])
            env["rF", j] = [run.send(core, v) for v in env["gF", 2 + j]]
        elif t in ("aF0", "aF1"):
            j = int(t[2])
            env["F", j] = run.compute(lambda v, *r: split_add(at, [v, r[0]], r[1:]), *env["gF", j], *env["rF", j])
        elif t == "mlpback":
            env["dres"], env["datt"], env["part2"] = run.compute(
                lambda *d: mlp_back(d, one("up"), env["resid"], cot, gain2), *[env["dpre", j] for j in range(4)]
            )
        elif t == "mlpout":
            env["output"] = run.compute(lambda *h: mlp_out(h, one("down"), env["resid"]), *[env["hid", j] for j in range(4)])
        elif t == "gout":
            env["gO"] = run.compute(lambda d: grad_out(d, [env["att", j][1] for j in range(4)]), env["datt"])
        elif t == "cO":
            env["rO"] = [run.send(core, v) for v in env["gO"][2:]]
        elif t == "aO":
            env["O"] = run.compute(lambda *v: pack(*v, env["rO"], env["g"], env["gr"]), *env["gO"][:2])
        elif t[:2] == "ab":
            j = int(t[2])
            got = env["rQ", j] if j < 2 else ()
            env["dqkv", j], env["gQ", j] = run.compute(
                lambda d: attend_back(env["a1"], d, w["out"][j][0], env["att", j][0], env["att", j][2], got), env["datt"]
            )
        elif t in ("cQ0", "cQ1"):
            j = int(t[2])
            env["rQ", j] = [run.send(core, v) for v in env["gQ", 2 + j]]
        elif t == "inback":
            env["gin"], env["g"] = run.compute(
                lambda *d: input_back(d, w["qkv"], x, env["dres"], gain1, env["part2"]), *[env["dqkv", j] for j in range(4)]
            )
        elif t == "g0":
            env["gr"] = run.send(core, env["g"])
        elif t.split("_")[1] in GROUPS:
            gather_task(*t.split("_"))
        else:
            chunk_task(*t.split("_"))

    for t in ORDER:
        task(t)
    return (
        env["output"].reshape(shape),
        env["gin"].reshape(shape),
        env["gain1"].reshape(-1),
        env["qkv"],
        env["out"],
        env["gain2"].reshape(-1),
        env["up"],
        env["down"],
    )


def solution(mesh):
    return jax.shard_map(
        functools.partial(per_device, dict(mesh.shape)),
        mesh=mesh,
        in_specs=(
            P(("rep", "mp"), "dp", None, None),
            P(),
            P(None, None, "mp"),
            P("mp", None),
            P(),
            P(None, "mp"),
            P("mp", None),
            P(("rep", "mp"), "dp", None, None),
        ),
        out_specs=(
            P(("rep", "mp"), "dp", None, None),
            P(("rep", "mp"), "dp", None, None),
            P(),
            P(None, None, "mp"),
            P("mp", None),
            P(),
            P(None, "mp"),
            P("mp", None),
        ),
        check_vma=False,
    )
```

```python
import functools

import jax
import jax.numpy as jnp
from jax import lax
from jax.experimental import pallas as pl
from jax.experimental.pallas import tpu as pltpu
from jax.sharding import PartitionSpec as P

HEAD_DIM = 128
PROJ_BLOCK = 256
GRAD_BLOCK = 512
EPS = 1e-05
LOG2E = 1.4426950408889634
GELU_A = 0.7978845608028654
GELU_B = 0.044715
f32 = jnp.float32
bf16 = jnp.bfloat16

NN = (((1,), (0,)), ((), ()))
NT = (((1,), (1,)), ((), ()))
TN = (((0,), (0,)), ((), ()))


def dot(a, b, dims=NN):
    return lax.dot_general(a, b, dims, preferred_element_type=f32)


def normed(v):
    mean = jnp.mean(v, axis=-1, keepdims=True)
    centred = v - mean
    r = lax.rsqrt(jnp.mean(centred * centred, axis=-1, keepdims=True) + EPS)
    return centred * r, r


def fold(v):
    return jnp.sum(v.reshape(-1, 8, v.shape[-1]), axis=0)


def params(mib=8):
    return pltpu.CompilerParams(vmem_limit_bytes=mib * 2**20)


def cost():
    return pl.CostEstimate(flops=1, bytes_accessed=1, transcendentals=0)


def whole(n):
    return [pl.BlockSpec(memory_space=pltpu.VMEM)] * n


def sds(shape, dtype):
    return jax.ShapeDtypeStruct(shape, dtype)


def by_rows(length, step, init=None, block=512):
    if block >= length:
        return step(slice(None), init)
    return lax.fori_loop(0, length // block, lambda i, c: step(span(i, block), c), init)


def span(i, size):
    if isinstance(i, int):
        return slice(i * size, (i + 1) * size)
    return pl.ds(pl.multiple_of(i * size, size), size)


def loop(n, step):
    lax.fori_loop(0, n, lambda i, _: step(i), None)


def unrolled(n, step):
    for i in range(n):
        step(i)


def places():
    rep, dp = lax.axis_index("rep"), lax.axis_index("dp")
    near = lax.rem(dp, 2)
    outer = jnp.where((dp == 0) | (dp == lax.axis_size("dp") - 1), 1, 0)
    quarters = [2 * r + n for r, n in ((rep, near), (1 - rep, near), (rep, 1 - near), (1 - rep, 1 - near))]
    return rep, 1 - rep, 2 + near, 3 - near, outer, *quarters


def placed_kernel(kernel, *refs):
    kernel(places(), *refs)


def call(kernel, ins, outs, name, mib=8, at=False, scratch=()):
    if at:
        kernel = functools.partial(placed_kernel, kernel)
    return pl.pallas_call(
        kernel,
        in_specs=whole(len(ins)),
        out_specs=whole(len(outs)),
        out_shape=list(outs),
        scratch_shapes=list(scratch),
        compiler_params=params(mib),
        cost_estimate=cost(),
        name=name,
    )(*ins)


def matrices(refs):
    return (lambda c: refs[0][c]) if len(refs) == 1 else (lambda c: refs[c][...])


def prep_kernel(x_ref, c_ref, g_ref, a_ref, d_ref):
    def step(rows, _):
        a_ref[rows, :] = (normed(x_ref[rows, :])[0] * g_ref[...]).astype(bf16)
        d_ref[rows, :] = c_ref[rows, :].astype(bf16)

    by_rows(x_ref.shape[0], step)


def prep(x, cot, gain):
    return call(prep_kernel, (x, cot, gain), (sds(x.shape, bf16),) * 2, "prep")


def attend_kernel(n, a_ref, *refs):
    w, (qkv_ref, mixed_ref, lse_ref) = matrices(refs[:n]), refs[n:]
    scale = HEAD_DIM**-0.5 * LOG2E

    def project_rows(rows, _):
        for c in range(3):
            qkv_ref[c, rows, :] = dot(a_ref[rows, :], w(c)).astype(bf16)

    def head(h):
        cols = span(h, HEAD_DIM)
        q, k, v = (qkv_ref[c, :, cols] for c in range(3))
        scores = dot(k, q, NT)
        top = jnp.max(scores, axis=0, keepdims=True)
        expd = jnp.exp2((scores - top) * scale)
        total = jnp.sum(expd, axis=0, keepdims=True)
        mixed = dot(v, expd.astype(bf16), TN) / total
        mixed_ref[:, cols] = mixed.T.astype(bf16)
        lse_ref[pl.ds(h, 1), :] = top * scale + jnp.log2(total)

    by_rows(a_ref.shape[0], project_rows, None, PROJ_BLOCK)
    loop(qkv_ref.shape[2] // HEAD_DIM, head)


def attend(a, w):
    length, local = a.shape[0], w[0].shape[-1]
    outs = (sds((3, length, local), bf16), sds((length, local), bf16), sds((local // HEAD_DIM, length), f32))
    return call(functools.partial(attend_kernel, len(w)), (a, *w), outs, "attend", 12)


def project_kernel(n, *refs):
    mixed, w = refs[:n], refs[n : 2 * n]
    x_ref, g_ref, resid_ref, a_ref = refs[2 * n :]

    def step(rows, _):
        total = dot(mixed[0][rows, :], w[0][...])
        for j in range(1, n):
            total += dot(mixed[j][rows, :], w[j][...])
        resid = x_ref[rows, :] + total
        resid_ref[rows, :] = resid
        a_ref[rows, :] = (normed(resid)[0] * g_ref[...]).astype(bf16)

    by_rows(x_ref.shape[0], step)


def project(mixed, w, x, gain):
    outs = (sds(x.shape, f32), sds(x.shape, bf16))
    return call(functools.partial(project_kernel, len(mixed)), (*mixed, *w, x, gain), outs, "project")


def mlp_kernel(n, *refs):
    a_ref, d_ref = refs[:2]
    up, down = refs[2 : 2 + n], refs[2 + n : 2 + 2 * n]
    outs = refs[2 + 2 * n :]
    hid, dpre, grads = outs[:n], outs[n : 2 * n], outs[2 * n :]
    for j in range(n):
        u = dot(a_ref[...], up[j][...])
        d_hidden = dot(d_ref[...], down[j][...], NT)
        sq = u * u
        t = jnp.tanh(GELU_A * u * (1.0 + GELU_B * sq))
        half = 0.5 * (1.0 + t)
        hidden = (u * half).astype(bf16)
        slope = half + 0.5 * u * (1.0 - t * t) * (GELU_A * (1.0 + 3.0 * GELU_B * sq))
        d_pre = (d_hidden * slope).astype(bf16)
        hid[j][...] = hidden
        dpre[j][...] = d_pre
        grads[2 * j][...] = dot(hidden, d_ref[...], TN).astype(bf16)
        grads[2 * j + 1][...] = dot(d_pre, a_ref[...], TN).astype(bf16)


def mlp(a, d, up, down):
    n = len(up)
    length, width = a.shape
    local = up[0].shape[1]
    act, grad = sds((length, local), bf16), sds((local, width), bf16)
    outs = call(functools.partial(mlp_kernel, n), (a, d, *up, *down), (act,) * (2 * n) + (grad,) * (2 * n), "mlp", 12)
    return outs[:n], outs[n : 2 * n], [outs[2 * n + 2 * j : 2 * n + 2 * j + 2] for j in range(n)]


def norm_back(d_a, v, gain):
    xhat, r = normed(v)
    e = d_a * gain
    back = r * (e - jnp.mean(e, axis=-1, keepdims=True) - xhat * jnp.mean(e * xhat, axis=-1, keepdims=True))
    return back, fold(d_a * xhat)


def mlp_back_kernel(n, *refs):
    d_pre, up = refs[:n], refs[n : 2 * n]
    resid_ref, c_ref, g_ref, dres_ref, datt_ref, gain_ref = refs[2 * n :]

    def step(rows, gain):
        total = dot(d_pre[0][rows, :], up[0][...], NT)
        for j in range(1, n):
            total += dot(d_pre[j][rows, :], up[j][...], NT)
        back, part = norm_back(total, resid_ref[rows, :], g_ref[...])
        d_resid = c_ref[rows, :] + back
        dres_ref[rows, :] = d_resid
        datt_ref[rows, :] = d_resid.astype(bf16)
        return gain + part

    gain_ref[...] = by_rows(c_ref.shape[0], step, jnp.zeros(gain_ref.shape, f32), 256)


def mlp_back(d_pre, up, resid, cot, gain):
    n = len(up)
    outs = (sds(resid.shape, f32), sds(resid.shape, bf16), sds((8, resid.shape[1]), f32))
    return call(functools.partial(mlp_back_kernel, n), (*d_pre, *up, resid, cot, gain), outs, "mlp_back")


def mlp_out_kernel(n, *refs):
    hid, down = refs[:n], refs[n : 2 * n]
    resid_ref, out_ref = refs[2 * n :]

    def step(rows, _):
        total = resid_ref[rows, :]
        for j in range(n):
            total += dot(hid[j][rows, :], down[j][...])
        out_ref[rows, :] = total

    by_rows(resid_ref.shape[0], step)


def mlp_out(hid, down, resid):
    n = len(down)
    return call(functools.partial(mlp_out_kernel, n), (*hid, *down, resid), (sds(resid.shape, f32),), "mlp_out")[0]


def grad_out_kernel(n, d_ref, *refs):
    for mixed, out in zip(refs[:n], refs[n:], strict=True):
        out[...] = dot(mixed[...], d_ref[...], TN).astype(bf16)


def grad_out(d, mixed):
    n = len(mixed)
    outs = (sds((mixed[0].shape[1], d.shape[1]), bf16),) * n
    return call(functools.partial(grad_out_kernel, n), (d, *mixed), outs, "grad_out")


def attend_back_kernel(added, a_ref, d_ref, w_ref, qkv_ref, lse_ref, *refs):
    scale = HEAD_DIM**-0.5
    got, dqkv_ref, grads, dm_ref = refs[:added], refs[added], refs[added + 1 : -1], refs[-1]
    dm_ref[...] = dot(d_ref[...], w_ref[...], NT).astype(bf16)

    def head(h):
        cols = span(h, HEAD_DIM)
        q, k, v = (qkv_ref[c, :, cols] for c in range(3))
        dm = dm_ref[:, cols]
        probs = jnp.exp2(dot(k, q, NT) * (scale * LOG2E) - lse_ref[pl.ds(h, 1), :])
        d_probs = dot(v, dm, NT)
        dqkv_ref[2, :, cols] = dot(probs.astype(bf16), dm).astype(bf16)
        delta = jnp.sum(d_probs * probs, axis=0, keepdims=True)
        d_scores = (probs * (d_probs - delta)).astype(bf16)
        dqkv_ref[1, :, cols] = (dot(d_scores, q) * scale).astype(bf16)
        dqkv_ref[0, :, cols] = (dot(k, d_scores, TN) * scale).T.astype(bf16)

    unrolled(w_ref.shape[0] // HEAD_DIM, head)
    size = GRAD_BLOCK

    def grad_cols(i):
        cols = span(i, size)
        for c in range(3):
            grad = dot(dqkv_ref[c], a_ref[:, cols], TN)
            grads[c][:, cols] = (grad + got[c][:, cols].astype(f32) if added else grad).astype(bf16)

    loop(a_ref.shape[1] // size, grad_cols)


def attend_back(a, d, w, qkv, lse, got=()):
    length, width = a.shape
    local = w.shape[0]
    outs = (sds((3, length, local), bf16), *[sds((local, width), bf16)] * 3)
    outs = call(functools.partial(attend_back_kernel, len(got)), (a, d, w, qkv, lse, *got), outs, "attend_back", 12, False, [pltpu.VMEM((length, local), bf16)])
    return outs[0], outs[1:]


def join_kernel(axes, at_ref, *refs):
    quarters, outs = refs[:4], refs[4:]
    width = quarters[0].shape[1]
    for p, quarter in enumerate(quarters):
        place = pl.ds(pl.multiple_of(at_ref[p] * width, width), width)
        for i, (out, axis) in enumerate(zip(outs, axes, strict=True)):
            if axis == 0:
                out[place, :] = quarter[i]
            else:
                out[:, place] = quarter[i]


def join(quarters, likes, axes):
    flat = [(v.shape[-2:], 0 if axis == 3 else axis) for v, axis in zip(likes, axes, strict=True) for _ in range(v.size // (v.shape[-1] * v.shape[-2]))]
    outs = [sds(shape, bf16) for shape, _ in flat]
    return call(functools.partial(join_kernel, tuple(axis for _, axis in flat)), quarters, outs, "join", 4, True)


def cut_kernel(axes, at_ref, *refs):
    n = len(axes)
    for out, p in zip(refs[n:], (0, 2), strict=True):
        size = out.shape[1]
        place = pl.ds(pl.multiple_of(at_ref[p] * size, size), size)
        i = 0
        for v, axis in zip(refs[:n], axes, strict=True):
            if axis == 3:
                for c in range(3):
                    out[i + c] = v[c, place, :]
                i += 3
            else:
                out[i] = v[place, :] if axis == 0 else v[:, place]
                i += 1


def cut(arrays, axes):
    size = max(arrays[0].shape) // 4
    outs = (sds((sum(v.size for v in arrays) // (4 * size * size), size, size), bf16),) * 2
    return call(functools.partial(cut_kernel, tuple(axes)), arrays, outs, "cut", 4, True)


def cut_one_kernel(at_ref, w_ref, out_ref):
    size = out_ref.shape[1]
    out_ref[...] = w_ref[:, span(at_ref[5], size), :]


def cut_one(w):
    n, width, local = w.shape
    return call(cut_one_kernel, (w,), (sds((n, width // 4, local), bf16),), "cut", 4, True)[0]


def middle_kernel(y_ref, z_ref, a_ref, b_ref):
    rows = a_ref.shape[1]
    a_ref[...] = z_ref[:, 0:rows, :]
    b_ref[...] = y_ref[:, rows : 2 * rows, :]


def middle(y, z):
    n, rows, local = y.shape
    return call(middle_kernel, (y, z), (sds((n, rows // 2, local), bf16),) * 2, "middle", 4)


def join_four_kernel(at_ref, own_ref, y_ref, z_ref, a_ref, b_ref, *outs):
    size = own_ref.shape[1]
    for i, out in enumerate(outs):
        out[span(at_ref[5], size), :] = own_ref[i]
        out[span(at_ref[6], size), :] = y_ref[i]
        out[span(at_ref[7], size), :] = z_ref[i]
        out[span(at_ref[8] * 2, size // 2), :] = a_ref[i]
        out[span(at_ref[8] * 2 + 1, size // 2), :] = b_ref[i]


def join_four(own, y, z, a, b):
    n, rows, local = own.shape
    return call(join_four_kernel, (own, y, z, a, b), (sds((4 * rows, local), bf16),) * n, "join", 4, True)


def half_of(ref, at, rows):
    place = pl.ds(pl.multiple_of(at * rows, rows), rows)
    return ref[place, :] if len(ref.shape) == 2 else ref[:, place, :]


def add_kernel(a_ref, b_ref, o_ref):
    o_ref[...] = a_ref[...] + b_ref[...]


def add(a, b):
    return call(add_kernel, (a, b), (sds(a.shape, a.dtype),), "add", 4)[0]


def halved(shape, n=None):
    half = (shape[-2] // 2, shape[-1])
    return sds(half if n is None else (n, *half), bf16)


def split_add_kernel(n, at_ref, *refs):
    a, b, (give_ref, keep_ref) = refs[:n], refs[n : 2 * n], refs[2 * n :]
    rows = give_ref.shape[-2]
    for at, out in ((1 - at_ref[0], give_ref), (at_ref[0], keep_ref)):
        for i in range(n):
            total = half_of(a[i], at, rows) + half_of(b[i], at, rows)
            if len(out.shape) == 2:
                out[...] = total
            else:
                out[i] = total


def split_add(a, b):
    n = len(a)
    outs = (halved(a[0].shape, None if n == 1 else n),) * 2
    return call(functools.partial(split_add_kernel, n), (*a, *b), outs, "split_add", 4, True)


EXTRA = 16


def pack_kernel(*refs):
    gains, got_gains, outs = refs[4], refs[5], refs[6:]
    total = (gains[...] + got_gains[...]).astype(bf16)
    for a, b, out in zip(refs[:2], refs[2:4], outs, strict=True):
        rows = a.shape[0]
        out[0:rows, :] = a[...] + b[...]
        out[rows : rows + EXTRA, :] = jnp.concatenate([total, jnp.zeros((EXTRA - total.shape[0], total.shape[1]), bf16)])


def pack(kept, sent, got, gains, got_gains):
    rows, width = kept.shape
    return call(pack_kernel, (kept, sent, *got, gains, got_gains), (sds((rows + EXTRA, width), bf16),) * 2, "pack", 4)


def split_packed_kernel(at_ref, a_ref, b_ref, give_ref, keep_ref):
    rows = give_ref.shape[0] - EXTRA
    extra = slice(2 * rows, 2 * rows + EXTRA)
    gains = a_ref[extra, :] + b_ref[extra, :]
    for at, out in ((1 - at_ref[0], give_ref), (at_ref[0], keep_ref)):
        out[0:rows, :] = half_of(a_ref, at, rows) + half_of(b_ref, at, rows)
        out[rows : rows + EXTRA, :] = gains


def split_packed(a, b):
    shape = ((a.shape[0] - EXTRA) // 2 + EXTRA, a.shape[1])
    return call(split_packed_kernel, (a, b), (sds(shape, bf16),) * 2, "split_add", 4, True)


def finish_packed_kernel(at_ref, mine_ref, other_ref, out_ref, gain1_ref, gain2_ref):
    rows = out_ref.shape[0] // 2
    for at, ref in ((at_ref[0], mine_ref), (1 - at_ref[0], other_ref)):
        out_ref[pl.ds(pl.multiple_of(at * rows, rows), rows), :] = ref[0:rows, :].astype(f32)
    gains = mine_ref[rows : rows + EXTRA, :].astype(f32)
    gain1_ref[...] = gains[0:1, :]
    gain2_ref[...] = gains[1:2, :]


def finish_packed(mine, other):
    rows, width = 2 * (mine.shape[0] - EXTRA), mine.shape[1]
    outs = (sds((rows, width), f32), sds((1, width), f32), sds((1, width), f32))
    return call(finish_packed_kernel, (mine, other), outs, "finish", 6, True)


def pick_kernel(at_ref, a_ref, b_ref, o_ref):
    @pl.when(at_ref[4] == 1)
    def _():
        o_ref[...] = b_ref[...]

    @pl.when(at_ref[4] == 0)
    def _():
        o_ref[...] = a_ref[...]


def pick(a, b):
    return call(pick_kernel, (a, b), (sds(a.shape, a.dtype),), "pick", 4, True)[0]


def placed(ref, at, index=None):
    rows = ref.shape[-2]
    return pl.ds(pl.multiple_of(at * rows, rows), rows), (ref[...] if index is None else ref[index]).astype(f32)


def finish_kernel(turned, at_ref, mine_ref, other_ref, *outs):
    for at, ref in ((at_ref[0], mine_ref), (1 - at_ref[0], other_ref)):
        for i, (out, turn) in enumerate(zip(outs, turned, strict=True)):
            place, v = placed(ref, at, i if len(turned) > 1 else None)
            if turn:
                out[:, place] = v.T
            else:
                out[place, :] = v


def finish(mine, other, turned):
    rows, width = 2 * mine.shape[-2], mine.shape[-1]
    outs = [sds((width, rows) if turn else (rows, width), f32) for turn in turned]
    return call(functools.partial(finish_kernel, turned), (mine, other), outs, "finish", 6, True)


def finish_slot_kernel(at_ref, mine_ref, other_ref, *refs):
    for at, ref in ((at_ref[0], mine_ref), (1 - at_ref[0], other_ref)):
        place, v = placed(ref, at)
        refs[-1][0, :, place] = v.T


def finish_slot(mine, other, slot, slots, into):
    rows, width = mine.shape
    spec = pl.BlockSpec(memory_space=pltpu.VMEM)
    return pl.pallas_call(
        functools.partial(placed_kernel, finish_slot_kernel),
        grid=(1,),
        in_specs=[spec, spec] + [pl.BlockSpec(memory_space=pl.ANY)] * (into is not None),
        out_specs=pl.BlockSpec((1, width, 2 * rows), lambda i: (slot, 0, 0)),
        out_shape=sds((slots, width, 2 * rows), f32),
        input_output_aliases={} if into is None else {2: 0},
        compiler_params=params(6),
        cost_estimate=cost(),
        name="finish",
    )(mine, other, *([] if into is None else [into]))


def input_back_kernel(n, counts, *refs):
    d_qkv, refs = refs[:n], refs[n:]
    w = []
    for count in counts:
        w.append(matrices(refs[:count]))
        refs = refs[count:]
    x_ref, dres_ref, g_ref, other_ref, out_ref, gains_ref = refs

    def step(rows, gain):
        total = None
        for j in range(n):
            for c in range(3):
                part = dot(d_qkv[j][c, rows, :], w[j](c), NT)
                total = part if total is None else total + part
        back, part = norm_back(total, x_ref[rows, :], g_ref[...])
        out_ref[rows, :] = dres_ref[rows, :] + back
        return gain + part

    gain = by_rows(x_ref.shape[0], step, jnp.zeros(other_ref.shape, f32), 256)
    gains_ref[0:1, :] = jnp.sum(gain, axis=0, keepdims=True)
    gains_ref[1:2, :] = jnp.sum(other_ref[...], axis=0, keepdims=True)


def input_back(d_qkv, w, x, d_resid, gain, other):
    outs = (sds(x.shape, f32), sds((2, x.shape[1]), f32))
    kernel = functools.partial(input_back_kernel, len(w), tuple(len(v) for v in w))
    return call(kernel, (*d_qkv, *[m for v in w for m in v], x, d_resid, gain, other), outs, "input_back", 12)


def swap(axis, size, bit):
    pairs = [(i, i ^ bit) for i in range(size)]
    return lambda v: lax.ppermute(v, axis, pairs)


def bits_of(size):
    return [1 << b for b in reversed(range(size.bit_length() - 1))]


class Run:
    def __init__(self):
        self.token = None

    def tie(self, v):
        if self.token is None:
            return v
        return lax.optimization_barrier((v, self.token))[0]

    def compute(self, step, first, *rest):
        outs = step(self.tie(first), *rest)
        self.token = jax.tree.leaves(outs)[0]
        return outs

    def send(self, move, v):
        v = self.tie(v)
        self.token = v
        return move(v)


class Names:
    def __getattr__(self, name):
        return name


N = Names()
ORDER = (
    N.c0_q, N.sl_q, N.xp_q, N.sl_d, N.c0_d, N.sl_ou, N.xp_ou, N.xp_d, N.xr_d, N.prep, N.c0_ou_0, N.y_q, N.z_q,
    N.y_ou, N.xr_ou, N.att2, N.sm_q, N.z_ou, N.att0, N.z_d, N.zz_q, N.yy_q, N.y_d, N.as_ou, N.as_q, N.cx_q_0,
    N.cx_q_1, N.cx_ou_0, N.att1, N.as_d, N.cx_d, N.cx_q_2, N.cx_ou_1, N.c0_ou_1, N.att3, N.proj, N.mlpR, N.cF1_0,
    N.cF1_1, N.mlpP, N.cF0_1, N.cF0_0, N.aF1, N.F_yx, N.mlpback, N.ab2, N.ab3, N.cQ1_1, N.cQ0_1, N.aF0, N.cQ1_0,
    N.cQ1_2, N.cQ0_0, N.F_ax, N.F_x, N.cQ0_2, N.F_yo, N.gout, N.cO_1, N.cO_0, N.ab1, N.Qb_x, N.ab0, N.F_ao,
    N.F_a2, N.F_z1, N.Qa_x, N.inback, N.g0, N.Qc_x, N.aO, N.O_x, N.Qb_a1, N.Qb_y, N.F_a3, N.Qb_a2, N.F_z2,
    N.O_a1, N.O_y, N.Qb_z1, N.O_a2, N.O_z1, N.F_a4, N.F_z3, N.Qb_a3, N.Qb_z2, N.Qa_a1, N.Qa_y, N.O_a3, N.O_z2,
    N.Qa_a2, N.Qa_z1, N.Qc_a1, N.Qc_y, N.Qb_a4, N.F_a5, N.F_w, N.O_a4, N.O_z3, N.Qa_a3, N.Qa_z2, N.Qc_a2,
    N.Qc_z1, N.Qb_z3, N.Qa_a4, N.Qa_z3, N.Qc_a3, N.O_a5, N.O_w, N.Qb_a5, N.Qb_w, N.F_f, N.Qc_z2, N.Qa_a5, N.Qa_w,
    N.O_f, N.Qc_a4, N.Qc_z3, N.Qa_f, N.mlpout, N.Qb_f, N.Qc_a5, N.Qc_w, N.Qc_f,
)
GROUPS = {"q": ("qkv",), "ou": ("out", "up"), "d": ("down",)}
FOUR = ("q",)
CHUNKS = {"F": "F", "O": "O", "Qa": "Q", "Qb": "Q", "Qc": "Q"}
AXES = {"qkv": 3, "out": 1, "up": 0, "down": 1}


def per_device(
    sizes,
    inputs,
    norm1_gain,
    weight_qkv,
    weight_out,
    norm2_gain,
    weight_up,
    weight_down,
    cotangent,
):
    n_rep, n_dp, n_mp = sizes["rep"], sizes["dp"], sizes["mp"]
    if n_mp != 4 or n_rep != 2 or n_dp & (n_dp - 1) or n_dp < 2:
        raise ValueError("unsupported mesh")
    shape = inputs.shape
    x = inputs.reshape(shape[-2:])
    cot = cotangent.reshape(shape[-2:])
    gain1, gain2 = norm1_gain.reshape(1, -1), norm2_gain.reshape(1, -1)
    width = x.shape[1]
    run = Run()
    line = n_dp == 4

    core = swap("mp", n_mp, 1)
    far = swap("mp", n_mp, 2)
    rep = swap("rep", n_rep, 1)
    near = swap("dp", n_dp, 1)
    own = {"qkv": weight_qkv, "out": weight_out, "up": weight_up, "down": weight_down}
    w = {k: [[v], None, None, None] for k, v in own.items()}
    env = {}

    def gather_task(kind, g, i="0"):
        names = GROUPS[g]
        if kind == "c0":
            k = names[int(i)]
            w[k][2] = [run.send(core, own[k])]
        elif kind == "x":
            for k in names:
                w[k][1] = [run.send(far, own[k])]
        elif g in FOUR and kind == "sl":
            env["p", g] = run.compute(cut_one, own[names[0]])
        elif g in FOUR and kind == "z":
            env["pz", g] = run.send(near, env["px", g])
        elif g in FOUR and kind == "sm":
            env["a", g], env["b", g] = run.compute(middle, env["py", g], env["pz", g])
        elif kind == "yy":
            env["ya", g] = run.send(rep, env["a", g])
        elif kind == "zz":
            env["zb", g] = run.send(near, env["b", g])
        elif g in FOUR and kind == "as":
            w[names[0]][1] = run.compute(join_four, env["px", g], env["py", g], env["pz", g], env["ya", g], env["zb", g])
        elif kind == "sl":
            env["p", g], env["r", g] = run.compute(lambda *v: cut(v, [AXES[k] for k in names]), *[own[k] for k in names])
        elif kind == "xp":
            env["px", g] = run.send(far, env["p", g])
        elif kind == "xr":
            env["rx", g] = run.send(far, env["r", g])
        elif kind == "y":
            env["py", g] = run.send(rep, env["px", g])
        elif kind == "z":
            env["rz", g] = run.send(near, env["rx", g])
        elif kind == "as":
            outs = run.compute(
                lambda *v: join(v, [own[k] for k in names], [AXES[k] for k in names]),
                env["px", g], env["py", g], env["rx", g], env["rz", g],
            )
            for k in names:
                n = 3 if AXES[k] == 3 else 1
                w[k][1], outs = outs[:n], outs[n:]
        elif kind == "cx":
            k, m = [(k, m) for k in names for m in range(len(w[k][1]))][int(i)]
            w[k][3] = w[k][3] or [None] * len(w[k][1])
            w[k][3][m] = run.send(core, w[k][1][m])

    def one(k):
        return [v[0] for v in w[k]]

    def over_dp(v):
        for bit in bits_of(n_dp):
            v = run.compute(add, v, run.send(swap("dp", n_dp, bit), v))
        return v

    def chunk_task(name, stage):
        source = CHUNKS[name]
        c = env.setdefault(("chunk", name), {})

        def z(pairs):
            return lambda v: lax.ppermute(v, "dp", pairs)

        if stage == "f":
            done(name, c["v"], c["w"])
        elif stage == "w":
            c["w"] = run.send(rep, c["v"])
        elif stage == "z1" and line:
            c["z"] = run.send(z([(0, 1), (3, 2)]), c["v"])
        elif stage == "z2" and line:
            c["z"] = run.send(z([(1, 2), (2, 1)]), c["v"])
        elif stage == "z3" and line:
            c["z"] = run.send(z([(1, 0), (2, 3)]), c["v"])
        elif stage == "a3" and line:
            c["v"] = run.compute(add, c["v"], c["z"])
        elif stage == "a4":
            c["v"] = run.compute(add, c["v"], c["z"]) if line else over_dp(c["v"])
        elif stage == "a5" and line:
            c["v"] = run.compute(lambda *v: pick(*v), c["v"], c["z"])
        elif source in ("Q", "O"):

            def part(j):
                return env["O"][j] if source == "O" else env["gQ", j]["abc".index(name[1])]

            if stage == "x":
                c["x"] = run.send(far, part(1))
            elif stage == "a1":
                step = (lambda *v: split_packed(*v)) if source == "O" else (lambda a, b: split_add([a], [b]))
                c["give"], c["v"] = run.compute(step, part(0), c["x"])
            elif stage == "y":
                c["y"] = run.send(rep, c["give"])
            elif stage == "a2":
                c["v"] = run.compute(add, c["v"], c["y"])
        elif source == "F":
            j = "ox".index(stage[1]) if stage[0] in "ya" and stage[1] in "ox" else None
            if stage in ("yo", "yx"):
                c[stage] = run.send(rep, env["F", j][0])
            elif stage in ("ao", "ax"):
                c[stage] = run.compute(add, env["F", j][1], c["y" + stage[1]])
            elif stage == "x":
                c["x"] = run.send(far, c["ax"])
            elif stage == "a2":
                c["v"] = run.compute(add, c["ao"], c["x"])

    def done(name, mine, other):
        if name == "F":
            env["down"], env["up"] = run.compute(lambda *v: finish(*v, (False, True)), mine, other)
        elif name == "O":
            env["out"], env["gain1"], env["gain2"] = run.compute(lambda *v: finish_packed(*v), mine, other)
        else:
            env["qkv"] = run.compute(lambda *v: finish_slot(*v, "abc".index(name[1]), 3, env.get("qkv")), mine, other)

    def task(t):
        if t == "prep":
            env["a1"], env["dm"] = run.compute(lambda c, v, g: prep(v, c, g), cot, x, gain1)
        elif t[:3] == "att":
            j = int(t[3])
            env["att", j] = run.compute(attend, env["a1"], w["qkv"][j])
        elif t == "proj":
            env["resid"], env["a2"] = run.compute(lambda *m: project(m, one("out"), x, gain2), *[env["att", j][1] for j in range(4)])
        elif t in ("mlpP", "mlpR"):
            js = (0, 2) if t == "mlpP" else (1, 3)
            hid, dpre, grads = run.compute(lambda a: mlp(a, env["dm"], [w["up"][j][0] for j in js], [w["down"][j][0] for j in js]), env["a2"])
            for i, j in enumerate(js):
                env["hid", j], env["dpre", j], env["gF", j] = hid[i], dpre[i], grads[i]
        elif t[:2] in ("cF", "cQ"):
            (kind, j), i = t[1:3], int(t[-1])
            grads = env["g" + kind, 2 + int(j)]
            env.setdefault(("r" + kind, int(j)), [None] * len(grads))[i] = run.send(core, grads[i])
        elif t in ("aF0", "aF1"):
            j = int(t[2])
            env["F", j] = run.compute(lambda *v: split_add(v[:2], v[2:]), *env["gF", j], *env["rF", j])
        elif t == "mlpback":
            env["dres"], env["datt"], env["part2"] = run.compute(
                lambda *d: mlp_back(d, one("up"), env["resid"], cot, gain2), *[env["dpre", j] for j in range(4)]
            )
        elif t == "mlpout":
            env["output"] = run.compute(lambda *h: mlp_out(h, one("down"), env["resid"]), *[env["hid", j] for j in range(4)])
        elif t == "gout":
            env["gO"] = run.compute(lambda d: grad_out(d, [env["att", j][1] for j in range(4)]), env["datt"])
        elif t[:2] == "cO":
            env.setdefault("rO", [None] * 2)[int(t[-1])] = run.send(core, env["gO"][2 + int(t[-1])])
        elif t == "aO":
            env["O"] = run.compute(lambda *v: pack(*v, env["rO"], env["g"], env["gr"]), *env["gO"][:2])
        elif t[:2] == "ab":
            j = int(t[2])
            got = env["rQ", j] if j < 2 else ()
            env["dqkv", j], env["gQ", j] = run.compute(
                lambda d: attend_back(env["a1"], d, w["out"][j][0], env["att", j][0], env["att", j][2], got), env["datt"]
            )
        elif t == "inback":
            env["gin"], env["g"] = run.compute(
                lambda *d: input_back(d, w["qkv"], x, env["dres"], gain1, env["part2"]), *[env["dqkv", j] for j in range(4)]
            )
        elif t == "g0":
            env["gr"] = run.send(core, env["g"])
        elif t.split("_")[1] in GROUPS:
            gather_task(*t.split("_"))
        else:
            chunk_task(*t.split("_"))

    for t in ORDER:
        task(t)
    return (
        env["output"].reshape(shape),
        env["gin"].reshape(shape),
        env["gain1"].reshape(-1),
        env["qkv"],
        env["out"],
        env["gain2"].reshape(-1),
        env["up"],
        env["down"],
    )


def solution(mesh):
    return jax.shard_map(
        functools.partial(per_device, dict(mesh.shape)),
        mesh=mesh,
        in_specs=(
            P(("rep", "mp"), "dp", None, None),
            P(),
            P(None, None, "mp"),
            P("mp", None),
            P(),
            P(None, "mp"),
            P("mp", None),
            P(("rep", "mp"), "dp", None, None),
        ),
        out_specs=(
            P(("rep", "mp"), "dp", None, None),
            P(("rep", "mp"), "dp", None, None),
            P(),
            P(None, None, "mp"),
            P("mp", None),
            P(),
            P(None, "mp"),
            P("mp", None),
        ),
        check_vma=False,
    )
```

```python
import functools

import jax
import jax.numpy as jnp
from jax import lax
from jax.experimental import pallas as pl
from jax.experimental.pallas import tpu as pltpu
from jax.sharding import PartitionSpec as P

HEAD_DIM = 128
PROJ_BLOCK = 256
GRAD_BLOCK = 512
EPS = 1e-05
LOG2E = 1.4426950408889634
GELU_A = 0.7978845608028654
GELU_B = 0.044715
f32 = jnp.float32
bf16 = jnp.bfloat16

NN = (((1,), (0,)), ((), ()))
NT = (((1,), (1,)), ((), ()))
TN = (((0,), (0,)), ((), ()))


def dot(a, b, dims=NN):
    return lax.dot_general(a, b, dims, preferred_element_type=f32)


def normed(v):
    mean = jnp.mean(v, axis=-1, keepdims=True)
    centred = v - mean
    r = lax.rsqrt(jnp.mean(centred * centred, axis=-1, keepdims=True) + EPS)
    return centred * r, r


def fold(v):
    return jnp.sum(v.reshape(-1, 8, v.shape[-1]), axis=0)


def params(mib=8):
    return pltpu.CompilerParams(vmem_limit_bytes=mib * 2**20)


def cost():
    return pl.CostEstimate(flops=1, bytes_accessed=1, transcendentals=0)


def whole(n):
    return [pl.BlockSpec(memory_space=pltpu.VMEM)] * n


def sds(shape, dtype):
    return jax.ShapeDtypeStruct(shape, dtype)


def by_rows(length, step, init=None, block=512):
    if block >= length:
        return step(slice(None), init)
    return lax.fori_loop(0, length // block, lambda i, c: step(span(i, block), c), init)


def span(i, size):
    if isinstance(i, int):
        return slice(i * size, (i + 1) * size)
    return pl.ds(pl.multiple_of(i * size, size), size)


def loop(n, step):
    lax.fori_loop(0, n, lambda i, _: step(i), None)


def unrolled(n, step):
    for i in range(n):
        step(i)


def places():
    rep, dp = lax.axis_index("rep"), lax.axis_index("dp")
    near = lax.rem(dp, 2)
    outer = jnp.where((dp == 0) | (dp == lax.axis_size("dp") - 1), 1, 0)
    quarters = [2 * r + n for r, n in ((rep, near), (1 - rep, near), (rep, 1 - near), (1 - rep, 1 - near))]
    return rep, 1 - rep, 2 + near, 3 - near, outer, *quarters


def placed_kernel(kernel, *refs):
    kernel(places(), *refs)


def call(kernel, ins, outs, name, mib=8, at=False, scratch=()):
    if at:
        kernel = functools.partial(placed_kernel, kernel)
    return pl.pallas_call(
        kernel,
        in_specs=whole(len(ins)),
        out_specs=whole(len(outs)),
        out_shape=list(outs),
        scratch_shapes=list(scratch),
        compiler_params=params(mib),
        cost_estimate=cost(),
        name=name,
    )(*ins)


def matrices(refs):
    return (lambda c: refs[0][c]) if len(refs) == 1 else (lambda c: refs[c][...])


def prep_kernel(x_ref, c_ref, g_ref, a_ref, d_ref):
    def step(rows, _):
        a_ref[rows, :] = (normed(x_ref[rows, :])[0] * g_ref[...]).astype(bf16)
        d_ref[rows, :] = c_ref[rows, :].astype(bf16)

    by_rows(x_ref.shape[0], step)


def prep(x, cot, gain):
    return call(prep_kernel, (x, cot, gain), (sds(x.shape, bf16),) * 2, "prep")


def attend_kernel(n, a_ref, *refs):
    w, (qkv_ref, mixed_ref, lse_ref) = matrices(refs[:n]), refs[n:]
    scale = HEAD_DIM**-0.5 * LOG2E

    def project_rows(rows, _):
        for c in range(3):
            qkv_ref[c, rows, :] = dot(a_ref[rows, :], w(c)).astype(bf16)

    def head(h):
        cols = span(h, HEAD_DIM)
        q, k, v = (qkv_ref[c, :, cols] for c in range(3))
        scores = dot(k, q, NT)
        top = jnp.max(scores, axis=0, keepdims=True)
        expd = jnp.exp2((scores - top) * scale)
        total = jnp.sum(expd, axis=0, keepdims=True)
        mixed = dot(v, expd.astype(bf16), TN) / total
        mixed_ref[:, cols] = mixed.T.astype(bf16)
        lse_ref[pl.ds(h, 1), :] = top * scale + jnp.log2(total)

    by_rows(a_ref.shape[0], project_rows, None, PROJ_BLOCK)
    loop(qkv_ref.shape[2] // HEAD_DIM, head)


def attend(a, w):
    length, local = a.shape[0], w[0].shape[-1]
    outs = (sds((3, length, local), bf16), sds((length, local), bf16), sds((local // HEAD_DIM, length), f32))
    return call(functools.partial(attend_kernel, len(w)), (a, *w), outs, "attend", 12)


def project_kernel(n, *refs):
    mixed, w = refs[:n], refs[n : 2 * n]
    x_ref, g_ref, resid_ref, a_ref = refs[2 * n :]

    def step(rows, _):
        total = dot(mixed[0][rows, :], w[0][...])
        for j in range(1, n):
            total += dot(mixed[j][rows, :], w[j][...])
        resid = x_ref[rows, :] + total
        resid_ref[rows, :] = resid
        a_ref[rows, :] = (normed(resid)[0] * g_ref[...]).astype(bf16)

    by_rows(x_ref.shape[0], step)


def project(mixed, w, x, gain):
    outs = (sds(x.shape, f32), sds(x.shape, bf16))
    return call(functools.partial(project_kernel, len(mixed)), (*mixed, *w, x, gain), outs, "project")


def mlp_kernel(n, *refs):
    a_ref, d_ref = refs[:2]
    up, down = refs[2 : 2 + n], refs[2 + n : 2 + 2 * n]
    outs = refs[2 + 2 * n :]
    hid, dpre, grads = outs[:n], outs[n : 2 * n], outs[2 * n :]
    for j in range(n):
        u = dot(a_ref[...], up[j][...])
        d_hidden = dot(d_ref[...], down[j][...], NT)
        sq = u * u
        t = jnp.tanh(GELU_A * u * (1.0 + GELU_B * sq))
        half = 0.5 * (1.0 + t)
        hidden = (u * half).astype(bf16)
        slope = half + 0.5 * u * (1.0 - t * t) * (GELU_A * (1.0 + 3.0 * GELU_B * sq))
        d_pre = (d_hidden * slope).astype(bf16)
        hid[j][...] = hidden
        dpre[j][...] = d_pre
        grads[2 * j][...] = dot(hidden, d_ref[...], TN).astype(bf16)
        grads[2 * j + 1][...] = dot(d_pre, a_ref[...], TN).astype(bf16)


def mlp(a, d, up, down):
    n = len(up)
    length, width = a.shape
    local = up[0].shape[1]
    act, grad = sds((length, local), bf16), sds((local, width), bf16)
    outs = call(functools.partial(mlp_kernel, n), (a, d, *up, *down), (act,) * (2 * n) + (grad,) * (2 * n), "mlp", 12)
    return outs[:n], outs[n : 2 * n], [outs[2 * n + 2 * j : 2 * n + 2 * j + 2] for j in range(n)]


def norm_back(d_a, v, gain):
    xhat, r = normed(v)
    e = d_a * gain
    back = r * (e - jnp.mean(e, axis=-1, keepdims=True) - xhat * jnp.mean(e * xhat, axis=-1, keepdims=True))
    return back, fold(d_a * xhat)


def mlp_back_kernel(n, *refs):
    d_pre, up = refs[:n], refs[n : 2 * n]
    resid_ref, c_ref, g_ref, dres_ref, datt_ref, gain_ref = refs[2 * n :]

    def step(rows, gain):
        total = dot(d_pre[0][rows, :], up[0][...], NT)
        for j in range(1, n):
            total += dot(d_pre[j][rows, :], up[j][...], NT)
        back, part = norm_back(total, resid_ref[rows, :], g_ref[...])
        d_resid = c_ref[rows, :] + back
        dres_ref[rows, :] = d_resid
        datt_ref[rows, :] = d_resid.astype(bf16)
        return gain + part

    gain_ref[...] = by_rows(c_ref.shape[0], step, jnp.zeros(gain_ref.shape, f32), 256)


def mlp_back(d_pre, up, resid, cot, gain):
    n = len(up)
    outs = (sds(resid.shape, f32), sds(resid.shape, bf16), sds((8, resid.shape[1]), f32))
    return call(functools.partial(mlp_back_kernel, n), (*d_pre, *up, resid, cot, gain), outs, "mlp_back")


def mlp_out_kernel(n, *refs):
    hid, down = refs[:n], refs[n : 2 * n]
    resid_ref, out_ref = refs[2 * n :]

    def step(rows, _):
        total = resid_ref[rows, :]
        for j in range(n):
            total += dot(hid[j][rows, :], down[j][...])
        out_ref[rows, :] = total

    by_rows(resid_ref.shape[0], step)


def mlp_out(hid, down, resid):
    n = len(down)
    return call(functools.partial(mlp_out_kernel, n), (*hid, *down, resid), (sds(resid.shape, f32),), "mlp_out")[0]


def grad_out_kernel(n, d_ref, *refs):
    for mixed, out in zip(refs[:n], refs[n:], strict=True):
        out[...] = dot(mixed[...], d_ref[...], TN).astype(bf16)


def grad_out(d, mixed):
    n = len(mixed)
    outs = (sds((mixed[0].shape[1], d.shape[1]), bf16),) * n
    return call(functools.partial(grad_out_kernel, n), (d, *mixed), outs, "grad_out")


def attend_back_kernel(added, a_ref, d_ref, w_ref, qkv_ref, lse_ref, *refs):
    scale = HEAD_DIM**-0.5
    got, dqkv_ref, grads, dm_ref = refs[:added], refs[added], refs[added + 1 : -1], refs[-1]
    dm_ref[...] = dot(d_ref[...], w_ref[...], NT).astype(bf16)

    def head(h):
        cols = span(h, HEAD_DIM)
        q, k, v = (qkv_ref[c, :, cols] for c in range(3))
        dm = dm_ref[:, cols]
        probs = jnp.exp2(dot(k, q, NT) * (scale * LOG2E) - lse_ref[pl.ds(h, 1), :])
        d_probs = dot(v, dm, NT)
        dqkv_ref[2, :, cols] = dot(probs.astype(bf16), dm).astype(bf16)
        delta = jnp.sum(d_probs * probs, axis=0, keepdims=True)
        d_scores = (probs * (d_probs - delta)).astype(bf16)
        dqkv_ref[1, :, cols] = (dot(d_scores, q) * scale).astype(bf16)
        dqkv_ref[0, :, cols] = (dot(k, d_scores, TN) * scale).T.astype(bf16)

    unrolled(w_ref.shape[0] // HEAD_DIM, head)
    size = GRAD_BLOCK

    def grad_cols(i):
        cols = span(i, size)
        for c in range(3):
            grad = dot(dqkv_ref[c], a_ref[:, cols], TN)
            grads[c][:, cols] = (grad + got[c][:, cols].astype(f32) if added else grad).astype(bf16)

    loop(a_ref.shape[1] // size, grad_cols)


def attend_back(a, d, w, qkv, lse, got=()):
    length, width = a.shape
    local = w.shape[0]
    outs = (sds((3, length, local), bf16), *[sds((local, width), bf16)] * 3)
    outs = call(functools.partial(attend_back_kernel, len(got)), (a, d, w, qkv, lse, *got), outs, "attend_back", 12, False, [pltpu.VMEM((length, local), bf16)])
    return outs[0], outs[1:]


def join_kernel(axes, at_ref, *refs):
    quarters, outs = refs[:4], refs[4:]
    width = quarters[0].shape[1]
    for p, quarter in enumerate(quarters):
        place = pl.ds(pl.multiple_of(at_ref[p] * width, width), width)
        for i, (out, axis) in enumerate(zip(outs, axes, strict=True)):
            if axis == 0:
                out[place, :] = quarter[i]
            else:
                out[:, place] = quarter[i]


def join(quarters, likes, axes):
    flat = [(v.shape[-2:], 0 if axis == 3 else axis) for v, axis in zip(likes, axes, strict=True) for _ in range(v.size // (v.shape[-1] * v.shape[-2]))]
    outs = [sds(shape, bf16) for shape, _ in flat]
    return call(functools.partial(join_kernel, tuple(axis for _, axis in flat)), quarters, outs, "join", 4, True)


def cut_kernel(axes, at_ref, *refs):
    n = len(axes)
    for out, p in zip(refs[n:], (0, 2), strict=True):
        size = out.shape[1]
        place = pl.ds(pl.multiple_of(at_ref[p] * size, size), size)
        i = 0
        for v, axis in zip(refs[:n], axes, strict=True):
            if axis == 3:
                for c in range(3):
                    out[i + c] = v[c, place, :]
                i += 3
            else:
                out[i] = v[place, :] if axis == 0 else v[:, place]
                i += 1


def cut(arrays, axes):
    size = max(arrays[0].shape) // 4
    outs = (sds((sum(v.size for v in arrays) // (4 * size * size), size, size), bf16),) * 2
    return call(functools.partial(cut_kernel, tuple(axes)), arrays, outs, "cut", 4, True)


def cut_one_kernel(at_ref, w_ref, out_ref):
    size = out_ref.shape[1]
    out_ref[...] = w_ref[:, span(at_ref[5], size), :]


def cut_one(w):
    n, width, local = w.shape
    return call(cut_one_kernel, (w,), (sds((n, width // 4, local), bf16),), "cut", 4, True)[0]


def middle_kernel(y_ref, z_ref, a_ref, b_ref):
    rows = a_ref.shape[1]
    a_ref[...] = z_ref[:, 0:rows, :]
    b_ref[...] = y_ref[:, rows : 2 * rows, :]


def middle(y, z):
    n, rows, local = y.shape
    return call(middle_kernel, (y, z), (sds((n, rows // 2, local), bf16),) * 2, "middle", 4)


def join_four_kernel(at_ref, own_ref, y_ref, z_ref, a_ref, b_ref, *outs):
    size = own_ref.shape[1]
    for i, out in enumerate(outs):
        out[span(at_ref[5], size), :] = own_ref[i]
        out[span(at_ref[6], size), :] = y_ref[i]
        out[span(at_ref[7], size), :] = z_ref[i]
        out[span(at_ref[8] * 2, size // 2), :] = a_ref[i]
        out[span(at_ref[8] * 2 + 1, size // 2), :] = b_ref[i]


def join_four(own, y, z, a, b):
    n, rows, local = own.shape
    return call(join_four_kernel, (own, y, z, a, b), (sds((4 * rows, local), bf16),) * n, "join", 4, True)


def half_of(ref, at, rows):
    place = pl.ds(pl.multiple_of(at * rows, rows), rows)
    return ref[place, :] if len(ref.shape) == 2 else ref[:, place, :]


def add_kernel(a_ref, b_ref, o_ref):
    o_ref[...] = a_ref[...] + b_ref[...]


def add(a, b):
    return call(add_kernel, (a, b), (sds(a.shape, a.dtype),), "add", 4)[0]


def halved(shape, n=None):
    half = (shape[-2] // 2, shape[-1])
    return sds(half if n is None else (n, *half), bf16)


def split_add_kernel(n, at_ref, *refs):
    a, b, (give_ref, keep_ref) = refs[:n], refs[n : 2 * n], refs[2 * n :]
    rows = give_ref.shape[-2]
    for at, out in ((1 - at_ref[0], give_ref), (at_ref[0], keep_ref)):
        for i in range(n):
            total = half_of(a[i], at, rows) + half_of(b[i], at, rows)
            if len(out.shape) == 2:
                out[...] = total
            else:
                out[i] = total


def split_add(a, b):
    n = len(a)
    outs = (halved(a[0].shape, None if n == 1 else n),) * 2
    return call(functools.partial(split_add_kernel, n), (*a, *b), outs, "split_add", 4, True)


EXTRA = 16


def pack_kernel(at_ref, *refs):
    gains, got_gains, give_ref, keep_ref = refs[4:]
    rows = give_ref.shape[1] - EXTRA
    total = (gains[...] + got_gains[...]).astype(bf16)
    extra = jnp.concatenate([total, jnp.zeros((EXTRA - total.shape[0], total.shape[1]), bf16)])
    for at, out in ((1 - at_ref[0], give_ref), (at_ref[0], keep_ref)):
        for i in range(2):
            out[i, 0:rows, :] = half_of(refs[i], at, rows) + half_of(refs[2 + i], at, rows)
            out[i, rows : rows + EXTRA, :] = extra


def pack(kept, sent, got, gains, got_gains):
    rows, width = kept.shape
    outs = (sds((2, rows // 2 + EXTRA, width), bf16),) * 2
    return call(pack_kernel, (kept, sent, *got, gains, got_gains), outs, "pack", 4, True)


def part_add_kernel(a_ref, b_ref, *outs):
    for i, out in enumerate(outs):
        out[...] = a_ref[i] + b_ref[i]


def part_add(a, b):
    return call(part_add_kernel, (a, b), [sds(a.shape[1:], bf16)] * a.shape[0], "add", 4)


def finish_packed_kernel(at_ref, mine_ref, other_ref, out_ref, gain1_ref, gain2_ref):
    rows = out_ref.shape[0] // 2
    for at, ref in ((at_ref[0], mine_ref), (1 - at_ref[0], other_ref)):
        out_ref[pl.ds(pl.multiple_of(at * rows, rows), rows), :] = ref[0:rows, :].astype(f32)
    gains = mine_ref[rows : rows + EXTRA, :].astype(f32)
    gain1_ref[...] = gains[0:1, :]
    gain2_ref[...] = gains[1:2, :]


def finish_packed(mine, other):
    rows, width = 2 * (mine.shape[0] - EXTRA), mine.shape[1]
    outs = (sds((rows, width), f32), sds((1, width), f32), sds((1, width), f32))
    return call(finish_packed_kernel, (mine, other), outs, "finish", 6, True)


def pick_kernel(at_ref, a_ref, b_ref, o_ref):
    @pl.when(at_ref[4] == 1)
    def _():
        o_ref[...] = b_ref[...]

    @pl.when(at_ref[4] == 0)
    def _():
        o_ref[...] = a_ref[...]


def pick(a, b):
    return call(pick_kernel, (a, b), (sds(a.shape, a.dtype),), "pick", 4, True)[0]


def placed(ref, at, index=None):
    rows = ref.shape[-2]
    return pl.ds(pl.multiple_of(at * rows, rows), rows), (ref[...] if index is None else ref[index]).astype(f32)


def finish_kernel(turned, at_ref, mine_ref, other_ref, *outs):
    for at, ref in ((at_ref[0], mine_ref), (1 - at_ref[0], other_ref)):
        for i, (out, turn) in enumerate(zip(outs, turned, strict=True)):
            place, v = placed(ref, at, i if len(turned) > 1 else None)
            if turn:
                out[:, place] = v.T
            else:
                out[place, :] = v


def finish(mine, other, turned):
    rows, width = 2 * mine.shape[-2], mine.shape[-1]
    outs = [sds((width, rows) if turn else (rows, width), f32) for turn in turned]
    return call(functools.partial(finish_kernel, turned), (mine, other), outs, "finish", 6, True)


def finish_slot_kernel(at_ref, mine_ref, other_ref, *refs):
    for at, ref in ((at_ref[0], mine_ref), (1 - at_ref[0], other_ref)):
        place, v = placed(ref, at)
        refs[-1][0, :, place] = v.T


def finish_slot(mine, other, slot, slots, into):
    rows, width = mine.shape
    spec = pl.BlockSpec(memory_space=pltpu.VMEM)
    return pl.pallas_call(
        functools.partial(placed_kernel, finish_slot_kernel),
        grid=(1,),
        in_specs=[spec, spec] + [pl.BlockSpec(memory_space=pl.ANY)] * (into is not None),
        out_specs=pl.BlockSpec((1, width, 2 * rows), lambda i: (slot, 0, 0)),
        out_shape=sds((slots, width, 2 * rows), f32),
        input_output_aliases={} if into is None else {2: 0},
        compiler_params=params(6),
        cost_estimate=cost(),
        name="finish",
    )(mine, other, *([] if into is None else [into]))


def input_back_kernel(n, counts, *refs):
    d_qkv, refs = refs[:n], refs[n:]
    w = []
    for count in counts:
        w.append(matrices(refs[:count]))
        refs = refs[count:]
    x_ref, dres_ref, g_ref, other_ref, out_ref, gains_ref = refs

    def step(rows, gain):
        total = None
        for j in range(n):
            for c in range(3):
                part = dot(d_qkv[j][c, rows, :], w[j](c), NT)
                total = part if total is None else total + part
        back, part = norm_back(total, x_ref[rows, :], g_ref[...])
        out_ref[rows, :] = dres_ref[rows, :] + back
        return gain + part

    gain = by_rows(x_ref.shape[0], step, jnp.zeros(other_ref.shape, f32), 256)
    gains_ref[0:1, :] = jnp.sum(gain, axis=0, keepdims=True)
    gains_ref[1:2, :] = jnp.sum(other_ref[...], axis=0, keepdims=True)


def input_back(d_qkv, w, x, d_resid, gain, other):
    outs = (sds(x.shape, f32), sds((2, x.shape[1]), f32))
    kernel = functools.partial(input_back_kernel, len(w), tuple(len(v) for v in w))
    return call(kernel, (*d_qkv, *[m for v in w for m in v], x, d_resid, gain, other), outs, "input_back", 12)


def swap(axis, size, bit):
    pairs = [(i, i ^ bit) for i in range(size)]
    return lambda v: lax.ppermute(v, axis, pairs)


def bits_of(size):
    return [1 << b for b in reversed(range(size.bit_length() - 1))]


class Run:
    def __init__(self):
        self.token = None

    def tie(self, v):
        if self.token is None:
            return v
        return lax.optimization_barrier((v, self.token))[0]

    def compute(self, step, first, *rest):
        outs = step(self.tie(first), *rest)
        self.token = jax.tree.leaves(outs)[0]
        return outs

    def send(self, move, v):
        v = self.tie(v)
        self.token = v
        return move(v)


class Names:
    def __getattr__(self, name):
        return name


N = Names()
ORDER = (
    N.c0_q, N.c0_ou_1, N.sl_q, N.xp_q, N.sl_ou, N.prep, N.att0, N.sl_d, N.xp_ou, N.c0_d, N.z_q, N.y_q, N.xr_ou,
    N.xp_d, N.att2, N.sm_q, N.y_ou, N.xr_d, N.zz_q, N.yy_q, N.z_ou, N.as_q, N.z_d, N.att1, N.cx_q_0, N.y_d,
    N.c0_ou_0, N.cx_q_1, N.as_d, N.as_ou, N.cx_ou_1, N.cx_ou_0, N.cx_q_2, N.cx_d, N.att3, N.proj, N.mlpR,
    N.cF1_0, N.cF1_1, N.mlpP, N.cF0_0, N.cF0_1, N.aF1, N.F_yx, N.mlpback, N.gout, N.ab3, N.cQ1_2, N.cQ1_0, N.aF0,
    N.cQ1_1, N.F_yo, N.F_ax, N.F_x, N.cO_1, N.ab1, N.Qa_x, N.ab2, N.cQ0_0, N.Qc_x, N.cO_0, N.cQ0_2, N.cQ0_1,
    N.F_ao, N.F_a2, N.F_z1, N.ab0, N.inback, N.g0, N.Qa_a1, N.F_a3, N.Qa_y, N.F_z2, N.aO, N.O_y, N.Qb_x, N.Qa_a2,
    N.Qc_a1, N.Qa_z1, N.mlpout, N.Qa_a3, N.Qa_z2, N.F_a4, N.F_z3, N.Qc_y, N.Qb_a1, N.Qb_y, N.O_a1, N.O_x,
    N.Qb_a2, N.Qb_z1, N.O_a2, N.Qa_a4, N.Qa_z3, N.F_a5, N.F_w, N.O_z1, N.Qc_a2, N.Qc_z1, N.Qb_a3, N.Qb_z2,
    N.O_a3, N.Qa_a5, N.O_z2, N.Qb_a4, N.Qb_z3, N.Qa_w, N.Qc_a3, N.Qc_z2, N.O_a4, N.F_f, N.O_z3, N.Qb_a5, N.Qa_f,
    N.Qb_w, N.Qc_a4, N.Qc_z3, N.O_a5, N.O_w, N.Qb_f, N.Qc_a5, N.Qc_w, N.O_f, N.Qc_f,
)
GROUPS = {"q": ("qkv",), "ou": ("out", "up"), "d": ("down",)}
FOUR = ("q",)
CHUNKS = {"F": "F", "O": "O", "Qa": "Q", "Qb": "Q", "Qc": "Q"}
AXES = {"qkv": 3, "out": 1, "up": 0, "down": 1}


def per_device(
    sizes,
    inputs,
    norm1_gain,
    weight_qkv,
    weight_out,
    norm2_gain,
    weight_up,
    weight_down,
    cotangent,
):
    n_rep, n_dp, n_mp = sizes["rep"], sizes["dp"], sizes["mp"]
    if n_mp != 4 or n_rep != 2 or n_dp & (n_dp - 1) or n_dp < 2:
        raise ValueError("unsupported mesh")
    shape = inputs.shape
    x = inputs.reshape(shape[-2:])
    cot = cotangent.reshape(shape[-2:])
    gain1, gain2 = norm1_gain.reshape(1, -1), norm2_gain.reshape(1, -1)
    width = x.shape[1]
    run = Run()
    line = n_dp == 4

    core = swap("mp", n_mp, 1)
    far = swap("mp", n_mp, 2)
    rep = swap("rep", n_rep, 1)
    near = swap("dp", n_dp, 1)
    own = {"qkv": weight_qkv, "out": weight_out, "up": weight_up, "down": weight_down}
    w = {k: [[v], None, None, None] for k, v in own.items()}
    env = {}

    def gather_task(kind, g, i="0"):
        names = GROUPS[g]
        if kind == "c0":
            k = names[int(i)]
            w[k][2] = [run.send(core, own[k])]
        elif kind == "x":
            for k in names:
                w[k][1] = [run.send(far, own[k])]
        elif g in FOUR and kind == "sl":
            env["p", g] = run.compute(cut_one, own[names[0]])
        elif g in FOUR and kind == "z":
            env["pz", g] = run.send(near, env["px", g])
        elif g in FOUR and kind == "sm":
            env["a", g], env["b", g] = run.compute(middle, env["py", g], env["pz", g])
        elif kind == "yy":
            env["ya", g] = run.send(rep, env["a", g])
        elif kind == "zz":
            env["zb", g] = run.send(near, env["b", g])
        elif g in FOUR and kind == "as":
            w[names[0]][1] = run.compute(join_four, env["px", g], env["py", g], env["pz", g], env["ya", g], env["zb", g])
        elif kind == "sl":
            env["p", g], env["r", g] = run.compute(lambda *v: cut(v, [AXES[k] for k in names]), *[own[k] for k in names])
        elif kind == "xp":
            env["px", g] = run.send(far, env["p", g])
        elif kind == "xr":
            env["rx", g] = run.send(far, env["r", g])
        elif kind == "y":
            env["py", g] = run.send(rep, env["px", g])
        elif kind == "z":
            env["rz", g] = run.send(near, env["rx", g])
        elif kind == "as":
            outs = run.compute(
                lambda *v: join(v, [own[k] for k in names], [AXES[k] for k in names]),
                env["px", g], env["py", g], env["rx", g], env["rz", g],
            )
            for k in names:
                n = 3 if AXES[k] == 3 else 1
                w[k][1], outs = outs[:n], outs[n:]
        elif kind == "cx":
            k, m = [(k, m) for k in names for m in range(len(w[k][1]))][int(i)]
            w[k][3] = w[k][3] or [None] * len(w[k][1])
            w[k][3][m] = run.send(core, w[k][1][m])

    def one(k):
        return [v[0] for v in w[k]]

    def over_dp(v):
        for bit in bits_of(n_dp):
            v = run.compute(add, v, run.send(swap("dp", n_dp, bit), v))
        return v

    def chunk_task(name, stage):
        source = CHUNKS[name]
        c = env.setdefault(("chunk", name), {})

        def z(pairs):
            return lambda v: lax.ppermute(v, "dp", pairs)

        if stage == "f":
            done(name, c["v"], c["w"])
        elif stage == "w":
            c["w"] = run.send(rep, c["v"])
        elif stage == "z1" and line:
            c["z"] = run.send(z([(0, 1), (3, 2)]), c["v"])
        elif stage == "z2" and line:
            c["z"] = run.send(z([(1, 2), (2, 1)]), c["v"])
        elif stage == "z3" and line:
            c["z"] = run.send(z([(1, 0), (2, 3)]), c["v"])
        elif stage == "a3" and line:
            c["v"] = run.compute(add, c["v"], c["z"])
        elif stage == "a4":
            c["v"] = run.compute(add, c["v"], c["z"]) if line else over_dp(c["v"])
        elif stage == "a5" and line:
            c["v"] = run.compute(lambda *v: pick(*v), c["v"], c["z"])
        elif source == "Q":
            index = "abc".index(name[1])
            if stage == "x":
                c["x"] = run.send(far, env["gQ", 1][index])
            elif stage == "a1":
                c["give"], c["v"] = run.compute(lambda a, b: split_add([a], [b]), env["gQ", 0][index], c["x"])
            elif stage == "y":
                c["y"] = run.send(rep, c["give"])
            elif stage == "a2":
                c["v"] = run.compute(add, c["v"], c["y"])
        elif source == "O":
            if stage == "y":
                c["y"] = run.send(rep, env["O"][0])
            elif stage == "a1":
                c["v"], c["give"] = run.compute(part_add, env["O"][1], c["y"])
            elif stage == "x":
                c["x"] = run.send(far, c["give"])
            elif stage == "a2":
                c["v"] = run.compute(add, c["v"], c["x"])
        elif source == "F":
            j = "ox".index(stage[1]) if stage[0] in "ya" and stage[1] in "ox" else None
            if stage in ("yo", "yx"):
                c[stage] = run.send(rep, env["F", j][0])
            elif stage in ("ao", "ax"):
                c[stage] = run.compute(add, env["F", j][1], c["y" + stage[1]])
            elif stage == "x":
                c["x"] = run.send(far, c["ax"])
            elif stage == "a2":
                c["v"] = run.compute(add, c["ao"], c["x"])

    def done(name, mine, other):
        if name == "F":
            env["down"], env["up"] = run.compute(lambda *v: finish(*v, (False, True)), mine, other)
        elif name == "O":
            env["out"], env["gain1"], env["gain2"] = run.compute(lambda *v: finish_packed(*v), mine, other)
        else:
            env["qkv"] = run.compute(lambda *v: finish_slot(*v, "abc".index(name[1]), 3, env.get("qkv")), mine, other)

    def task(t):
        if t == "prep":
            env["a1"], env["dm"] = run.compute(lambda c, v, g: prep(v, c, g), cot, x, gain1)
        elif t[:3] == "att":
            j = int(t[3])
            env["att", j] = run.compute(attend, env["a1"], w["qkv"][j])
        elif t == "proj":
            env["resid"], env["a2"] = run.compute(lambda *m: project(m, one("out"), x, gain2), *[env["att", j][1] for j in range(4)])
        elif t in ("mlpP", "mlpR"):
            js = (0, 2) if t == "mlpP" else (1, 3)
            hid, dpre, grads = run.compute(lambda a: mlp(a, env["dm"], [w["up"][j][0] for j in js], [w["down"][j][0] for j in js]), env["a2"])
            for i, j in enumerate(js):
                env["hid", j], env["dpre", j], env["gF", j] = hid[i], dpre[i], grads[i]
        elif t[:2] in ("cF", "cQ"):
            (kind, j), i = t[1:3], int(t[-1])
            grads = env["g" + kind, 2 + int(j)]
            env.setdefault(("r" + kind, int(j)), [None] * len(grads))[i] = run.send(core, grads[i])
        elif t in ("aF0", "aF1"):
            j = int(t[2])
            env["F", j] = run.compute(lambda *v: split_add(v[:2], v[2:]), *env["gF", j], *env["rF", j])
        elif t == "mlpback":
            env["dres"], env["datt"], env["part2"] = run.compute(
                lambda *d: mlp_back(d, one("up"), env["resid"], cot, gain2), *[env["dpre", j] for j in range(4)]
            )
        elif t == "mlpout":
            env["output"] = run.compute(lambda *h: mlp_out(h, one("down"), env["resid"]), *[env["hid", j] for j in range(4)])
        elif t == "gout":
            env["gO"] = run.compute(lambda d: grad_out(d, [env["att", j][1] for j in range(4)]), env["datt"])
        elif t[:2] == "cO":
            env.setdefault("rO", [None] * 2)[int(t[-1])] = run.send(core, env["gO"][2 + int(t[-1])])
        elif t == "aO":
            env["O"] = run.compute(lambda *v: pack(*v, env["rO"], env["g"], env["gr"]), *env["gO"][:2])
        elif t[:2] == "ab":
            j = int(t[2])
            got = env["rQ", j] if j < 2 else ()
            env["dqkv", j], env["gQ", j] = run.compute(
                lambda d: attend_back(env["a1"], d, w["out"][j][0], env["att", j][0], env["att", j][2], got), env["datt"]
            )
        elif t == "inback":
            env["gin"], env["g"] = run.compute(
                lambda *d: input_back(d, w["qkv"], x, env["dres"], gain1, env["part2"]), *[env["dqkv", j] for j in range(4)]
            )
        elif t == "g0":
            env["gr"] = run.send(core, env["g"])
        elif t.split("_")[1] in GROUPS:
            gather_task(*t.split("_"))
        else:
            chunk_task(*t.split("_"))

    for t in ORDER:
        task(t)
    return (
        env["output"].reshape(shape),
        env["gin"].reshape(shape),
        env["gain1"].reshape(-1),
        env["qkv"],
        env["out"],
        env["gain2"].reshape(-1),
        env["up"],
        env["down"],
    )


def solution(mesh):
    return jax.shard_map(
        functools.partial(per_device, dict(mesh.shape)),
        mesh=mesh,
        in_specs=(
            P(("rep", "mp"), "dp", None, None),
            P(),
            P(None, None, "mp"),
            P("mp", None),
            P(),
            P(None, "mp"),
            P("mp", None),
            P(("rep", "mp"), "dp", None, None),
        ),
        out_specs=(
            P(("rep", "mp"), "dp", None, None),
            P(("rep", "mp"), "dp", None, None),
            P(),
            P(None, None, "mp"),
            P("mp", None),
            P(),
            P(None, "mp"),
            P("mp", None),
        ),
        check_vma=False,
    )
```

```python
import functools

import jax
import jax.numpy as jnp
from jax import lax
from jax.experimental import pallas as pl
from jax.experimental.pallas import tpu as pltpu
from jax.sharding import PartitionSpec as P

HEAD_DIM = 128
PROJ_BLOCK = 256
GRAD_BLOCK = 512
EPS = 1e-05
LOG2E = 1.4426950408889634
GELU_A = 0.7978845608028654
GELU_B = 0.044715
f32 = jnp.float32
bf16 = jnp.bfloat16

NN = (((1,), (0,)), ((), ()))
NT = (((1,), (1,)), ((), ()))
TN = (((0,), (0,)), ((), ()))


def dot(a, b, dims=NN):
    return lax.dot_general(a, b, dims, preferred_element_type=f32)


def normed(v):
    mean = jnp.mean(v, axis=-1, keepdims=True)
    centred = v - mean
    r = lax.rsqrt(jnp.mean(centred * centred, axis=-1, keepdims=True) + EPS)
    return centred * r, r


def fold(v):
    return jnp.sum(v.reshape(-1, 8, v.shape[-1]), axis=0)


def params(mib=8):
    return pltpu.CompilerParams(vmem_limit_bytes=mib * 2**20)


def cost():
    return pl.CostEstimate(flops=1, bytes_accessed=1, transcendentals=0)


def whole(n):
    return [pl.BlockSpec(memory_space=pltpu.VMEM)] * n


def sds(shape, dtype):
    return jax.ShapeDtypeStruct(shape, dtype)


def by_rows(length, step, init=None, block=512):
    if block >= length:
        return step(slice(None), init)
    return lax.fori_loop(0, length // block, lambda i, c: step(span(i, block), c), init)


def span(i, size):
    if isinstance(i, int):
        return slice(i * size, (i + 1) * size)
    return pl.ds(pl.multiple_of(i * size, size), size)


def loop(n, step):
    lax.fori_loop(0, n, lambda i, _: step(i), None)


def unrolled(n, step):
    for i in range(n):
        step(i)


def places():
    rep, dp = lax.axis_index("rep"), lax.axis_index("dp")
    near = lax.rem(dp, 2)
    outer = jnp.where((dp == 0) | (dp == lax.axis_size("dp") - 1), 1, 0)
    quarters = [2 * r + n for r, n in ((rep, near), (1 - rep, near), (rep, 1 - near), (1 - rep, 1 - near))]
    return rep, 1 - rep, 2 + near, 3 - near, outer, *quarters


def placed_kernel(kernel, *refs):
    kernel(places(), *refs)


def call(kernel, ins, outs, name, mib=8, at=False, scratch=()):
    if at:
        kernel = functools.partial(placed_kernel, kernel)
    return pl.pallas_call(
        kernel,
        in_specs=whole(len(ins)),
        out_specs=whole(len(outs)),
        out_shape=list(outs),
        scratch_shapes=list(scratch),
        compiler_params=params(mib),
        cost_estimate=cost(),
        name=name,
    )(*ins)


def matrices(refs):
    return (lambda c: refs[0][c]) if len(refs) == 1 else (lambda c: refs[c][...])


def prep_kernel(x_ref, c_ref, g_ref, a_ref, d_ref):
    def step(rows, _):
        a_ref[rows, :] = (normed(x_ref[rows, :])[0] * g_ref[...]).astype(bf16)
        d_ref[rows, :] = c_ref[rows, :].astype(bf16)

    by_rows(x_ref.shape[0], step)


def prep(x, cot, gain):
    return call(prep_kernel, (x, cot, gain), (sds(x.shape, bf16),) * 2, "prep")


def attend_kernel(n, a_ref, *refs):
    w, (qkv_ref, mixed_ref, lse_ref) = matrices(refs[:n]), refs[n:]
    scale = HEAD_DIM**-0.5 * LOG2E

    def project_rows(rows, _):
        for c in range(3):
            qkv_ref[c, rows, :] = dot(a_ref[rows, :], w(c)).astype(bf16)

    def head(h):
        cols = span(h, HEAD_DIM)
        q, k, v = (qkv_ref[c, :, cols] for c in range(3))
        scores = dot(k, q, NT)
        top = jnp.max(scores, axis=0, keepdims=True)
        expd = jnp.exp2((scores - top) * scale)
        total = jnp.sum(expd, axis=0, keepdims=True)
        mixed = dot(v, expd.astype(bf16), TN) / total
        mixed_ref[:, cols] = mixed.T.astype(bf16)
        lse_ref[pl.ds(h, 1), :] = top * scale + jnp.log2(total)

    by_rows(a_ref.shape[0], project_rows, None, PROJ_BLOCK)
    loop(qkv_ref.shape[2] // HEAD_DIM, head)


def attend(a, w):
    length, local = a.shape[0], w[0].shape[-1]
    outs = (sds((3, length, local), bf16), sds((length, local), bf16), sds((local // HEAD_DIM, length), f32))
    return call(functools.partial(attend_kernel, len(w)), (a, *w), outs, "attend", 12)


def project_kernel(n, *refs):
    mixed, w = refs[:n], refs[n : 2 * n]
    x_ref, g_ref, resid_ref, a_ref = refs[2 * n :]

    def step(rows, _):
        total = dot(mixed[0][rows, :], w[0][...])
        for j in range(1, n):
            total += dot(mixed[j][rows, :], w[j][...])
        resid = x_ref[rows, :] + total
        resid_ref[rows, :] = resid
        a_ref[rows, :] = (normed(resid)[0] * g_ref[...]).astype(bf16)

    by_rows(x_ref.shape[0], step)


def project(mixed, w, x, gain):
    outs = (sds(x.shape, f32), sds(x.shape, bf16))
    return call(functools.partial(project_kernel, len(mixed)), (*mixed, *w, x, gain), outs, "project")


def mlp_kernel(n, *refs):
    a_ref, d_ref = refs[:2]
    up, down = refs[2 : 2 + n], refs[2 + n : 2 + 2 * n]
    outs = refs[2 + 2 * n :]
    hid, dpre, grads = outs[:n], outs[n : 2 * n], outs[2 * n :]
    for j in range(n):
        u = dot(a_ref[...], up[j][...])
        d_hidden = dot(d_ref[...], down[j][...], NT)
        sq = u * u
        t = jnp.tanh(GELU_A * u * (1.0 + GELU_B * sq))
        half = 0.5 * (1.0 + t)
        hidden = (u * half).astype(bf16)
        slope = half + 0.5 * u * (1.0 - t * t) * (GELU_A * (1.0 + 3.0 * GELU_B * sq))
        d_pre = (d_hidden * slope).astype(bf16)
        hid[j][...] = hidden
        dpre[j][...] = d_pre
        grads[2 * j][...] = dot(hidden, d_ref[...], TN).astype(bf16)
        grads[2 * j + 1][...] = dot(d_pre, a_ref[...], TN).astype(bf16)


def mlp(a, d, up, down):
    n = len(up)
    length, width = a.shape
    local = up[0].shape[1]
    act, grad = sds((length, local), bf16), sds((local, width), bf16)
    outs = call(functools.partial(mlp_kernel, n), (a, d, *up, *down), (act,) * (2 * n) + (grad,) * (2 * n), "mlp", 12)
    return outs[:n], outs[n : 2 * n], [outs[2 * n + 2 * j : 2 * n + 2 * j + 2] for j in range(n)]


def norm_back(d_a, v, gain):
    xhat, r = normed(v)
    e = d_a * gain
    back = r * (e - jnp.mean(e, axis=-1, keepdims=True) - xhat * jnp.mean(e * xhat, axis=-1, keepdims=True))
    return back, fold(d_a * xhat)


def mlp_back_kernel(n, *refs):
    d_pre, up = refs[:n], refs[n : 2 * n]
    resid_ref, c_ref, g_ref, dres_ref, datt_ref, gain_ref = refs[2 * n :]

    def step(rows, gain):
        total = dot(d_pre[0][rows, :], up[0][...], NT)
        for j in range(1, n):
            total += dot(d_pre[j][rows, :], up[j][...], NT)
        back, part = norm_back(total, resid_ref[rows, :], g_ref[...])
        d_resid = c_ref[rows, :] + back
        dres_ref[rows, :] = d_resid
        datt_ref[rows, :] = d_resid.astype(bf16)
        return gain + part

    gain_ref[...] = by_rows(c_ref.shape[0], step, jnp.zeros(gain_ref.shape, f32), 256)


def mlp_back(d_pre, up, resid, cot, gain):
    n = len(up)
    outs = (sds(resid.shape, f32), sds(resid.shape, bf16), sds((8, resid.shape[1]), f32))
    return call(functools.partial(mlp_back_kernel, n), (*d_pre, *up, resid, cot, gain), outs, "mlp_back")


def mlp_out_kernel(n, *refs):
    hid, down = refs[:n], refs[n : 2 * n]
    resid_ref, out_ref = refs[2 * n :]

    def step(rows, _):
        total = resid_ref[rows, :]
        for j in range(n):
            total += dot(hid[j][rows, :], down[j][...])
        out_ref[rows, :] = total

    by_rows(resid_ref.shape[0], step)


def mlp_out(hid, down, resid):
    n = len(down)
    return call(functools.partial(mlp_out_kernel, n), (*hid, *down, resid), (sds(resid.shape, f32),), "mlp_out")[0]


def grad_out_kernel(n, d_ref, *refs):
    for mixed, out in zip(refs[:n], refs[n:], strict=True):
        out[...] = dot(mixed[...], d_ref[...], TN).astype(bf16)


def grad_out(d, mixed):
    n = len(mixed)
    outs = (sds((mixed[0].shape[1], d.shape[1]), bf16),) * n
    return call(functools.partial(grad_out_kernel, n), (d, *mixed), outs, "grad_out")


def attend_back_kernel(added, a_ref, d_ref, w_ref, qkv_ref, lse_ref, *refs):
    scale = HEAD_DIM**-0.5
    got, dqkv_ref, grads, dm_ref = refs[:added], refs[added], refs[added + 1 : -1], refs[-1]
    dm_ref[...] = dot(d_ref[...], w_ref[...], NT).astype(bf16)

    def head(h):
        cols = span(h, HEAD_DIM)
        q, k, v = (qkv_ref[c, :, cols] for c in range(3))
        dm = dm_ref[:, cols]
        probs = jnp.exp2(dot(k, q, NT) * (scale * LOG2E) - lse_ref[pl.ds(h, 1), :])
        d_probs = dot(v, dm, NT)
        dqkv_ref[2, :, cols] = dot(probs.astype(bf16), dm).astype(bf16)
        delta = jnp.sum(d_probs * probs, axis=0, keepdims=True)
        d_scores = (probs * (d_probs - delta)).astype(bf16)
        dqkv_ref[1, :, cols] = (dot(d_scores, q) * scale).astype(bf16)
        dqkv_ref[0, :, cols] = (dot(k, d_scores, TN) * scale).T.astype(bf16)

    unrolled(w_ref.shape[0] // HEAD_DIM, head)
    size = GRAD_BLOCK

    def grad_cols(i):
        cols = span(i, size)
        for c in range(3):
            grad = dot(dqkv_ref[c], a_ref[:, cols], TN)
            grads[c][:, cols] = (grad + got[c][:, cols].astype(f32) if added else grad).astype(bf16)

    loop(a_ref.shape[1] // size, grad_cols)


def attend_back(a, d, w, qkv, lse, got=()):
    length, width = a.shape
    local = w.shape[0]
    outs = (sds((3, length, local), bf16), *[sds((local, width), bf16)] * 3)
    outs = call(functools.partial(attend_back_kernel, len(got)), (a, d, w, qkv, lse, *got), outs, "attend_back", 12, False, [pltpu.VMEM((length, local), bf16)])
    return outs[0], outs[1:]


def join_kernel(axes, at_ref, *refs):
    quarters, outs = refs[:4], refs[4:]
    width = quarters[0].shape[1]
    for p, quarter in enumerate(quarters):
        place = pl.ds(pl.multiple_of(at_ref[p] * width, width), width)
        for i, (out, axis) in enumerate(zip(outs, axes, strict=True)):
            if axis == 0:
                out[place, :] = quarter[i]
            else:
                out[:, place] = quarter[i]


def join(quarters, likes, axes):
    flat = [(v.shape[-2:], 0 if axis == 3 else axis) for v, axis in zip(likes, axes, strict=True) for _ in range(v.size // (v.shape[-1] * v.shape[-2]))]
    outs = [sds(shape, bf16) for shape, _ in flat]
    return call(functools.partial(join_kernel, tuple(axis for _, axis in flat)), quarters, outs, "join", 4, True)


def cut_kernel(axes, at_ref, *refs):
    n = len(axes)
    for out, p in zip(refs[n:], (0, 2), strict=True):
        size = out.shape[1]
        place = pl.ds(pl.multiple_of(at_ref[p] * size, size), size)
        i = 0
        for v, axis in zip(refs[:n], axes, strict=True):
            if axis == 3:
                for c in range(3):
                    out[i + c] = v[c, place, :]
                i += 3
            else:
                out[i] = v[place, :] if axis == 0 else v[:, place]
                i += 1


def cut(arrays, axes):
    size = max(arrays[0].shape) // 4
    outs = (sds((sum(v.size for v in arrays) // (4 * size * size), size, size), bf16),) * 2
    return call(functools.partial(cut_kernel, tuple(axes)), arrays, outs, "cut", 4, True)


def cut_one_kernel(at_ref, w_ref, out_ref):
    size = out_ref.shape[1]
    out_ref[...] = w_ref[:, span(at_ref[5], size), :]


def cut_one(w):
    n, width, local = w.shape
    return call(cut_one_kernel, (w,), (sds((n, width // 4, local), bf16),), "cut", 4, True)[0]


def middle_kernel(y_ref, z_ref, a_ref, b_ref):
    rows = a_ref.shape[1]
    a_ref[...] = z_ref[:, 0:rows, :]
    b_ref[...] = y_ref[:, rows : 2 * rows, :]


def middle(y, z):
    n, rows, local = y.shape
    return call(middle_kernel, (y, z), (sds((n, rows // 2, local), bf16),) * 2, "middle", 4)


def join_four_kernel(at_ref, own_ref, y_ref, z_ref, a_ref, b_ref, *outs):
    size = own_ref.shape[1]
    for i, out in enumerate(outs):
        out[span(at_ref[5], size), :] = own_ref[i]
        out[span(at_ref[6], size), :] = y_ref[i]
        out[span(at_ref[7], size), :] = z_ref[i]
        out[span(at_ref[8] * 2, size // 2), :] = a_ref[i]
        out[span(at_ref[8] * 2 + 1, size // 2), :] = b_ref[i]


def join_four(own, y, z, a, b):
    n, rows, local = own.shape
    return call(join_four_kernel, (own, y, z, a, b), (sds((4 * rows, local), bf16),) * n, "join", 4, True)


def half_of(ref, at, rows):
    place = pl.ds(pl.multiple_of(at * rows, rows), rows)
    return ref[place, :] if len(ref.shape) == 2 else ref[:, place, :]


def add_kernel(a_ref, b_ref, o_ref):
    o_ref[...] = a_ref[...] + b_ref[...]


def add(a, b):
    return call(add_kernel, (a, b), (sds(a.shape, a.dtype),), "add", 4)[0]


def halved(shape, n=None):
    half = (shape[-2] // 2, shape[-1])
    return sds(half if n is None else (n, *half), bf16)


def split_add_kernel(n, at_ref, *refs):
    a, b, (give_ref, keep_ref) = refs[:n], refs[n : 2 * n], refs[2 * n :]
    rows = give_ref.shape[-2]
    for at, out in ((1 - at_ref[0], give_ref), (at_ref[0], keep_ref)):
        for i in range(n):
            total = half_of(a[i], at, rows) + half_of(b[i], at, rows)
            if len(out.shape) == 2:
                out[...] = total
            else:
                out[i] = total


def split_add(a, b):
    n = len(a)
    outs = (halved(a[0].shape, None if n == 1 else n),) * 2
    return call(functools.partial(split_add_kernel, n), (*a, *b), outs, "split_add", 4, True)


EXTRA = 16


def pack_kernel(at_ref, *refs):
    gains, got_gains, give_ref, keep_ref = refs[4:]
    rows = give_ref.shape[1] - EXTRA
    total = (gains[...] + got_gains[...]).astype(bf16)
    extra = jnp.concatenate([total, jnp.zeros((EXTRA - total.shape[0], total.shape[1]), bf16)])
    for at, out in ((1 - at_ref[0], give_ref), (at_ref[0], keep_ref)):
        for i in range(2):
            out[i, 0:rows, :] = half_of(refs[i], at, rows) + half_of(refs[2 + i], at, rows)
            out[i, rows : rows + EXTRA, :] = extra


def pack(kept, sent, got, gains, got_gains):
    rows, width = kept.shape
    outs = (sds((2, rows // 2 + EXTRA, width), bf16),) * 2
    return call(pack_kernel, (kept, sent, *got, gains, got_gains), outs, "pack", 4, True)


def part_add_kernel(a_ref, b_ref, *outs):
    for i, out in enumerate(outs):
        out[...] = a_ref[i] + b_ref[i]


def part_add(a, b):
    return call(part_add_kernel, (a, b), [sds(a.shape[1:], bf16)] * a.shape[0], "add", 4)


def finish_packed_kernel(at_ref, mine_ref, other_ref, out_ref, gain1_ref, gain2_ref):
    rows = out_ref.shape[0] // 2
    for at, ref in ((at_ref[0], mine_ref), (1 - at_ref[0], other_ref)):
        out_ref[pl.ds(pl.multiple_of(at * rows, rows), rows), :] = ref[0:rows, :].astype(f32)
    gains = mine_ref[rows : rows + EXTRA, :].astype(f32)
    gain1_ref[...] = gains[0:1, :]
    gain2_ref[...] = gains[1:2, :]


def finish_packed(mine, other):
    rows, width = 2 * (mine.shape[0] - EXTRA), mine.shape[1]
    outs = (sds((rows, width), f32), sds((1, width), f32), sds((1, width), f32))
    return call(finish_packed_kernel, (mine, other), outs, "finish", 6, True)


def pick_kernel(at_ref, a_ref, b_ref, o_ref):
    @pl.when(at_ref[4] == 1)
    def _():
        o_ref[...] = b_ref[...]

    @pl.when(at_ref[4] == 0)
    def _():
        o_ref[...] = a_ref[...]


def pick(a, b):
    return call(pick_kernel, (a, b), (sds(a.shape, a.dtype),), "pick", 4, True)[0]


def placed(ref, at, index=None):
    rows = ref.shape[-2]
    return pl.ds(pl.multiple_of(at * rows, rows), rows), (ref[...] if index is None else ref[index]).astype(f32)


def finish_kernel(turned, at_ref, mine_ref, other_ref, *outs):
    for at, ref in ((at_ref[0], mine_ref), (1 - at_ref[0], other_ref)):
        for i, (out, turn) in enumerate(zip(outs, turned, strict=True)):
            place, v = placed(ref, at, i if len(turned) > 1 else None)
            if turn:
                out[:, place] = v.T
            else:
                out[place, :] = v


def finish(mine, other, turned):
    rows, width = 2 * mine.shape[-2], mine.shape[-1]
    outs = [sds((width, rows) if turn else (rows, width), f32) for turn in turned]
    return call(functools.partial(finish_kernel, turned), (mine, other), outs, "finish", 6, True)


def finish_slot_kernel(at_ref, mine_ref, other_ref, *refs):
    for at, ref in ((at_ref[0], mine_ref), (1 - at_ref[0], other_ref)):
        place, v = placed(ref, at)
        refs[-1][0, :, place] = v.T


def finish_slot(mine, other, slot, slots, into):
    rows, width = mine.shape
    spec = pl.BlockSpec(memory_space=pltpu.VMEM)
    return pl.pallas_call(
        functools.partial(placed_kernel, finish_slot_kernel),
        grid=(1,),
        in_specs=[spec, spec] + [pl.BlockSpec(memory_space=pl.ANY)] * (into is not None),
        out_specs=pl.BlockSpec((1, width, 2 * rows), lambda i: (slot, 0, 0)),
        out_shape=sds((slots, width, 2 * rows), f32),
        input_output_aliases={} if into is None else {2: 0},
        compiler_params=params(6),
        cost_estimate=cost(),
        name="finish",
    )(mine, other, *([] if into is None else [into]))


def input_back_kernel(n, counts, *refs):
    d_qkv, refs = refs[:n], refs[n:]
    w = []
    for count in counts:
        w.append(matrices(refs[:count]))
        refs = refs[count:]
    x_ref, dres_ref, g_ref, other_ref, out_ref, gains_ref = refs

    def step(rows, gain):
        total = None
        for j in range(n):
            for c in range(3):
                part = dot(d_qkv[j][c, rows, :], w[j](c), NT)
                total = part if total is None else total + part
        back, part = norm_back(total, x_ref[rows, :], g_ref[...])
        out_ref[rows, :] = dres_ref[rows, :] + back
        return gain + part

    gain = by_rows(x_ref.shape[0], step, jnp.zeros(other_ref.shape, f32), 256)
    gains_ref[0:1, :] = jnp.sum(gain, axis=0, keepdims=True)
    gains_ref[1:2, :] = jnp.sum(other_ref[...], axis=0, keepdims=True)


def input_back(d_qkv, w, x, d_resid, gain, other):
    outs = (sds(x.shape, f32), sds((2, x.shape[1]), f32))
    kernel = functools.partial(input_back_kernel, len(w), tuple(len(v) for v in w))
    return call(kernel, (*d_qkv, *[m for v in w for m in v], x, d_resid, gain, other), outs, "input_back", 12)


def swap(axis, size, bit):
    pairs = [(i, i ^ bit) for i in range(size)]
    return lambda v: lax.ppermute(v, axis, pairs)


def bits_of(size):
    return [1 << b for b in reversed(range(size.bit_length() - 1))]


class Run:
    def __init__(self):
        self.token = None

    def tie(self, v):
        if self.token is None:
            return v
        return lax.optimization_barrier((v, self.token))[0]

    def compute(self, step, first, *rest):
        outs = step(self.tie(first), *rest)
        self.token = jax.tree.leaves(outs)[0]
        return outs

    def send(self, move, v):
        v = self.tie(v)
        self.token = v
        return move(v)


class Names:
    def __getattr__(self, name):
        return name


N = Names()
ORDER = (
    N.c0_q, N.sl_q, N.xp_q, N.sl_d, N.sl_ou, N.prep, N.c0_ou_0, N.xp_d, N.xr_d, N.att0, N.xp_ou, N.y_q, N.z_q,
    N.y_ou, N.xr_ou, N.att2, N.sm_q, N.zz_q, N.yy_q, N.z_ou, N.z_d, N.as_q, N.cx_q_1, N.c0_d, N.att1, N.y_d,
    N.cx_q_0, N.c0_ou_1, N.as_ou, N.as_d, N.cx_ou_0, N.cx_ou_1, N.cx_d, N.cx_q_2, N.att3, N.proj, N.mlpR,
    N.cF1_1, N.cF1_0, N.mlpP, N.cF0_0, N.cF0_1, N.aF1, N.F_yx, N.mlpback, N.ab3, N.cQ1_1, N.cQ1_0, N.aF0, N.F_yo,
    N.cQ1_2, N.F_ax, N.F_x, N.ab2, N.ab1, N.cQ0_0, N.cQ0_2, N.gout, N.cO_1, N.cQ0_1, N.cO_0, N.Qa_x, N.F_ao,
    N.F_a2, N.F_z1, N.Qb_x, N.ab0, N.inback, N.g0, N.Qa_a1, N.Qa_y, N.F_a3, N.aO, N.F_z2, N.O_y, N.Qa_a2,
    N.Qa_z1, N.Qb_a1, N.Qc_x, N.F_a4, N.F_z3, N.Qb_y, N.O_a1, N.Qa_a3, N.Qc_a1, N.Qc_y, N.Qa_z2, N.O_x, N.Qb_a2,
    N.Qb_z1, N.F_a5, N.F_w, N.O_a2, N.O_z1, N.Qa_a4, N.Qa_z3, N.Qb_a3, N.Qb_z2, N.Qc_a2, N.Qc_z1, N.O_a3, N.O_z2,
    N.Qa_a5, N.Qa_w, N.Qb_a4, N.Qb_z3, N.Qc_a3, N.Qc_z2, N.F_f, N.O_a4, N.O_z3, N.Qb_a5, N.Qa_f, N.Qb_w, N.Qc_a4,
    N.Qc_z3, N.O_a5, N.O_w, N.Qb_f, N.mlpout, N.Qc_a5, N.Qc_w, N.O_f, N.Qc_f,
)
GROUPS = {"q": ("qkv",), "ou": ("out", "up"), "d": ("down",)}
FOUR = ("q",)
CHUNKS = {"F": "F", "O": "O", "Qa": "Q", "Qb": "Q", "Qc": "Q"}
AXES = {"qkv": 3, "out": 1, "up": 0, "down": 1}


def per_device(
    sizes,
    inputs,
    norm1_gain,
    weight_qkv,
    weight_out,
    norm2_gain,
    weight_up,
    weight_down,
    cotangent,
):
    n_rep, n_dp, n_mp = sizes["rep"], sizes["dp"], sizes["mp"]
    if n_mp != 4 or n_rep != 2 or n_dp & (n_dp - 1) or n_dp < 2:
        raise ValueError("unsupported mesh")
    shape = inputs.shape
    x = inputs.reshape(shape[-2:])
    cot = cotangent.reshape(shape[-2:])
    gain1, gain2 = norm1_gain.reshape(1, -1), norm2_gain.reshape(1, -1)
    width = x.shape[1]
    run = Run()
    line = n_dp == 4

    core = swap("mp", n_mp, 1)
    far = swap("mp", n_mp, 2)
    rep = swap("rep", n_rep, 1)
    near = swap("dp", n_dp, 1)
    own = {"qkv": weight_qkv, "out": weight_out, "up": weight_up, "down": weight_down}
    w = {k: [[v], None, None, None] for k, v in own.items()}
    env = {}

    def gather_task(kind, g, i="0"):
        names = GROUPS[g]
        if kind == "c0":
            k = names[int(i)]
            w[k][2] = [run.send(core, own[k])]
        elif kind == "x":
            for k in names:
                w[k][1] = [run.send(far, own[k])]
        elif g in FOUR and kind == "sl":
            env["p", g] = run.compute(cut_one, own[names[0]])
        elif g in FOUR and kind == "z":
            env["pz", g] = run.send(near, env["px", g])
        elif g in FOUR and kind == "sm":
            env["a", g], env["b", g] = run.compute(middle, env["py", g], env["pz", g])
        elif kind == "yy":
            env["ya", g] = run.send(rep, env["a", g])
        elif kind == "zz":
            env["zb", g] = run.send(near, env["b", g])
        elif g in FOUR and kind == "as":
            w[names[0]][1] = run.compute(join_four, env["px", g], env["py", g], env["pz", g], env["ya", g], env["zb", g])
        elif kind == "sl":
            env["p", g], env["r", g] = run.compute(lambda *v: cut(v, [AXES[k] for k in names]), *[own[k] for k in names])
        elif kind == "xp":
            env["px", g] = run.send(far, env["p", g])
        elif kind == "xr":
            env["rx", g] = run.send(far, env["r", g])
        elif kind == "y":
            env["py", g] = run.send(rep, env["px", g])
        elif kind == "z":
            env["rz", g] = run.send(near, env["rx", g])
        elif kind == "as":
            outs = run.compute(
                lambda *v: join(v, [own[k] for k in names], [AXES[k] for k in names]),
                env["px", g], env["py", g], env["rx", g], env["rz", g],
            )
            for k in names:
                n = 3 if AXES[k] == 3 else 1
                w[k][1], outs = outs[:n], outs[n:]
        elif kind == "cx":
            k, m = [(k, m) for k in names for m in range(len(w[k][1]))][int(i)]
            w[k][3] = w[k][3] or [None] * len(w[k][1])
            w[k][3][m] = run.send(core, w[k][1][m])

    def one(k):
        return [v[0] for v in w[k]]

    def over_dp(v):
        for bit in bits_of(n_dp):
            v = run.compute(add, v, run.send(swap("dp", n_dp, bit), v))
        return v

    def chunk_task(name, stage):
        source = CHUNKS[name]
        c = env.setdefault(("chunk", name), {})

        def z(pairs):
            return lambda v: lax.ppermute(v, "dp", pairs)

        if stage == "f":
            done(name, c["v"], c["w"])
        elif stage == "w":
            c["w"] = run.send(rep, c["v"])
        elif stage == "z1" and line:
            c["z"] = run.send(z([(0, 1), (3, 2)]), c["v"])
        elif stage == "z2" and line:
            c["z"] = run.send(z([(1, 2), (2, 1)]), c["v"])
        elif stage == "z3" and line:
            c["z"] = run.send(z([(1, 0), (2, 3)]), c["v"])
        elif stage == "a3" and line:
            c["v"] = run.compute(add, c["v"], c["z"])
        elif stage == "a4":
            c["v"] = run.compute(add, c["v"], c["z"]) if line else over_dp(c["v"])
        elif stage == "a5" and line:
            c["v"] = run.compute(lambda *v: pick(*v), c["v"], c["z"])
        elif source == "Q":
            index = "abc".index(name[1])
            if stage == "x":
                c["x"] = run.send(far, env["gQ", 1][index])
            elif stage == "a1":
                c["give"], c["v"] = run.compute(lambda a, b: split_add([a], [b]), env["gQ", 0][index], c["x"])
            elif stage == "y":
                c["y"] = run.send(rep, c["give"])
            elif stage == "a2":
                c["v"] = run.compute(add, c["v"], c["y"])
        elif source == "O":
            if stage == "y":
                c["y"] = run.send(rep, env["O"][0])
            elif stage == "a1":
                c["v"], c["give"] = run.compute(part_add, env["O"][1], c["y"])
            elif stage == "x":
                c["x"] = run.send(far, c["give"])
            elif stage == "a2":
                c["v"] = run.compute(add, c["v"], c["x"])
        elif source == "F":
            j = "ox".index(stage[1]) if stage[0] in "ya" and stage[1] in "ox" else None
            if stage in ("yo", "yx"):
                c[stage] = run.send(rep, env["F", j][0])
            elif stage in ("ao", "ax"):
                c[stage] = run.compute(add, env["F", j][1], c["y" + stage[1]])
            elif stage == "x":
                c["x"] = run.send(far, c["ax"])
            elif stage == "a2":
                c["v"] = run.compute(add, c["ao"], c["x"])

    def done(name, mine, other):
        if name == "F":
            env["down"], env["up"] = run.compute(lambda *v: finish(*v, (False, True)), mine, other)
        elif name == "O":
            env["out"], env["gain1"], env["gain2"] = run.compute(lambda *v: finish_packed(*v), mine, other)
        else:
            env["qkv"] = run.compute(lambda *v: finish_slot(*v, "abc".index(name[1]), 3, env.get("qkv")), mine, other)

    def task(t):
        if t == "prep":
            env["a1"], env["dm"] = run.compute(lambda c, v, g: prep(v, c, g), cot, x, gain1)
        elif t[:3] == "att":
            j = int(t[3])
            env["att", j] = run.compute(attend, env["a1"], w["qkv"][j])
        elif t == "proj":
            env["resid"], env["a2"] = run.compute(lambda *m: project(m, one("out"), x, gain2), *[env["att", j][1] for j in range(4)])
        elif t in ("mlpP", "mlpR"):
            js = (0, 2) if t == "mlpP" else (1, 3)
            hid, dpre, grads = run.compute(lambda a: mlp(a, env["dm"], [w["up"][j][0] for j in js], [w["down"][j][0] for j in js]), env["a2"])
            for i, j in enumerate(js):
                env["hid", j], env["dpre", j], env["gF", j] = hid[i], dpre[i], grads[i]
        elif t[:2] in ("cF", "cQ"):
            (kind, j), i = t[1:3], int(t[-1])
            grads = env["g" + kind, 2 + int(j)]
            env.setdefault(("r" + kind, int(j)), [None] * len(grads))[i] = run.send(core, grads[i])
        elif t in ("aF0", "aF1"):
            j = int(t[2])
            env["F", j] = run.compute(lambda *v: split_add(v[:2], v[2:]), *env["gF", j], *env["rF", j])
        elif t == "mlpback":
            env["dres"], env["datt"], env["part2"] = run.compute(
                lambda *d: mlp_back(d, one("up"), env["resid"], cot, gain2), *[env["dpre", j] for j in range(4)]
            )
        elif t == "mlpout":
            env["output"] = run.compute(lambda *h: mlp_out(h, one("down"), env["resid"]), *[env["hid", j] for j in range(4)])
        elif t == "gout":
            env["gO"] = run.compute(lambda d: grad_out(d, [env["att", j][1] for j in range(4)]), env["datt"])
        elif t[:2] == "cO":
            env.setdefault("rO", [None] * 2)[int(t[-1])] = run.send(core, env["gO"][2 + int(t[-1])])
        elif t == "aO":
            env["O"] = run.compute(lambda *v: pack(*v, env["rO"], env["g"], env["gr"]), *env["gO"][:2])
        elif t[:2] == "ab":
            j = int(t[2])
            got = env["rQ", j] if j < 2 else ()
            env["dqkv", j], env["gQ", j] = run.compute(
                lambda d: attend_back(env["a1"], d, w["out"][j][0], env["att", j][0], env["att", j][2], got), env["datt"]
            )
        elif t == "inback":
            env["gin"], env["g"] = run.compute(
                lambda *d: input_back(d, w["qkv"], x, env["dres"], gain1, env["part2"]), *[env["dqkv", j] for j in range(4)]
            )
        elif t == "g0":
            env["gr"] = run.send(core, env["g"])
        elif t.split("_")[1] in GROUPS:
            gather_task(*t.split("_"))
        else:
            chunk_task(*t.split("_"))

    for t in ORDER:
        task(t)
    return (
        env["output"].reshape(shape),
        env["gin"].reshape(shape),
        env["gain1"].reshape(-1),
        env["qkv"],
        env["out"],
        env["gain2"].reshape(-1),
        env["up"],
        env["down"],
    )


def solution(mesh):
    return jax.shard_map(
        functools.partial(per_device, dict(mesh.shape)),
        mesh=mesh,
        in_specs=(
            P(("rep", "mp"), "dp", None, None),
            P(),
            P(None, None, "mp"),
            P("mp", None),
            P(),
            P(None, "mp"),
            P("mp", None),
            P(("rep", "mp"), "dp", None, None),
        ),
        out_specs=(
            P(("rep", "mp"), "dp", None, None),
            P(("rep", "mp"), "dp", None, None),
            P(),
            P(None, None, "mp"),
            P("mp", None),
            P(),
            P(None, "mp"),
            P("mp", None),
        ),
        check_vma=False,
    )
```

```python
import functools

import jax
import jax.numpy as jnp
from jax import lax
from jax.experimental import pallas as pl
from jax.experimental.pallas import tpu as pltpu
from jax.sharding import PartitionSpec as P

HEAD_DIM = 128
PROJ_BLOCK = 512
GRAD_BLOCK = 512
EPS = 1e-05
LOG2E = 1.4426950408889634
GELU_A = 0.7978845608028654
GELU_B = 0.044715
f32 = jnp.float32
bf16 = jnp.bfloat16

NN = (((1,), (0,)), ((), ()))
NT = (((1,), (1,)), ((), ()))
TN = (((0,), (0,)), ((), ()))


def dot(a, b, dims=NN):
    return lax.dot_general(a, b, dims, preferred_element_type=f32)


def normed(v):
    mean = jnp.mean(v, axis=-1, keepdims=True)
    centred = v - mean
    r = lax.rsqrt(jnp.mean(centred * centred, axis=-1, keepdims=True) + EPS)
    return centred * r, r


def fold(v):
    return jnp.sum(v.reshape(-1, 8, v.shape[-1]), axis=0)


def params(mib=8):
    return pltpu.CompilerParams(vmem_limit_bytes=mib * 2**20)


def cost():
    return pl.CostEstimate(flops=1, bytes_accessed=1, transcendentals=0)


def whole(n):
    return [pl.BlockSpec(memory_space=pltpu.VMEM)] * n


def sds(shape, dtype):
    return jax.ShapeDtypeStruct(shape, dtype)


def by_rows(length, step, init=None, block=256):
    if block >= length:
        return step(slice(None), init)
    return lax.fori_loop(0, length // block, lambda i, c: step(span(i, block), c), init)


def span(i, size):
    if isinstance(i, int):
        return slice(i * size, (i + 1) * size)
    return pl.ds(pl.multiple_of(i * size, size), size)


def loop(n, step):
    lax.fori_loop(0, n, lambda i, _: step(i), None)


def unrolled(n, step):
    for i in range(n):
        step(i)


def places():
    rep, dp = lax.axis_index("rep"), lax.axis_index("dp")
    near = lax.rem(dp, 2)
    outer = jnp.where((dp == 0) | (dp == lax.axis_size("dp") - 1), 1, 0)
    quarters = [2 * r + n for r, n in ((rep, near), (1 - rep, near), (rep, 1 - near), (1 - rep, 1 - near))]
    return rep, 1 - rep, 2 + near, 3 - near, outer, *quarters


def placed_kernel(kernel, *refs):
    kernel(places(), *refs)


def call(kernel, ins, outs, name, mib=8, at=False, scratch=()):
    if at:
        kernel = functools.partial(placed_kernel, kernel)
    return pl.pallas_call(
        kernel,
        in_specs=whole(len(ins)),
        out_specs=whole(len(outs)),
        out_shape=list(outs),
        scratch_shapes=list(scratch),
        compiler_params=params(mib),
        cost_estimate=cost(),
        name=name,
    )(*ins)


def matrices(refs):
    return (lambda c: refs[0][c]) if len(refs) == 1 else (lambda c: refs[c][...])


def prep_kernel(x_ref, c_ref, g_ref, a_ref, d_ref):
    def step(rows, _):
        a_ref[rows, :] = (normed(x_ref[rows, :])[0] * g_ref[...]).astype(bf16)
        d_ref[rows, :] = c_ref[rows, :].astype(bf16)

    by_rows(x_ref.shape[0], step)


def prep(x, cot, gain):
    return call(prep_kernel, (x, cot, gain), (sds(x.shape, bf16),) * 2, "prep")


def attend_kernel(n, a_ref, *refs):
    w, (qkv_ref, mixed_ref, lse_ref) = matrices(refs[:n]), refs[n:]
    scale = HEAD_DIM**-0.5 * LOG2E

    def project_rows(rows, _):
        for c in range(3):
            qkv_ref[c, rows, :] = dot(a_ref[rows, :], w(c)).astype(bf16)

    def head(h):
        cols = span(h, HEAD_DIM)
        q, k, v = (qkv_ref[c, :, cols] for c in range(3))
        scores = dot(k, q, NT)
        top = jnp.max(scores, axis=0, keepdims=True)
        expd = jnp.exp2((scores - top) * scale)
        total = jnp.sum(expd, axis=0, keepdims=True)
        mixed = dot(v, expd.astype(bf16), TN) / total
        mixed_ref[:, cols] = mixed.T.astype(bf16)
        lse_ref[pl.ds(h, 1), :] = top * scale + jnp.log2(total)

    by_rows(a_ref.shape[0], project_rows, None, PROJ_BLOCK)
    loop(qkv_ref.shape[2] // HEAD_DIM, head)


def attend(a, w):
    length, local = a.shape[0], w[0].shape[-1]
    outs = (sds((3, length, local), bf16), sds((length, local), bf16), sds((local // HEAD_DIM, length), f32))
    return call(functools.partial(attend_kernel, len(w)), (a, *w), outs, "attend", 12)


def project_kernel(n, *refs):
    mixed, w = refs[:n], refs[n : 2 * n]
    x_ref, g_ref, resid_ref, a_ref = refs[2 * n :]

    def step(rows, _):
        total = dot(mixed[0][rows, :], w[0][...])
        for j in range(1, n):
            total += dot(mixed[j][rows, :], w[j][...])
        resid = x_ref[rows, :] + total
        resid_ref[rows, :] = resid
        a_ref[rows, :] = (normed(resid)[0] * g_ref[...]).astype(bf16)

    by_rows(x_ref.shape[0], step)


def project(mixed, w, x, gain):
    outs = (sds(x.shape, f32), sds(x.shape, bf16))
    return call(functools.partial(project_kernel, len(mixed)), (*mixed, *w, x, gain), outs, "project")


def mlp_kernel(n, *refs):
    a_ref, d_ref = refs[:2]
    up, down = refs[2 : 2 + n], refs[2 + n : 2 + 2 * n]
    outs = refs[2 + 2 * n :]
    hid, dpre, grads = outs[:n], outs[n : 2 * n], outs[2 * n :]
    for j in range(n):
        u = dot(a_ref[...], up[j][...])
        d_hidden = dot(d_ref[...], down[j][...], NT)
        sq = u * u
        t = jnp.tanh(GELU_A * u * (1.0 + GELU_B * sq))
        half = 0.5 * (1.0 + t)
        hidden = (u * half).astype(bf16)
        slope = half + 0.5 * u * (1.0 - t * t) * (GELU_A * (1.0 + 3.0 * GELU_B * sq))
        d_pre = (d_hidden * slope).astype(bf16)
        hid[j][...] = hidden
        dpre[j][...] = d_pre
        grads[2 * j][...] = dot(hidden, d_ref[...], TN).astype(bf16)
        grads[2 * j + 1][...] = dot(d_pre, a_ref[...], TN).astype(bf16)


def mlp(a, d, up, down):
    n = len(up)
    length, width = a.shape
    local = up[0].shape[1]
    act, grad = sds((length, local), bf16), sds((local, width), bf16)
    outs = call(functools.partial(mlp_kernel, n), (a, d, *up, *down), (act,) * (2 * n) + (grad,) * (2 * n), "mlp", 12)
    return outs[:n], outs[n : 2 * n], [outs[2 * n + 2 * j : 2 * n + 2 * j + 2] for j in range(n)]


def norm_back(d_a, v, gain):
    xhat, r = normed(v)
    e = d_a * gain
    back = r * (e - jnp.mean(e, axis=-1, keepdims=True) - xhat * jnp.mean(e * xhat, axis=-1, keepdims=True))
    return back, fold(d_a * xhat)


def mlp_back_kernel(n, *refs):
    d_pre, up = refs[:n], refs[n : 2 * n]
    resid_ref, c_ref, g_ref, dres_ref, datt_ref, gain_ref = refs[2 * n :]

    def step(rows, gain):
        total = dot(d_pre[0][rows, :], up[0][...], NT)
        for j in range(1, n):
            total += dot(d_pre[j][rows, :], up[j][...], NT)
        back, part = norm_back(total, resid_ref[rows, :], g_ref[...])
        d_resid = c_ref[rows, :] + back
        dres_ref[rows, :] = d_resid
        datt_ref[rows, :] = d_resid.astype(bf16)
        return gain + part

    gain_ref[...] = by_rows(c_ref.shape[0], step, jnp.zeros(gain_ref.shape, f32), 256)


def mlp_back(d_pre, up, resid, cot, gain):
    n = len(up)
    outs = (sds(resid.shape, f32), sds(resid.shape, bf16), sds((8, resid.shape[1]), f32))
    return call(functools.partial(mlp_back_kernel, n), (*d_pre, *up, resid, cot, gain), outs, "mlp_back")


def mlp_out_kernel(n, *refs):
    hid, down = refs[:n], refs[n : 2 * n]
    resid_ref, out_ref = refs[2 * n :]

    def step(rows, _):
        total = resid_ref[rows, :]
        for j in range(n):
            total += dot(hid[j][rows, :], down[j][...])
        out_ref[rows, :] = total

    by_rows(resid_ref.shape[0], step)


def mlp_out(hid, down, resid):
    n = len(down)
    return call(functools.partial(mlp_out_kernel, n), (*hid, *down, resid), (sds(resid.shape, f32),), "mlp_out")[0]


def grad_out_kernel(n, d_ref, *refs):
    for mixed, out in zip(refs[:n], refs[n:], strict=True):
        out[...] = dot(mixed[...], d_ref[...], TN).astype(bf16)


def grad_out(d, mixed):
    n = len(mixed)
    outs = (sds((mixed[0].shape[1], d.shape[1]), bf16),) * n
    return call(functools.partial(grad_out_kernel, n), (d, *mixed), outs, "grad_out")


def attend_back_kernel(added, a_ref, d_ref, w_ref, qkv_ref, lse_ref, *refs):
    scale = HEAD_DIM**-0.5
    got, dqkv_ref, grads, dm_ref = refs[:added], refs[added], refs[added + 1 : -1], refs[-1]
    dm_ref[...] = dot(d_ref[...], w_ref[...], NT).astype(bf16)

    def head(h):
        cols = span(h, HEAD_DIM)
        q, k, v = (qkv_ref[c, :, cols] for c in range(3))
        dm = dm_ref[:, cols]
        probs = jnp.exp2(dot(k, q, NT) * (scale * LOG2E) - lse_ref[pl.ds(h, 1), :])
        d_probs = dot(v, dm, NT)
        dqkv_ref[2, :, cols] = dot(probs.astype(bf16), dm).astype(bf16)
        delta = jnp.sum(d_probs * probs, axis=0, keepdims=True)
        d_scores = (probs * (d_probs - delta)).astype(bf16)
        dqkv_ref[1, :, cols] = (dot(d_scores, q) * scale).astype(bf16)
        dqkv_ref[0, :, cols] = (dot(k, d_scores, TN) * scale).T.astype(bf16)

    unrolled(w_ref.shape[0] // HEAD_DIM, head)
    size = GRAD_BLOCK

    def grad_cols(i):
        cols = span(i, size)
        for c in range(3):
            grad = dot(dqkv_ref[c], a_ref[:, cols], TN)
            grads[c][:, cols] = (grad + got[c][:, cols].astype(f32) if added else grad).astype(bf16)

    loop(a_ref.shape[1] // size, grad_cols)


def attend_back(a, d, w, qkv, lse, got=()):
    length, width = a.shape
    local = w.shape[0]
    outs = (sds((3, length, local), bf16), *[sds((local, width), bf16)] * 3)
    outs = call(functools.partial(attend_back_kernel, len(got)), (a, d, w, qkv, lse, *got), outs, "attend_back", 12, False, [pltpu.VMEM((length, local), bf16)])
    return outs[0], outs[1:]


def join_kernel(axes, at_ref, *refs):
    quarters, outs = refs[:4], refs[4:]
    width = quarters[0].shape[1]
    for p, quarter in enumerate(quarters):
        place = pl.ds(pl.multiple_of(at_ref[p] * width, width), width)
        for i, (out, axis) in enumerate(zip(outs, axes, strict=True)):
            if axis == 0:
                out[place, :] = quarter[i]
            else:
                out[:, place] = quarter[i]


def join(quarters, likes, axes):
    flat = [(v.shape[-2:], 0 if axis == 3 else axis) for v, axis in zip(likes, axes, strict=True) for _ in range(v.size // (v.shape[-1] * v.shape[-2]))]
    outs = [sds(shape, bf16) for shape, _ in flat]
    return call(functools.partial(join_kernel, tuple(axis for _, axis in flat)), quarters, outs, "join", 4, True)


def cut_kernel(axes, at_ref, *refs):
    n = len(axes)
    for out, p in zip(refs[n:], (0, 2), strict=True):
        size = out.shape[1]
        place = pl.ds(pl.multiple_of(at_ref[p] * size, size), size)
        i = 0
        for v, axis in zip(refs[:n], axes, strict=True):
            if axis == 3:
                for c in range(3):
                    out[i + c] = v[c, place, :]
                i += 3
            else:
                out[i] = v[place, :] if axis == 0 else v[:, place]
                i += 1


def cut(arrays, axes):
    size = max(arrays[0].shape) // 4
    outs = (sds((sum(v.size for v in arrays) // (4 * size * size), size, size), bf16),) * 2
    return call(functools.partial(cut_kernel, tuple(axes)), arrays, outs, "cut", 4, True)


def cut_one_kernel(at_ref, w_ref, out_ref):
    size = out_ref.shape[1]
    out_ref[...] = w_ref[:, span(at_ref[5], size), :]


def cut_one(w):
    n, width, local = w.shape
    return call(cut_one_kernel, (w,), (sds((n, width // 4, local), bf16),), "cut", 4, True)[0]


def middle_kernel(y_ref, z_ref, a_ref, b_ref):
    rows = a_ref.shape[1]
    a_ref[...] = z_ref[:, 0:rows, :]
    b_ref[...] = y_ref[:, rows : 2 * rows, :]


def middle(y, z):
    n, rows, local = y.shape
    return call(middle_kernel, (y, z), (sds((n, rows // 2, local), bf16),) * 2, "middle", 4)


def join_four_kernel(at_ref, own_ref, y_ref, z_ref, a_ref, b_ref, *outs):
    size = own_ref.shape[1]
    for i, out in enumerate(outs):
        out[span(at_ref[5], size), :] = own_ref[i]
        out[span(at_ref[6], size), :] = y_ref[i]
        out[span(at_ref[7], size), :] = z_ref[i]
        out[span(at_ref[8] * 2, size // 2), :] = a_ref[i]
        out[span(at_ref[8] * 2 + 1, size // 2), :] = b_ref[i]


def join_four(own, y, z, a, b):
    n, rows, local = own.shape
    return call(join_four_kernel, (own, y, z, a, b), (sds((4 * rows, local), bf16),) * n, "join", 4, True)


def half_of(ref, at, rows):
    place = pl.ds(pl.multiple_of(at * rows, rows), rows)
    return ref[place, :] if len(ref.shape) == 2 else ref[:, place, :]


def add_kernel(a_ref, b_ref, o_ref):
    o_ref[...] = a_ref[...] + b_ref[...]


def add(a, b):
    return call(add_kernel, (a, b), (sds(a.shape, a.dtype),), "add", 4)[0]


def halved(shape, n=None):
    half = (shape[-2] // 2, shape[-1])
    return sds(half if n is None else (n, *half), bf16)


def split_add_kernel(n, at_ref, *refs):
    a, b, (give_ref, keep_ref) = refs[:n], refs[n : 2 * n], refs[2 * n :]
    rows = give_ref.shape[-2]
    for at, out in ((1 - at_ref[0], give_ref), (at_ref[0], keep_ref)):
        for i in range(n):
            total = half_of(a[i], at, rows) + half_of(b[i], at, rows)
            if len(out.shape) == 2:
                out[...] = total
            else:
                out[i] = total


def split_add(a, b):
    n = len(a)
    outs = (halved(a[0].shape, None if n == 1 else n),) * 2
    return call(functools.partial(split_add_kernel, n), (*a, *b), outs, "split_add", 4, True)


EXTRA = 16


def pack_kernel(at_ref, *refs):
    gains, got_gains, give_ref, keep_ref = refs[4:]
    rows = give_ref.shape[1] - EXTRA
    total = (gains[...] + got_gains[...]).astype(bf16)
    extra = jnp.concatenate([total, jnp.zeros((EXTRA - total.shape[0], total.shape[1]), bf16)])
    for at, out in ((1 - at_ref[0], give_ref), (at_ref[0], keep_ref)):
        for i in range(2):
            out[i, 0:rows, :] = half_of(refs[i], at, rows) + half_of(refs[2 + i], at, rows)
            out[i, rows : rows + EXTRA, :] = extra


def pack(kept, sent, got, gains, got_gains):
    rows, width = kept.shape
    outs = (sds((2, rows // 2 + EXTRA, width), bf16),) * 2
    return call(pack_kernel, (kept, sent, *got, gains, got_gains), outs, "pack", 4, True)


def part_add_kernel(a_ref, b_ref, *outs):
    for i, out in enumerate(outs):
        out[...] = a_ref[i] + b_ref[i]


def part_add(a, b):
    return call(part_add_kernel, (a, b), [sds(a.shape[1:], bf16)] * a.shape[0], "add", 4)


def finish_packed_kernel(at_ref, mine_ref, other_ref, out_ref, gain1_ref, gain2_ref):
    rows = out_ref.shape[0] // 2
    for at, ref in ((at_ref[0], mine_ref), (1 - at_ref[0], other_ref)):
        out_ref[pl.ds(pl.multiple_of(at * rows, rows), rows), :] = ref[0:rows, :].astype(f32)
    gains = mine_ref[rows : rows + EXTRA, :].astype(f32)
    gain1_ref[...] = gains[0:1, :]
    gain2_ref[...] = gains[1:2, :]


def finish_packed(mine, other):
    rows, width = 2 * (mine.shape[0] - EXTRA), mine.shape[1]
    outs = (sds((rows, width), f32), sds((1, width), f32), sds((1, width), f32))
    return call(finish_packed_kernel, (mine, other), outs, "finish", 6, True)


def pick_kernel(at_ref, a_ref, b_ref, o_ref):
    @pl.when(at_ref[4] == 1)
    def _():
        o_ref[...] = b_ref[...]

    @pl.when(at_ref[4] == 0)
    def _():
        o_ref[...] = a_ref[...]


def pick(a, b):
    return call(pick_kernel, (a, b), (sds(a.shape, a.dtype),), "pick", 4, True)[0]


def placed(ref, at, index=None):
    rows = ref.shape[-2]
    return pl.ds(pl.multiple_of(at * rows, rows), rows), (ref[...] if index is None else ref[index]).astype(f32)


def finish_kernel(turned, at_ref, mine_ref, other_ref, *outs):
    for at, ref in ((at_ref[0], mine_ref), (1 - at_ref[0], other_ref)):
        for i, (out, turn) in enumerate(zip(outs, turned, strict=True)):
            place, v = placed(ref, at, i if len(turned) > 1 else None)
            if turn:
                out[:, place] = v.T
            else:
                out[place, :] = v


def finish(mine, other, turned):
    rows, width = 2 * mine.shape[-2], mine.shape[-1]
    outs = [sds((width, rows) if turn else (rows, width), f32) for turn in turned]
    return call(functools.partial(finish_kernel, turned), (mine, other), outs, "finish", 6, True)


def finish_slot_kernel(at_ref, mine_ref, other_ref, *refs):
    for at, ref in ((at_ref[0], mine_ref), (1 - at_ref[0], other_ref)):
        place, v = placed(ref, at)
        refs[-1][0, :, place] = v.T


def finish_slot(mine, other, slot, slots, into):
    rows, width = mine.shape
    spec = pl.BlockSpec(memory_space=pltpu.VMEM)
    return pl.pallas_call(
        functools.partial(placed_kernel, finish_slot_kernel),
        grid=(1,),
        in_specs=[spec, spec] + [pl.BlockSpec(memory_space=pl.ANY)] * (into is not None),
        out_specs=pl.BlockSpec((1, width, 2 * rows), lambda i: (slot, 0, 0)),
        out_shape=sds((slots, width, 2 * rows), f32),
        input_output_aliases={} if into is None else {2: 0},
        compiler_params=params(6),
        cost_estimate=cost(),
        name="finish",
    )(mine, other, *([] if into is None else [into]))


def input_back_kernel(n, counts, *refs):
    d_qkv, refs = refs[:n], refs[n:]
    w = []
    for count in counts:
        w.append(matrices(refs[:count]))
        refs = refs[count:]
    x_ref, dres_ref, g_ref, other_ref, out_ref, gains_ref = refs

    def step(rows, gain):
        total = None
        for j in range(n):
            for c in range(3):
                part = dot(d_qkv[j][c, rows, :], w[j](c), NT)
                total = part if total is None else total + part
        back, part = norm_back(total, x_ref[rows, :], g_ref[...])
        out_ref[rows, :] = dres_ref[rows, :] + back
        return gain + part

    gain = by_rows(x_ref.shape[0], step, jnp.zeros(other_ref.shape, f32), 256)
    gains_ref[0:1, :] = jnp.sum(gain, axis=0, keepdims=True)
    gains_ref[1:2, :] = jnp.sum(other_ref[...], axis=0, keepdims=True)


def input_back(d_qkv, w, x, d_resid, gain, other):
    outs = (sds(x.shape, f32), sds((2, x.shape[1]), f32))
    kernel = functools.partial(input_back_kernel, len(w), tuple(len(v) for v in w))
    return call(kernel, (*d_qkv, *[m for v in w for m in v], x, d_resid, gain, other), outs, "input_back", 12)


def swap(axis, size, bit):
    pairs = [(i, i ^ bit) for i in range(size)]
    return lambda v: lax.ppermute(v, axis, pairs)


def bits_of(size):
    return [1 << b for b in reversed(range(size.bit_length() - 1))]


class Run:
    def __init__(self):
        self.token = None

    def tie(self, v):
        if self.token is None:
            return v
        return lax.optimization_barrier((v, self.token))[0]

    def compute(self, step, first, *rest):
        outs = step(self.tie(first), *rest)
        self.token = jax.tree.leaves(outs)[0]
        return outs

    def send(self, move, v):
        v = self.tie(v)
        self.token = v
        return move(v)


class Names:
    def __getattr__(self, name):
        return name


N = Names()
ORDER = (
    N.c0_q, N.sl_q, N.xp_q, N.sl_d, N.sl_ou, N.prep, N.c0_ou_0, N.xp_d, N.xr_d, N.att0, N.xp_ou, N.y_q, N.z_q,
    N.y_ou, N.xr_ou, N.att2, N.sm_q, N.zz_q, N.yy_q, N.z_ou, N.z_d, N.as_q, N.cx_q_1, N.c0_d, N.att1, N.y_d,
    N.cx_q_0, N.c0_ou_1, N.as_ou, N.as_d, N.cx_ou_0, N.cx_ou_1, N.cx_d, N.cx_q_2, N.att3, N.proj, N.mlpR,
    N.cF1_1, N.cF1_0, N.mlpP, N.cF0_0, N.cF0_1, N.aF1, N.F_yx, N.mlpback, N.ab3, N.cQ1_1, N.cQ1_0, N.aF0, N.F_yo,
    N.cQ1_2, N.F_ax, N.F_x, N.ab2, N.ab1, N.cQ0_0, N.cQ0_2, N.gout, N.cO_1, N.cQ0_1, N.cO_0, N.Qa_x, N.F_ao,
    N.F_a2, N.F_z1, N.Qb_x, N.ab0, N.inback, N.g0, N.Qa_a1, N.Qa_y, N.F_a3, N.aO, N.F_z2, N.O_y, N.Qa_a2,
    N.Qa_z1, N.Qb_a1, N.Qc_x, N.F_a4, N.F_z3, N.Qb_y, N.O_a1, N.Qa_a3, N.Qc_a1, N.Qc_y, N.Qa_z2, N.O_x, N.Qb_a2,
    N.Qb_z1, N.F_a5, N.F_w, N.O_a2, N.O_z1, N.Qa_a4, N.Qa_z3, N.Qb_a3, N.Qb_z2, N.Qc_a2, N.Qc_z1, N.O_a3, N.O_z2,
    N.Qa_a5, N.Qa_w, N.Qb_a4, N.Qb_z3, N.Qc_a3, N.Qc_z2, N.F_f, N.O_a4, N.O_z3, N.Qb_a5, N.Qa_f, N.Qb_w, N.Qc_a4,
    N.Qc_z3, N.O_a5, N.O_w, N.Qb_f, N.mlpout, N.Qc_a5, N.Qc_w, N.O_f, N.Qc_f,
)
GROUPS = {"q": ("qkv",), "ou": ("out", "up"), "d": ("down",)}
FOUR = ("q",)
CHUNKS = {"F": "F", "O": "O", "Qa": "Q", "Qb": "Q", "Qc": "Q"}
AXES = {"qkv": 3, "out": 1, "up": 0, "down": 1}


def per_device(
    sizes,
    inputs,
    norm1_gain,
    weight_qkv,
    weight_out,
    norm2_gain,
    weight_up,
    weight_down,
    cotangent,
):
    n_rep, n_dp, n_mp = sizes["rep"], sizes["dp"], sizes["mp"]
    if n_mp != 4 or n_rep != 2 or n_dp & (n_dp - 1) or n_dp < 2:
        raise ValueError("unsupported mesh")
    shape = inputs.shape
    x = inputs.reshape(shape[-2:])
    cot = cotangent.reshape(shape[-2:])
    gain1, gain2 = norm1_gain.reshape(1, -1), norm2_gain.reshape(1, -1)
    width = x.shape[1]
    run = Run()
    line = n_dp == 4

    core = swap("mp", n_mp, 1)
    far = swap("mp", n_mp, 2)
    rep = swap("rep", n_rep, 1)
    near = swap("dp", n_dp, 1)
    own = {"qkv": weight_qkv, "out": weight_out, "up": weight_up, "down": weight_down}
    w = {k: [[v], None, None, None] for k, v in own.items()}
    env = {}

    def gather_task(kind, g, i="0"):
        names = GROUPS[g]
        if kind == "c0":
            k = names[int(i)]
            w[k][2] = [run.send(core, own[k])]
        elif kind == "x":
            for k in names:
                w[k][1] = [run.send(far, own[k])]
        elif g in FOUR and kind == "sl":
            env["p", g] = run.compute(cut_one, own[names[0]])
        elif g in FOUR and kind == "z":
            env["pz", g] = run.send(near, env["px", g])
        elif g in FOUR and kind == "sm":
            env["a", g], env["b", g] = run.compute(middle, env["py", g], env["pz", g])
        elif kind == "yy":
            env["ya", g] = run.send(rep, env["a", g])
        elif kind == "zz":
            env["zb", g] = run.send(near, env["b", g])
        elif g in FOUR and kind == "as":
            w[names[0]][1] = run.compute(join_four, env["px", g], env["py", g], env["pz", g], env["ya", g], env["zb", g])
        elif kind == "sl":
            env["p", g], env["r", g] = run.compute(lambda *v: cut(v, [AXES[k] for k in names]), *[own[k] for k in names])
        elif kind == "xp":
            env["px", g] = run.send(far, env["p", g])
        elif kind == "xr":
            env["rx", g] = run.send(far, env["r", g])
        elif kind == "y":
            env["py", g] = run.send(rep, env["px", g])
        elif kind == "z":
            env["rz", g] = run.send(near, env["rx", g])
        elif kind == "as":
            outs = run.compute(
                lambda *v: join(v, [own[k] for k in names], [AXES[k] for k in names]),
                env["px", g], env["py", g], env["rx", g], env["rz", g],
            )
            for k in names:
                n = 3 if AXES[k] == 3 else 1
                w[k][1], outs = outs[:n], outs[n:]
        elif kind == "cx":
            k, m = [(k, m) for k in names for m in range(len(w[k][1]))][int(i)]
            w[k][3] = w[k][3] or [None] * len(w[k][1])
            w[k][3][m] = run.send(core, w[k][1][m])

    def one(k):
        return [v[0] for v in w[k]]

    def over_dp(v):
        for bit in bits_of(n_dp):
            v = run.compute(add, v, run.send(swap("dp", n_dp, bit), v))
        return v

    def chunk_task(name, stage):
        source = CHUNKS[name]
        c = env.setdefault(("chunk", name), {})

        def z(pairs):
            return lambda v: lax.ppermute(v, "dp", pairs)

        if stage == "f":
            done(name, c["v"], c["w"])
        elif stage == "w":
            c["w"] = run.send(rep, c["v"])
        elif stage == "z1" and line:
            c["z"] = run.send(z([(0, 1), (3, 2)]), c["v"])
        elif stage == "z2" and line:
            c["z"] = run.send(z([(1, 2), (2, 1)]), c["v"])
        elif stage == "z3" and line:
            c["z"] = run.send(z([(1, 0), (2, 3)]), c["v"])
        elif stage == "a3" and line:
            c["v"] = run.compute(add, c["v"], c["z"])
        elif stage == "a4":
            c["v"] = run.compute(add, c["v"], c["z"]) if line else over_dp(c["v"])
        elif stage == "a5" and line:
            c["v"] = run.compute(lambda *v: pick(*v), c["v"], c["z"])
        elif source == "Q":
            index = "abc".index(name[1])
            if stage == "x":
                c["x"] = run.send(far, env["gQ", 1][index])
            elif stage == "a1":
                c["give"], c["v"] = run.compute(lambda a, b: split_add([a], [b]), env["gQ", 0][index], c["x"])
            elif stage == "y":
                c["y"] = run.send(rep, c["give"])
            elif stage == "a2":
                c["v"] = run.compute(add, c["v"], c["y"])
        elif source == "O":
            if stage == "y":
                c["y"] = run.send(rep, env["O"][0])
            elif stage == "a1":
                c["v"], c["give"] = run.compute(part_add, env["O"][1], c["y"])
            elif stage == "x":
                c["x"] = run.send(far, c["give"])
            elif stage == "a2":
                c["v"] = run.compute(add, c["v"], c["x"])
        elif source == "F":
            j = "ox".index(stage[1]) if stage[0] in "ya" and stage[1] in "ox" else None
            if stage in ("yo", "yx"):
                c[stage] = run.send(rep, env["F", j][0])
            elif stage in ("ao", "ax"):
                c[stage] = run.compute(add, env["F", j][1], c["y" + stage[1]])
            elif stage == "x":
                c["x"] = run.send(far, c["ax"])
            elif stage == "a2":
                c["v"] = run.compute(add, c["ao"], c["x"])

    def done(name, mine, other):
        if name == "F":
            env["down"], env["up"] = run.compute(lambda *v: finish(*v, (False, True)), mine, other)
        elif name == "O":
            env["out"], env["gain1"], env["gain2"] = run.compute(lambda *v: finish_packed(*v), mine, other)
        else:
            env["qkv"] = run.compute(lambda *v: finish_slot(*v, "abc".index(name[1]), 3, env.get("qkv")), mine, other)

    def task(t):
        if t == "prep":
            env["a1"], env["dm"] = run.compute(lambda c, v, g: prep(v, c, g), cot, x, gain1)
        elif t[:3] == "att":
            j = int(t[3])
            env["att", j] = run.compute(attend, env["a1"], w["qkv"][j])
        elif t == "proj":
            env["resid"], env["a2"] = run.compute(lambda *m: project(m, one("out"), x, gain2), *[env["att", j][1] for j in range(4)])
        elif t in ("mlpP", "mlpR"):
            js = (0, 2) if t == "mlpP" else (1, 3)
            hid, dpre, grads = run.compute(lambda a: mlp(a, env["dm"], [w["up"][j][0] for j in js], [w["down"][j][0] for j in js]), env["a2"])
            for i, j in enumerate(js):
                env["hid", j], env["dpre", j], env["gF", j] = hid[i], dpre[i], grads[i]
        elif t[:2] in ("cF", "cQ"):
            (kind, j), i = t[1:3], int(t[-1])
            grads = env["g" + kind, 2 + int(j)]
            env.setdefault(("r" + kind, int(j)), [None] * len(grads))[i] = run.send(core, grads[i])
        elif t in ("aF0", "aF1"):
            j = int(t[2])
            env["F", j] = run.compute(lambda *v: split_add(v[:2], v[2:]), *env["gF", j], *env["rF", j])
        elif t == "mlpback":
            env["dres"], env["datt"], env["part2"] = run.compute(
                lambda *d: mlp_back(d, one("up"), env["resid"], cot, gain2), *[env["dpre", j] for j in range(4)]
            )
        elif t == "mlpout":
            env["output"] = run.compute(lambda *h: mlp_out(h, one("down"), env["resid"]), *[env["hid", j] for j in range(4)])
        elif t == "gout":
            env["gO"] = run.compute(lambda d: grad_out(d, [env["att", j][1] for j in range(4)]), env["datt"])
        elif t[:2] == "cO":
            env.setdefault("rO", [None] * 2)[int(t[-1])] = run.send(core, env["gO"][2 + int(t[-1])])
        elif t == "aO":
            env["O"] = run.compute(lambda *v: pack(*v, env["rO"], env["g"], env["gr"]), *env["gO"][:2])
        elif t[:2] == "ab":
            j = int(t[2])
            got = env["rQ", j] if j < 2 else ()
            env["dqkv", j], env["gQ", j] = run.compute(
                lambda d: attend_back(env["a1"], d, w["out"][j][0], env["att", j][0], env["att", j][2], got), env["datt"]
            )
        elif t == "inback":
            env["gin"], env["g"] = run.compute(
                lambda *d: input_back(d, w["qkv"], x, env["dres"], gain1, env["part2"]), *[env["dqkv", j] for j in range(4)]
            )
        elif t == "g0":
            env["gr"] = run.send(core, env["g"])
        elif t.split("_")[1] in GROUPS:
            gather_task(*t.split("_"))
        else:
            chunk_task(*t.split("_"))

    for t in ORDER:
        task(t)
    return (
        env["output"].reshape(shape),
        env["gin"].reshape(shape),
        env["gain1"].reshape(-1),
        env["qkv"],
        env["out"],
        env["gain2"].reshape(-1),
        env["up"],
        env["down"],
    )


def solution(mesh):
    return jax.shard_map(
        functools.partial(per_device, dict(mesh.shape)),
        mesh=mesh,
        in_specs=(
            P(("rep", "mp"), "dp", None, None),
            P(),
            P(None, None, "mp"),
            P("mp", None),
            P(),
            P(None, "mp"),
            P("mp", None),
            P(("rep", "mp"), "dp", None, None),
        ),
        out_specs=(
            P(("rep", "mp"), "dp", None, None),
            P(("rep", "mp"), "dp", None, None),
            P(),
            P(None, None, "mp"),
            P("mp", None),
            P(),
            P(None, "mp"),
            P("mp", None),
        ),
        check_vma=False,
    )
```
